32 devices in a mesh: tx: 2 (over core), ty: 4 (over y, x), lz: 4 (over z).
Axes of the slice: x: 2, y: 2, z: 4, core: 2. Of those that a mesh axis runs over, the one named last changes fastest.
Arguments:
- test_field: bfloat16 [64, 6, 48, 512], P('tx', None, 'lz', 'ty'), may hold values from -6 to 6
- dir_field: bfloat16 [64, 6, 48, 512], P('tx', None, 'lz', 'ty'), may hold values from -6 to 6
- border_b: bfloat16 [64, 6, 48, 512], P('tx', None, 'lz', 'ty')
- border_c: bfloat16 [64, 6, 48, 512], P('tx', None, 'lz', 'ty')
- land_mask: int32 [64, 512], P('tx', 'ty'), may hold values from 0 to 1, as said below
- active_rows: int32 [64, 4], P('tx', 'ty'), may hold values from -1 to 31, as said below
- cell_blocks: bfloat16 [64, 36, 512], P('tx', None, 'ty'), may hold values from -2.5 to 2.5
- column_k: bfloat16 [288, 288], replicated, may hold values from -0.375 to 0.375
- kappa: float32 [6], replicated, may hold values from 0.2 to 1
Outputs:
- test_image: bfloat16 [64, 6, 48, 512], P('tx', None, 'lz', 'ty')
- dir_image: bfloat16 [64, 6, 48, 512], P('tx', None, 'lz', 'ty')
- border: float32 [3], replicated
The draws below stay inside these ranges and needn't reach their ends.
Inputs may be any that keep to these rules, and one draw needn't show every extreme that they name: `active_rows`: in each tile the 32 entries name distinct local rows, the active ones, followed by -1 for the rest; some tile has all 32 rows active. `land_mask`: cells whose latitude index y has y % 128 equal to 0 or 127 are ocean.
All inputs are finite; a program needn't handle non-finite values.
Results may differ from the reference program's by a relative error of at most 0.0028.
Values may be sent and summed in bfloat16 or wider, within the bound.
A program may use at most 192 MiB of HBM per device.

```python
import math
import jax
import jax.numpy as jnp
from jax import lax

NU = 6
NZ = 48
BLK = 128
TXD = 32
COL = 288
NX = 64
NY = 512


def border_law(key):
    shape = (NX, NU, NZ, NY)
    longitude = jnp.arange(NX, dtype=jnp.float32) / NX
    rising = jnp.exp(jnp.log(10.0) * longitude)[:, None, None, None]
    return jax.random.normal(key, shape, jnp.float32) * rising


def draw_border_b(key, part):
    return border_law(jax.random.fold_in(key, 11)).astype(jnp.bfloat16)


def draw_border_c(key, part):
    return border_law(jax.random.fold_in(key, 23)).astype(jnp.bfloat16)


def draw_land_mask(key, part):
    wet = jax.random.randint(jax.random.fold_in(key, 53), (NX, NY), 0, 10) < 7
    inside = jnp.arange(NY, dtype=jnp.int32) % BLK
    edges = (inside == 0) | (inside == BLK - 1)
    return jnp.where(edges[None, :], True, wet).astype(jnp.int32)


def draw_active_rows(key, part):
    tiles_x = NX // TXD
    tiles_y = NY // BLK
    first, second, third = jax.random.split(jax.random.fold_in(key, 37), 3)
    counts = jax.random.randint(first, (tiles_x * tiles_y,), 1, TXD + 1)
    full = jax.random.randint(second, (), 0, tiles_x * tiles_y)
    counts = counts.at[full].set(TXD)
    orders = jax.vmap(lambda k: jax.random.permutation(k, TXD))(jax.random.split(third, tiles_x * tiles_y))
    lines = jnp.arange(TXD, dtype=jnp.int32)
    entries = jnp.where(lines[None, :] < counts[:, None], orders.astype(jnp.int32), -1)
    entries = entries.reshape(tiles_x, tiles_y, TXD).transpose(0, 2, 1)
    return entries.reshape(NX, tiles_y).astype(jnp.int32)


def level_of(rng, dims, shards, smallest, largest):
    gain, own = 1.0, jax.random.fold_in(rng, 6)
    for position, parts in shards:
        draws = jnp.exp(jax.random.uniform(jax.random.fold_in(own, position), (parts,), jnp.float32, smallest / len(shards), largest / len(shards)))
        gain = gain * jnp.repeat(draws, dims[position] // parts).reshape([-1 if axis == position else 1 for axis in range(len(dims))])
    return gain


def noise(key, dims, scale, reach, shards=(), kind=jnp.bfloat16):
    gain = level_of(key, dims, shards, -0.22, 0.18) if shards else 1.0
    result = jax.random.normal(key, dims, jnp.float32) * scale * gain
    return jnp.minimum(jnp.maximum(result, -reach), reach).astype(kind)


def setup_inputs(seed: int = 0) -> dict:
    key_of = jax.random.split(jax.random.key(seed), 10)
    return {
        "test_field": noise(key_of[0], (NX, NU, NZ, NY), 1.0, 6.0, ((0, 2), (2, 4), (3, 4))),
        "dir_field": noise(key_of[1], (NX, NU, NZ, NY), 1.0, 6.0, ((0, 2), (2, 4), (3, 4))),
        "border_b": draw_border_b(jax.random.fold_in(key_of[9], 71), 0),
        "border_c": draw_border_c(jax.random.fold_in(key_of[9], 71), 0),
        "land_mask": draw_land_mask(jax.random.fold_in(key_of[9], 71), 0),
        "active_rows": draw_active_rows(jax.random.fold_in(key_of[9], 71), 0),
        "cell_blocks": noise(key_of[6], (NX, NU * NU, NY), NU ** -0.5, 2.5, ((0, 2), (2, 4))),
        "column_k": noise(key_of[7], (COL, COL), COL ** -0.5, 0.375),
        "kappa": jnp.clip(jnp.exp(jax.random.uniform(key_of[8], (NU,), jnp.float32, math.log(0.2), math.log(1.0))), 0.2, 1.0),
    }


def ocean_weight(land_mask, active_rows):
    tiles_x = NX // TXD
    tiles_y = active_rows.shape[1]
    lists = active_rows.reshape(tiles_x, TXD, tiles_y)
    lines = jnp.arange(TXD, dtype=jnp.int32)
    named = jnp.any(lists[:, :, None, :] == lines[None, None, :, None], axis=1)
    active = jnp.repeat(named.reshape(NX, tiles_y).astype(jnp.float32), BLK, axis=1)
    return land_mask.astype(jnp.float32) * active

def apply_jacobian(field, weight, cell_blocks, column_k, kappa):
    masked = field * weight.astype(jnp.bfloat16)[:, None, None, :]
    after = jnp.roll(masked, -1, axis=0)
    before = jnp.roll(masked, 1, axis=0)
    groups = NX // TXD
    dense = column_k.astype(jnp.float32)

    def one_group(items):
        center, ahead, behind, ocean, blocks = items
        here = center.astype(jnp.float32)
        coupled = jnp.einsum('pq,gqy->gpy', dense, here.reshape(TXD, COL, NY))
        coupled = lax.optimization_barrier(coupled.astype(jnp.bfloat16)).astype(jnp.float32)
        coupled = coupled.reshape(TXD, NU, NZ, NY)
        local = jnp.einsum('guwy,gwzy->guzy', blocks.astype(jnp.float32).reshape(TXD, NU, NU, NY), here)
        edge = jnp.zeros_like(here[..., :1])
        north = jnp.concatenate([here[..., 1:], edge], axis=3)
        south = jnp.concatenate([edge, here[..., :-1]], axis=3)
        spread = ahead.astype(jnp.float32) + behind.astype(jnp.float32) + north + south - 4.0 * here
        return ocean[:, None, None, :] * (coupled + local + kappa[None, :, None, None] * spread)
    shaped = (masked.reshape(groups, TXD, NU, NZ, NY), after.reshape(groups, TXD, NU, NZ, NY), before.reshape(groups, TXD, NU, NZ, NY), weight.reshape(groups, TXD, NY), cell_blocks.reshape(groups, TXD, NU * NU, NY))
    return lax.map(one_group, shaped).reshape(NX, NU, NZ, NY)

def reference(test_field, dir_field, border_b, border_c, land_mask, active_rows, cell_blocks, column_k, kappa):
    weight = ocean_weight(land_mask, active_rows)
    test_full = apply_jacobian(test_field, weight, cell_blocks, column_k, kappa)
    dir_full = apply_jacobian(dir_field, weight, cell_blocks, column_k, kappa)
    column_b = border_b.astype(jnp.float32)
    row_c = border_c.astype(jnp.float32)
    norm_b = jnp.sum(column_b * column_b)
    norm_c = jnp.sum(row_c * row_c)
    value_c = jnp.sum(row_c * test_field.astype(jnp.float32))
    value_a = jnp.sum(column_b * test_full)
    value_e = jnp.sum(column_b * dir_full)
    border = jnp.stack([value_a / jnp.sqrt(norm_b), value_e / jnp.sqrt(norm_b), value_c / jnp.sqrt(norm_c)])
    return (test_full.astype(jnp.bfloat16), dir_full.astype(jnp.bfloat16), border)
```

```python
import functools
import jax
import jax.numpy as jnp
from jax import lax
from jax.experimental import pallas as pl
from jax.experimental.pallas import tpu as pltpu
from jax.sharding import PartitionSpec as P

MESH = pl.DeviceIdType.MESH
F32 = jnp.float32
BF16 = jnp.bfloat16


MARGIN = 8


def dense_kernel(
    sizes, chunks, units,
    test_hbm, dir_hbm, b_hbm, c_hbm, land_ref, active_ref, blocks_hbm, k_hbm, kappa_ref,
    out_t, out_d, border_ref,
    test_ref, dir_ref, b_ref, c_ref, blocks_ref, k_ref,
    masked, arrived, product, coupled, weight, big_k, field, back, before_image, halo,
    edge_out, edge_in, edge_f, stat_out, stat_z, stat_y,
    ls, fs, fr, bs, br, xs, xr, ys, yr, ss, sr_z, sr_y,
):
    nx, ny, nz = sizes
    slab, rows, cells = test_ref.shape
    layers = slab // units
    full = 2 * slab
    group = rows // nz
    step = group // chunks
    pitch = rows + 2 * MARGIN
    mx, my, mz = lax.axis_index("tx"), lax.axis_index("ty"), lax.axis_index("lz")
    fields = (test_ref, dir_ref)
    outs = (out_t, out_d)

    loads = [
        pltpu.make_async_copy(source, target, ls.at[i])
        for i, (source, target) in enumerate((
            (test_hbm, test_ref), (dir_hbm, dir_ref), (k_hbm, k_ref), (b_hbm, b_ref),
            (c_hbm, c_ref), (blocks_hbm, blocks_ref),
        ))
    ]
    for load in loads:
        load.start()

    barrier = pltpu.get_barrier_semaphore()
    for k in range(1, nz):
        pl.semaphore_signal(
            barrier, inc=1, device_id={"lz": lax.rem(mz + k, nz)}, device_id_type=MESH
        )
    for k in range(1, nx * ny):
        near = {"ty": lax.rem(my + k // nx, ny), "tx": lax.rem(mx + k % nx, nx)}
        pl.semaphore_signal(barrier, inc=1, device_id=near, device_id_type=MESH)

    lane = lax.broadcasted_iota(jnp.int32, (rows, cells), 1)
    line = lax.broadcasted_iota(jnp.int32, (rows, rows), 0)
    named = jnp.max(
        jnp.where(jnp.broadcast_to(active_ref[...], (rows, rows)) == line, 1.0, 0.0),
        axis=1, keepdims=True,
    )
    weight[...] = land_ref[...].astype(F32) * named
    ocean = weight[...]

    def middle(q):
        return pl.ds(pl.multiple_of(q * pitch + MARGIN, 8), rows)

    for f in range(2):
        loads[f].wait()

        def mask(j, carry):
            field[middle(f * slab + j), :] = fields[f][j].astype(F32) * ocean
            return carry

        lax.fori_loop(0, slab, mask, 0, unroll=8)

    def pack(c):
        def pack_row(i, carry):
            x = lax.div(i, step) * group + c * step + lax.rem(i, step)
            masked[x] = field[pl.ds(MARGIN + x, full, stride=pitch), :].astype(BF16)
            return carry

        lax.fori_loop(0, nz * step, pack_row, 0, unroll=4)

    pack(0)

    pl.semaphore_wait(barrier, nx * ny + nz - 2)

    def forward(c, k):
        to = lax.rem(mz + k, nz)
        return pltpu.make_async_remote_copy(
            src_ref=masked.at[pl.ds(to * group + c * step, step)],
            dst_ref=arrived.at[c, mz],
            send_sem=fs.at[c, to],
            recv_sem=fr.at[c, mz],
            device_id={"lz": to},
            device_id_type=MESH,
        )

    def forward_in(c, k):
        src = lax.rem(mz + nz - k, nz)
        return pltpu.make_async_remote_copy(
            src_ref=arrived.at[c, src],
            dst_ref=arrived.at[c, src],
            send_sem=fs.at[c, src],
            recv_sem=fr.at[c, src],
            device_id={"lz": src},
            device_id_type=MESH,
        )

    def backward(c, k):
        to = lax.rem(mz + k, nz)
        return pltpu.make_async_remote_copy(
            src_ref=product.at[c, to],
            dst_ref=coupled.at[pl.ds(mz * group + c * step, step)],
            send_sem=bs.at[c, to],
            recv_sem=br.at[c, mz],
            device_id={"lz": to},
            device_id_type=MESH,
        )

    def backward_in(c, k):
        src = lax.rem(mz + nz - k, nz)
        return pltpu.make_async_remote_copy(
            src_ref=product.at[c, src],
            dst_ref=coupled.at[pl.ds(src * group + c * step, step)],
            send_sem=bs.at[c, src],
            recv_sem=br.at[c, src],
            device_id={"lz": src},
            device_id_type=MESH,
        )

    order = sorted(range(1, nz), key=lambda k: -min(k, nz - k))
    for c in range(1, chunks):
        pack(c)
        for k in order:
            forward(c - 1, k).start()

    def own_row(i, carry):
        arrived[lax.div(i, step), mz, lax.rem(i, step)] = masked[mz * group + i]
        return carry

    lax.fori_loop(0, group, own_row, 0)
    for k in order:
        forward(chunks - 1, k).start()
    later, before = lax.rem(mx + 1, nx), lax.rem(mx + nx - 1, nx)
    to_later = pltpu.make_async_remote_copy(
        src_ref=masked.at[rows - 1], dst_ref=halo.at[0], send_sem=xs.at[0], recv_sem=xr.at[0],
        device_id={"tx": later}, device_id_type=MESH,
    )
    to_before = pltpu.make_async_remote_copy(
        src_ref=masked.at[0], dst_ref=halo.at[1], send_sem=xs.at[1], recv_sem=xr.at[1],
        device_id={"tx": before}, device_id_type=MESH,
    )
    to_later.start()
    to_before.start()
    for f in range(2):
        def edges(j, carry):
            first, last = carry
            value = field[middle(f * slab + j), :]
            first = jnp.where(lane == j, pltpu.roll(value, j, 1), first)
            last = jnp.where(lane == j, pltpu.roll(value, j + 1, 1), last)
            return first, last

        blank = jnp.zeros((rows, cells), F32)
        first, last = lax.fori_loop(0, slab, edges, (blank, blank), unroll=4)
        edge_out[0, f] = first.astype(BF16)
        edge_out[1, f] = last.astype(BF16)

    up, down = lax.rem(my + 1, ny), lax.rem(my + ny - 1, ny)
    to_up = pltpu.make_async_remote_copy(
        src_ref=edge_out.at[1], dst_ref=edge_in.at[0], send_sem=ys.at[0], recv_sem=yr.at[0],
        device_id={"ty": up}, device_id_type=MESH,
    )
    to_down = pltpu.make_async_remote_copy(
        src_ref=edge_out.at[0], dst_ref=edge_in.at[1], send_sem=ys.at[1], recv_sem=yr.at[1],
        device_id={"ty": down}, device_id_type=MESH,
    )
    col = units * layers * nz
    wide = nz * full

    def chooser(shape, dim, f):
        i = lax.broadcasted_iota(jnp.int32, shape, dim)
        j = lax.broadcasted_iota(jnp.int32, shape, 1 - dim)
        part, rest = i // full, lax.rem(i, full)
        field, entry = rest // slab, lax.rem(rest, slab)
        unit, layer = entry // layers, lax.rem(entry, layers)
        target = unit * (layers * nz) + part * layers + layer
        return jnp.where((target == j) & (field == f), 1.0, 0.0).astype(BF16)

    loads[2].wait()
    dense = k_ref[...]
    total = None
    for f in range(2):
        left = jnp.dot(
            chooser((wide, col), 0, f), dense, preferred_element_type=F32
        ).astype(BF16)
        both = jnp.dot(left, chooser((col, wide), 1, f), preferred_element_type=F32)
        total = both if total is None else total + both
    big_k[...] = total.astype(BF16)
    to_up.start()
    to_down.start()

    for load in loads[3:]:
        load.wait()
    zero = jnp.zeros((rows, cells), F32)
    sums = (zero, zero, zero)

    def norms(j, carry):
        bb, cc, cv = carry
        b = b_ref[j].astype(F32)
        c = c_ref[j].astype(F32)
        return bb + b * b, cc + c * c, cv + c * test_ref[j].astype(F32)

    quarter = slab // chunks
    for c in range(chunks):
        for k in order:
            forward_in(c, k).wait_recv()
        part = jnp.concatenate(
            [arrived[c, :, r].reshape(wide, cells) for r in range(step)], axis=1
        )
        result = jnp.dot(big_k[...], part, preferred_element_type=F32).astype(BF16)
        for d in range(nz):
            for r in range(step):
                product[c, d, r] = result[d * full:(d + 1) * full, r * cells:(r + 1) * cells]
        sums = lax.fori_loop(c * quarter, (c + 1) * quarter, norms, sums, unroll=2)
        for k in order:
            backward(c, k).start()
        for r in range(step):
            coupled[mz * group + c * step + r] = product[c, mz, r]

    to_later.wait_recv()
    to_before.wait_recv()
    to_up.wait_recv()
    to_down.wait_recv()
    field[pl.ds(MARGIN - 1, full, stride=pitch), :] = halo[0].astype(F32)
    field[pl.ds(MARGIN + rows, full, stride=pitch), :] = halo[1].astype(F32)

    @pl.when(my > 0)
    def _():
        edge_f[0] = edge_in[0].astype(F32)

    @pl.when(my == 0)
    def _():
        edge_f[0] = jnp.zeros((2, rows, cells), F32)

    @pl.when(my < ny - 1)
    def _():
        edge_f[1] = edge_in[1].astype(F32)

    @pl.when(my == ny - 1)
    def _():
        edge_f[1] = jnp.zeros((2, rows, cells), F32)

    for f in range(2):
        for u in range(units):
            def local(z, carry):
                j = u * layers + z
                q = f * slab + j
                here = field[middle(q), :]
                south = jnp.where(
                    lane == 0, pltpu.roll(edge_f[0, f], lax.rem(cells - j, cells), 1),
                    pltpu.roll(here, 1, 1),
                )
                north = jnp.where(
                    lane == cells - 1, pltpu.roll(edge_f[1, f], cells - 1 - j, 1),
                    pltpu.roll(here, cells - 1, 1),
                )
                near = field[pl.ds(q * pitch + MARGIN - 1, rows), :]
                near = near + field[pl.ds(q * pitch + MARGIN + 1, rows), :]
                value = kappa_ref[u] * (near + south + north - 4.0 * here)
                for w in range(units):
                    value = value + blocks_ref[units * u + w].astype(F32) * field[
                        middle(f * slab + w * layers + z), :
                    ]
                before_image[q] = value
                return carry

            lax.fori_loop(0, layers, local, 0, unroll=2)

    def insert(x, carry):
        back[pl.ds(x, full, stride=rows), :] = coupled[x].astype(F32)
        return carry

    for c in range(chunks):
        for k in order:
            backward_in(c, k).wait_recv()

        def chunk_row(i, carry):
            return insert(lax.div(i, step) * group + c * step + lax.rem(i, step), carry)

        lax.fori_loop(0, nz * step, chunk_row, 0, unroll=4)

    def image(j, carry):
        ba, be = carry
        b = b_ref[j].astype(F32)
        images = []
        for f in range(2):
            q = f * slab + j
            coup = back[pl.ds(pl.multiple_of(q * rows, 8), rows), :]
            images.append(ocean * (coup + before_image[q]))
            outs[f][j] = images[f].astype(BF16)
        return ba + b * images[0], be + b * images[1]

    pair = lax.fori_loop(0, slab, image, (zero, zero), unroll=6)

    lines = [jnp.sum(v, axis=0, keepdims=True) for v in (*sums, *pair)]
    value = jnp.concatenate(lines + [jnp.zeros((3, cells), F32)], axis=0)
    base = 0
    plane = [(i, k) for i in range(ny) for k in range(nx)]
    stages = (
        ([{"lz": lax.rem(mz + k, nz)} for k in range(nz)], nz, stat_z, sr_z, mz,
         [lax.rem(mz + nz - k, nz) for k in range(nz)]),
        ([{"ty": lax.rem(my + i, ny), "tx": lax.rem(mx + k, nx)} for i, k in plane],
         ny * nx, stat_y, sr_y, my * nx + mx,
         [lax.rem(my + ny - i, ny) * nx + lax.rem(mx + nx - k, nx) for i, k in plane]),
    )
    sends = []
    for s, (peers, size, box, sem, me, sources) in enumerate(stages):
        stat_out[s] = value
        box[me] = value
        for k in range(1, size):
            copy = pltpu.make_async_remote_copy(
                src_ref=stat_out.at[s], dst_ref=box.at[me], send_sem=ss.at[base + k - 1],
                recv_sem=sem.at[me], device_id=peers[k], device_id_type=MESH,
            )
            copy.start()
            sends.append(copy)
        base += size - 1
        for k in range(1, size):
            src = sources[k]
            pltpu.make_async_remote_copy(
                src_ref=stat_out.at[s], dst_ref=box.at[src], send_sem=ss.at[0],
                recv_sem=sem.at[src], device_id=peers[k], device_id_type=MESH,
            ).wait_recv()
        value = box[0]
        for i in range(1, size):
            value = value + box[i]
    final = jnp.broadcast_to(jnp.sum(value, axis=1, keepdims=True), (8, cells))
    bb, cc, cv, ba, be = (final[i:i + 1] for i in range(5))
    line = lax.broadcasted_iota(jnp.int32, (1, cells), 1)
    top = jnp.where(line == 0, ba, jnp.where(line == 1, be, cv))
    low = jnp.where(line == 2, cc, bb)
    border_ref[...] = top / jnp.sqrt(low)

    for c in range(chunks):
        for k in order:
            forward(c, k).wait_send()
            backward(c, k).wait_send()
    to_later.wait_send()
    to_before.wait_send()
    to_up.wait_send()
    to_down.wait_send()
    for copy in sends:
        copy.wait_send()


def fast_kernel(
    sizes, span, units,
    test_hbm, dir_hbm, b_hbm, c_hbm, land_ref, active_ref, blocks_hbm, k_hbm, kappa_ref,
    out_t, out_d, border_ref, flag_ref,
    test_ref, dir_ref, b_ref, c_ref, blocks_ref, k_ref,
    wide_ref, pick, packed, arrived, product, coupled, partial, weight, place, big_k, field, back,
    before_image, halo_out, halo, edge_out, edge_in, edge_f, stat_out, stat_z, stat_y,
    ls, fs, fr, bs, br, xs, xr, ys, yr, ss, sr_z, sr_y,
):
    nx, ny, nz = sizes
    slab, rows, cells = test_ref.shape
    layers = slab // units
    full = 2 * slab
    halves = rows // span
    slots = packed.shape[0] * nz // halves
    per = slots // nz
    chunks = halves * per
    pitch = rows + 2 * MARGIN
    quad = nz * cells
    mx, my, mz = lax.axis_index("tx"), lax.axis_index("ty"), lax.axis_index("lz")
    fields = (test_ref, dir_ref)
    outs = (out_t, out_d)

    loads = [
        pltpu.make_async_copy(source, target, ls.at[i])
        for i, (source, target) in enumerate((
            (test_hbm, test_ref), (dir_hbm, dir_ref), (k_hbm, k_ref), (b_hbm, b_ref),
            (c_hbm, c_ref), (blocks_hbm, blocks_ref),
        ))
    ]
    for load in loads:
        load.start()

    barrier = pltpu.get_barrier_semaphore()
    for k in range(1, nz):
        pl.semaphore_signal(
            barrier, inc=1, device_id={"lz": lax.rem(mz + k, nz)}, device_id_type=MESH
        )
    for k in range(1, nx * ny):
        near = {"ty": lax.rem(my + k // nx, ny), "tx": lax.rem(mx + k % nx, nx)}
        pl.semaphore_signal(barrier, inc=1, device_id=near, device_id_type=MESH)

    lane = lax.broadcasted_iota(jnp.int32, (rows, cells), 1)
    line = lax.broadcasted_iota(jnp.int32, (rows, rows), 0)
    named = jnp.max(
        jnp.where(jnp.broadcast_to(active_ref[...], (rows, rows)) == line, 1.0, 0.0),
        axis=1, keepdims=True,
    )
    ocean = land_ref[...].astype(F32) * named
    weight[...] = ocean

    wet = ocean.astype(BF16)
    other = lax.broadcasted_iota(jnp.int32, (rows, rows), 1)
    earlier = jnp.where((other < line) & (other // span == line // span), 1.0, 0.0).astype(BF16)
    cell_i = lax.broadcasted_iota(jnp.int32, (cells, cells), 0)
    cell_j = lax.broadcasted_iota(jnp.int32, (cells, cells), 1)
    ahead = jnp.where(cell_i < cell_j, 1.0, 0.0).astype(BF16)
    above = jnp.dot(earlier, wet, preferred_element_type=F32).astype(BF16)
    count = jnp.dot(wet, ahead, preferred_element_type=F32)
    count = count + jnp.dot(above, jnp.ones((cells, cells), BF16), preferred_element_type=F32)
    place[...] = jnp.where(ocean > 0.0, count, -1.0)
    excess = jnp.where((ocean > 0.0) & (count >= float(slots * cells)), 1.0, 0.0)

    spot = lax.broadcasted_iota(jnp.int32, (quad, cells), 0).astype(F32)

    def choose(h, s):
        def one(i, carry):
            where = place[pl.ds(h * span + i, 1), :] - float(s * quad)
            hit = jnp.where(jnp.broadcast_to(where, (quad, cells)) == spot, 1.0, 0.0)
            pick[h * per + s, :, pl.ds(pl.multiple_of(i * cells, cells), cells)] = hit.astype(BF16)
            return carry

        lax.fori_loop(nz * s, span, one, 0, unroll=2)

    choose(0, 0)

    def middle(q, start, size):
        return pl.ds(pl.multiple_of(q * pitch + MARGIN + start, 8), size)

    def prepare(h):
        part = weight[h * span:(h + 1) * span, :]
        for f in range(2):
            def mask(j, carry):
                value = fields[f][j, h * span:(h + 1) * span, :].astype(F32) * part
                field[middle(f * slab + j, h * span, span), :] = value
                return carry

            lax.fori_loop(0, slab, mask, 0, unroll=8)

        def pack_row(i, carry):
            row = field[pl.ds(MARGIN + h * span + i, full, stride=pitch), :].astype(BF16)
            wide_ref[h, :, pl.ds(pl.multiple_of(i * cells, cells), cells)] = row
            return carry

        lax.fori_loop(0, span, pack_row, 0, unroll=4)

    def compact(h, s):
        c = h * per + s
        found = lax.dot_general(
            wide_ref[h, :, s * quad:span * cells], pick[c, :, s * quad:span * cells],
            (((1,), (1,)), ((), ())), preferred_element_type=F32,
        ).astype(BF16)
        for d in range(nz):
            packed[c, d] = found[:, d * cells:(d + 1) * cells]

    def forward(c, k):
        to = lax.rem(mz + k, nz)
        return pltpu.make_async_remote_copy(
            src_ref=packed.at[c, to], dst_ref=arrived.at[c, mz], send_sem=fs.at[c, to],
            recv_sem=fr.at[c, mz], device_id={"lz": to}, device_id_type=MESH,
        )

    def forward_in(c, k):
        src = lax.rem(mz + nz - k, nz)
        return pltpu.make_async_remote_copy(
            src_ref=arrived.at[c, src], dst_ref=arrived.at[c, src], send_sem=fs.at[c, src],
            recv_sem=fr.at[c, src], device_id={"lz": src}, device_id_type=MESH,
        )

    def backward(c, k):
        to = lax.rem(mz + k, nz)
        return pltpu.make_async_remote_copy(
            src_ref=product.at[c, to], dst_ref=coupled.at[c, mz], send_sem=bs.at[c, to],
            recv_sem=br.at[c, mz], device_id={"lz": to}, device_id_type=MESH,
        )

    def backward_in(c, k):
        src = lax.rem(mz + nz - k, nz)
        return pltpu.make_async_remote_copy(
            src_ref=product.at[c, src], dst_ref=coupled.at[c, src], send_sem=bs.at[c, src],
            recv_sem=br.at[c, src], device_id={"lz": src}, device_id_type=MESH,
        )

    order = sorted(range(1, nz), key=lambda k: -min(k, nz - k))
    loads[0].wait()
    loads[1].wait()
    for h in range(halves):
        prepare(h)
        for s in range(per):
            c = h * per + s
            if c:
                choose(h, s)
            compact(h, s)
            if c == 0:
                pl.semaphore_wait(barrier, nx * ny + nz - 2)
            for k in order:
                forward(c, k).start()
            arrived[c, mz] = packed[c, mz]

    halo_out[0] = wide_ref[halves - 1, :, (span - 1) * cells:span * cells]
    halo_out[1] = wide_ref[0, :, :cells]
    later, before = lax.rem(mx + 1, nx), lax.rem(mx + nx - 1, nx)
    to_later = pltpu.make_async_remote_copy(
        src_ref=halo_out.at[0], dst_ref=halo.at[0], send_sem=xs.at[0], recv_sem=xr.at[0],
        device_id={"tx": later}, device_id_type=MESH,
    )
    to_before = pltpu.make_async_remote_copy(
        src_ref=halo_out.at[1], dst_ref=halo.at[1], send_sem=xs.at[1], recv_sem=xr.at[1],
        device_id={"tx": before}, device_id_type=MESH,
    )
    to_later.start()
    to_before.start()
    for f in range(2):
        def edges(j, carry):
            first, last = carry
            value = field[middle(f * slab + j, 0, rows), :]
            first = jnp.where(lane == j, pltpu.roll(value, j, 1), first)
            last = jnp.where(lane == j, pltpu.roll(value, j + 1, 1), last)
            return first, last

        blank = jnp.zeros((rows, cells), F32)
        first, last = lax.fori_loop(0, slab, edges, (blank, blank), unroll=4)
        edge_out[0, f] = first.astype(BF16)
        edge_out[1, f] = last.astype(BF16)

    up, down = lax.rem(my + 1, ny), lax.rem(my + ny - 1, ny)
    to_up = pltpu.make_async_remote_copy(
        src_ref=edge_out.at[1], dst_ref=edge_in.at[0], send_sem=ys.at[0], recv_sem=yr.at[0],
        device_id={"ty": up}, device_id_type=MESH,
    )
    to_down = pltpu.make_async_remote_copy(
        src_ref=edge_out.at[0], dst_ref=edge_in.at[1], send_sem=ys.at[1], recv_sem=yr.at[1],
        device_id={"ty": down}, device_id_type=MESH,
    )
    col = units * layers * nz
    wide = nz * full

    def chooser(shape, dim, f):
        i = lax.broadcasted_iota(jnp.int32, shape, dim)
        j = lax.broadcasted_iota(jnp.int32, shape, 1 - dim)
        part, rest = i // full, lax.rem(i, full)
        field, entry = rest // slab, lax.rem(rest, slab)
        unit, layer = entry // layers, lax.rem(entry, layers)
        target = unit * (layers * nz) + part * layers + layer
        return jnp.where((target == j) & (field == f), 1.0, 0.0).astype(BF16)

    loads[2].wait()
    dense = k_ref[...]
    total = None
    for f in range(2):
        left = jnp.dot(
            chooser((wide, col), 0, f), dense, preferred_element_type=F32
        ).astype(BF16)
        both = jnp.dot(left, chooser((col, wide), 1, f), preferred_element_type=F32)
        total = both if total is None else total + both
    big_k[...] = total.astype(BF16)
    to_up.start()
    to_down.start()

    for load in loads[3:]:
        load.wait()
    zero = jnp.zeros((rows, cells), F32)
    sums = (zero, zero, zero)

    def norms(j, carry):
        bb, cc, cv = carry
        b = b_ref[j].astype(F32)
        c = c_ref[j].astype(F32)
        return bb + b * b, cc + c * c, cv + c * test_ref[j].astype(F32)

    share = slab // chunks
    for c in range(chunks):
        for k in order:
            forward_in(c, k).wait_recv()
        part = arrived[c].reshape(wide, cells)
        result = jnp.dot(big_k[...], part, preferred_element_type=F32).astype(BF16)
        for d in range(nz):
            product[c, d] = result[d * full:(d + 1) * full]
        for k in order:
            backward(c, k).start()
        coupled[c, mz] = product[c, mz]
        sums = lax.fori_loop(c * share, (c + 1) * share, norms, sums, unroll=2)
    if share * chunks < slab:
        sums = lax.fori_loop(share * chunks, slab, norms, sums)

    to_later.wait_recv()
    to_before.wait_recv()
    to_up.wait_recv()
    to_down.wait_recv()
    field[pl.ds(MARGIN - 1, full, stride=pitch), :] = halo[0].astype(F32)
    field[pl.ds(MARGIN + rows, full, stride=pitch), :] = halo[1].astype(F32)

    @pl.when(my > 0)
    def _():
        edge_f[0] = edge_in[0].astype(F32)

    @pl.when(my == 0)
    def _():
        edge_f[0] = jnp.zeros((2, rows, cells), F32)

    @pl.when(my < ny - 1)
    def _():
        edge_f[1] = edge_in[1].astype(F32)

    @pl.when(my == ny - 1)
    def _():
        edge_f[1] = jnp.zeros((2, rows, cells), F32)

    for f in range(2):
        for u in range(units):
            def local(z, carry):
                j = u * layers + z
                q = f * slab + j
                here = field[middle(q, 0, rows), :]
                south = jnp.where(
                    lane == 0, pltpu.roll(edge_f[0, f], lax.rem(cells - j, cells), 1),
                    pltpu.roll(here, 1, 1),
                )
                north = jnp.where(
                    lane == cells - 1, pltpu.roll(edge_f[1, f], cells - 1 - j, 1),
                    pltpu.roll(here, cells - 1, 1),
                )
                near = field[pl.ds(q * pitch + MARGIN - 1, rows), :]
                near = near + field[pl.ds(q * pitch + MARGIN + 1, rows), :]
                value = kappa_ref[u] * (near + south + north - 4.0 * here)
                for w in range(units):
                    value = value + blocks_ref[units * u + w].astype(F32) * field[
                        middle(f * slab + w * layers + z, 0, rows), :
                    ]
                before_image[q] = value
                return carry

            lax.fori_loop(0, layers, local, 0, unroll=2)

    none = jnp.zeros((span, cells), F32)
    pair = (none, none)
    for h in range(halves):
        for s in range(per):
            c = h * per + s
            for k in order:
                backward_in(c, k).wait_recv()
            block = jnp.concatenate([coupled[c, d] for d in range(nz)], axis=1)
            spread = jnp.dot(
                block, pick[c, :, s * quad:span * cells], preferred_element_type=F32
            )
            if s:
                spread = spread + partial[:, s * quad:span * cells]
            done = nz if s + 1 < per else span - nz * s
            for i in range(done):
                x = h * span + nz * s + i
                back[pl.ds(x, full, stride=rows), :] = spread[:, i * cells:(i + 1) * cells]
            if s + 1 < per:
                partial[:, (s + 1) * quad:span * cells] = spread[:, quad:]
        part = weight[h * span:(h + 1) * span, :]

        def image(j, carry):
            ba, be = carry
            b = b_ref[j, h * span:(h + 1) * span, :].astype(F32)
            images = []
            for f in range(2):
                q = f * slab + j
                coup = back[pl.ds(pl.multiple_of(q * rows + h * span, 8), span), :]
                images.append(part * (coup + before_image[q, h * span:(h + 1) * span, :]))
                outs[f][j, h * span:(h + 1) * span, :] = images[f].astype(BF16)
            return ba + b * images[0], be + b * images[1]

        pair = lax.fori_loop(0, slab, image, pair, unroll=6)

    lines = [jnp.sum(v, axis=0, keepdims=True) for v in (*sums, *pair, excess)]
    value = jnp.concatenate(lines + [jnp.zeros((2, cells), F32)], axis=0)
    base = 0
    plane = [(i, k) for i in range(ny) for k in range(nx)]
    stages = (
        ([{"lz": lax.rem(mz + k, nz)} for k in range(nz)], nz, stat_z, sr_z, mz,
         [lax.rem(mz + nz - k, nz) for k in range(nz)]),
        ([{"ty": lax.rem(my + i, ny), "tx": lax.rem(mx + k, nx)} for i, k in plane],
         ny * nx, stat_y, sr_y, my * nx + mx,
         [lax.rem(my + ny - i, ny) * nx + lax.rem(mx + nx - k, nx) for i, k in plane]),
    )
    sends = []
    for s, (peers, size, box, sem, me, sources) in enumerate(stages):
        stat_out[s] = value
        box[me] = value
        for k in range(1, size):
            copy = pltpu.make_async_remote_copy(
                src_ref=stat_out.at[s], dst_ref=box.at[me], send_sem=ss.at[base + k - 1],
                recv_sem=sem.at[me], device_id=peers[k], device_id_type=MESH,
            )
            copy.start()
            sends.append(copy)
        base += size - 1
        for k in range(1, size):
            src = sources[k]
            pltpu.make_async_remote_copy(
                src_ref=stat_out.at[s], dst_ref=box.at[src], send_sem=ss.at[0],
                recv_sem=sem.at[src], device_id=peers[k], device_id_type=MESH,
            ).wait_recv()
        value = box[0]
        for i in range(1, size):
            value = value + box[i]
    final = jnp.broadcast_to(jnp.sum(value, axis=1, keepdims=True), (8, cells))
    bb, cc, cv, ba, be, over = (final[i:i + 1] for i in range(6))
    line = lax.broadcasted_iota(jnp.int32, (1, cells), 1)
    top = jnp.where(line == 0, ba, jnp.where(line == 1, be, cv))
    low = jnp.where(line == 2, cc, bb)
    border_ref[...] = top / jnp.sqrt(low)
    flag_ref[0] = jnp.where(jnp.max(over) > 0.0, 1, 0)

    for c in range(chunks):
        for k in order:
            forward(c, k).wait_send()
            backward(c, k).wait_send()
    to_later.wait_send()
    to_before.wait_send()
    to_up.wait_send()
    to_down.wait_send()
    for copy in sends:
        copy.wait_send()


def dense_call(sizes, units, layers, args):
    nx, ny, nz = sizes
    slab, rows, cells = args[0].shape
    full = 2 * slab
    group = rows // nz
    chunks = 4 if group % 4 == 0 else 1
    step = group // chunks
    vmem = pl.BlockSpec(memory_space=pltpu.VMEM)
    smem = pl.BlockSpec(memory_space=pltpu.SMEM)
    hbm = pl.BlockSpec(memory_space=pl.ANY)
    dma = pltpu.SemaphoreType.DMA
    return pl.pallas_call(
        functools.partial(dense_kernel, sizes, chunks, units),
        out_shape=(
            jax.ShapeDtypeStruct((slab, rows, cells), BF16),
            jax.ShapeDtypeStruct((slab, rows, cells), BF16),
            jax.ShapeDtypeStruct((1, cells), F32),
        ),
        in_specs=[hbm] * 4 + [vmem] * 2 + [hbm] * 2 + [smem],
        out_specs=(vmem, vmem, vmem),
        scratch_shapes=[
            *[pltpu.VMEM((slab, rows, cells), BF16)] * 4,
            pltpu.VMEM(args[6].shape, BF16),
            pltpu.VMEM(args[7].shape, BF16),
            pltpu.VMEM((rows, full, cells), BF16),
            pltpu.VMEM((chunks, nz, step, full, cells), BF16),
            pltpu.VMEM((chunks, nz, step, full, cells), BF16),
            pltpu.VMEM((rows, full, cells), BF16),
            pltpu.VMEM((rows, cells), F32),
            pltpu.VMEM((nz * full, nz * full), BF16),
            pltpu.VMEM((full * (rows + 2 * MARGIN), cells), F32),
            pltpu.VMEM((full * rows, cells), F32),
            pltpu.VMEM((full, rows, cells), F32),
            pltpu.VMEM((2, full, cells), BF16),
            pltpu.VMEM((2, 2, rows, cells), BF16),
            pltpu.VMEM((2, 2, rows, cells), BF16),
            pltpu.VMEM((2, 2, rows, cells), F32),
            pltpu.VMEM((2, 8, cells), F32),
            pltpu.VMEM((nz, 8, cells), F32),
            pltpu.VMEM((ny * nx, 8, cells), F32),
            dma((6,)),
            *[dma((chunks, nz))] * 4,
            *[dma((2,))] * 4,
            dma((nx * ny + nz - 2,)),
            dma((nz,)),
            dma((ny * nx,)),
        ],
        compiler_params=pltpu.CompilerParams(
            collective_id=0, has_side_effects=True, vmem_limit_bytes=52 * 1024 * 1024
        ),
    )(*args)


def fast_call(sizes, span, units, layers, args):
    nx, ny, nz = sizes
    slab, rows, cells = args[0].shape
    full = 2 * slab
    chunks = (rows * 3 // 4) // nz
    quad = nz * cells
    vmem = pl.BlockSpec(memory_space=pltpu.VMEM)
    smem = pl.BlockSpec(memory_space=pltpu.SMEM)
    hbm = pl.BlockSpec(memory_space=pl.ANY)
    dma = pltpu.SemaphoreType.DMA
    return pl.pallas_call(
        functools.partial(fast_kernel, sizes, span, units),
        out_shape=(
            jax.ShapeDtypeStruct((slab, rows, cells), BF16),
            jax.ShapeDtypeStruct((slab, rows, cells), BF16),
            jax.ShapeDtypeStruct((1, cells), F32),
            jax.ShapeDtypeStruct((1,), jnp.int32),
        ),
        in_specs=[hbm] * 4 + [vmem] * 2 + [hbm] * 2 + [smem],
        out_specs=(vmem, vmem, vmem, smem),
        scratch_shapes=[
            *[pltpu.VMEM((slab, rows, cells), BF16)] * 4,
            pltpu.VMEM(args[6].shape, BF16),
            pltpu.VMEM(args[7].shape, BF16),
            pltpu.VMEM((rows // span, full, span * cells), BF16),
            pltpu.VMEM((chunks, quad, span * cells), BF16),
            *[pltpu.VMEM((chunks, nz, full, cells), BF16)] * 4,
            pltpu.VMEM((full, span * cells), F32),
            pltpu.VMEM((rows, cells), F32),
            pltpu.VMEM((rows, cells), F32),
            pltpu.VMEM((nz * full, nz * full), BF16),
            pltpu.VMEM((full * (rows + 2 * MARGIN), cells), F32),
            pltpu.VMEM((full * rows, cells), F32),
            pltpu.VMEM((full, rows, cells), F32),
            pltpu.VMEM((2, full, cells), BF16),
            pltpu.VMEM((2, full, cells), BF16),
            pltpu.VMEM((2, 2, rows, cells), BF16),
            pltpu.VMEM((2, 2, rows, cells), BF16),
            pltpu.VMEM((2, 2, rows, cells), F32),
            pltpu.VMEM((2, 8, cells), F32),
            pltpu.VMEM((nz, 8, cells), F32),
            pltpu.VMEM((ny * nx, 8, cells), F32),
            dma((6,)),
            *[dma((chunks, nz))] * 4,
            *[dma((2,))] * 4,
            dma((nx * ny + nz - 2,)),
            dma((nz,)),
            dma((ny * nx,)),
        ],
        compiler_params=pltpu.CompilerParams(
            collective_id=1, has_side_effects=True, vmem_limit_bytes=52 * 1024 * 1024
        ),
    )(*args)


def body(sizes, *arrays):
    nx, ny, nz = sizes
    rows, units, layers, cells = arrays[0].shape
    slab = units * layers
    wide = [v.transpose(1, 2, 0, 3).reshape(slab, rows, cells) for v in arrays[:4]]
    args = (*wide, arrays[4], arrays[5].T, arrays[6].transpose(1, 0, 2), *arrays[7:])
    args = (*[pltpu.with_memory_space_constraint(v, pltpu.HBM) for v in args[:8]], args[8])
    span = rows // 2
    if rows % 16 == 0 and (span * 3 // 4) % nz == 0:
        *quick, flag = fast_call(sizes, span, units, layers, args)
        out_t, out_d, border = lax.cond(
            flag[0] > 0, lambda: dense_call(sizes, units, layers, args), lambda: tuple(quick)
        )
    else:
        out_t, out_d, border = dense_call(sizes, units, layers, args)
    outs = [
        v.reshape(units, layers, rows, cells).transpose(2, 0, 1, 3) for v in (out_t, out_d)
    ]
    return (*outs, border[0, :3])


def solution(mesh):
    wide = P("tx", None, "lz", "ty")
    in_specs = (
        wide, wide, wide, wide, P("tx", "ty"), P("tx", "ty"), P("tx", None, "ty"), P(), P(),
    )
    sizes = tuple(mesh.shape[name] for name in ("tx", "ty", "lz"))
    return jax.shard_map(
        functools.partial(body, sizes), mesh=mesh, in_specs=in_specs,
        out_specs=(wide, wide, P()), check_vma=False,
    )
```

```python
import functools
import itertools
import math
import jax
import jax.numpy as jnp
from jax import lax
from jax.experimental import pallas as pl
from jax.experimental.pallas import tpu as pltpu
from jax.sharding import PartitionSpec as P

MESH = pl.DeviceIdType.MESH
F32 = jnp.float32
BF16 = jnp.bfloat16


MARGIN = 8


def dense_kernel(
    sizes, chunks, units,
    test_hbm, dir_hbm, b_hbm, c_hbm, land_ref, active_ref, blocks_hbm, k_hbm, kappa_ref,
    out_t, out_d, border_ref,
    test_ref, dir_ref, b_ref, c_ref, blocks_ref, k_ref,
    masked, arrived, product, coupled, weight, big_k, field, back, before_image, halo,
    edge_out, edge_in, edge_f, stat_out, stat_z, stat_y,
    ls, fs, fr, bs, br, xs, xr, ys, yr, ss, sr_z, sr_y,
):
    nx, ny, nz = sizes
    slab, rows, cells = test_ref.shape
    layers = slab // units
    full = 2 * slab
    group = rows // nz
    step = group // chunks
    pitch = rows + 2 * MARGIN
    mx, my, mz = lax.axis_index("tx"), lax.axis_index("ty"), lax.axis_index("lz")
    fields = (test_ref, dir_ref)
    outs = (out_t, out_d)

    loads = [
        pltpu.make_async_copy(source, target, ls.at[i])
        for i, (source, target) in enumerate((
            (test_hbm, test_ref), (dir_hbm, dir_ref), (k_hbm, k_ref), (b_hbm, b_ref),
            (c_hbm, c_ref), (blocks_hbm, blocks_ref),
        ))
    ]
    for load in loads:
        load.start()

    barrier = pltpu.get_barrier_semaphore()
    for k in range(1, nz):
        pl.semaphore_signal(
            barrier, inc=1, device_id={"lz": lax.rem(mz + k, nz)}, device_id_type=MESH
        )
    for k in range(1, nx * ny):
        near = {"ty": lax.rem(my + k // nx, ny), "tx": lax.rem(mx + k % nx, nx)}
        pl.semaphore_signal(barrier, inc=1, device_id=near, device_id_type=MESH)

    lane = lax.broadcasted_iota(jnp.int32, (rows, cells), 1)
    line = lax.broadcasted_iota(jnp.int32, (rows, rows), 0)
    named = jnp.max(
        jnp.where(jnp.broadcast_to(active_ref[...], (rows, rows)) == line, 1.0, 0.0),
        axis=1, keepdims=True,
    )
    weight[...] = land_ref[...].astype(F32) * named
    ocean = weight[...]

    def middle(q):
        return pl.ds(pl.multiple_of(q * pitch + MARGIN, 8), rows)

    for f in range(2):
        loads[f].wait()

        def mask(j, carry):
            field[middle(f * slab + j), :] = fields[f][j].astype(F32) * ocean
            return carry

        lax.fori_loop(0, slab, mask, 0, unroll=8)

    def pack(c):
        def pack_row(i, carry):
            x = lax.div(i, step) * group + c * step + lax.rem(i, step)
            masked[x] = field[pl.ds(MARGIN + x, full, stride=pitch), :].astype(BF16)
            return carry

        lax.fori_loop(0, nz * step, pack_row, 0, unroll=4)

    pack(0)

    pl.semaphore_wait(barrier, nx * ny + nz - 2)

    def forward(c, k):
        to = lax.rem(mz + k, nz)
        return pltpu.make_async_remote_copy(
            src_ref=masked.at[pl.ds(to * group + c * step, step)],
            dst_ref=arrived.at[c, mz],
            send_sem=fs.at[c, to],
            recv_sem=fr.at[c, mz],
            device_id={"lz": to},
            device_id_type=MESH,
        )

    def forward_in(c, k):
        src = lax.rem(mz + nz - k, nz)
        return pltpu.make_async_remote_copy(
            src_ref=arrived.at[c, src],
            dst_ref=arrived.at[c, src],
            send_sem=fs.at[c, src],
            recv_sem=fr.at[c, src],
            device_id={"lz": src},
            device_id_type=MESH,
        )

    def backward(c, k):
        to = lax.rem(mz + k, nz)
        return pltpu.make_async_remote_copy(
            src_ref=product.at[c, to],
            dst_ref=coupled.at[pl.ds(mz * group + c * step, step)],
            send_sem=bs.at[c, to],
            recv_sem=br.at[c, mz],
            device_id={"lz": to},
            device_id_type=MESH,
        )

    def backward_in(c, k):
        src = lax.rem(mz + nz - k, nz)
        return pltpu.make_async_remote_copy(
            src_ref=product.at[c, src],
            dst_ref=coupled.at[pl.ds(src * group + c * step, step)],
            send_sem=bs.at[c, src],
            recv_sem=br.at[c, src],
            device_id={"lz": src},
            device_id_type=MESH,
        )

    order = sorted(range(1, nz), key=lambda k: -min(k, nz - k))
    for c in range(1, chunks):
        pack(c)
        for k in order:
            forward(c - 1, k).start()

    def own_row(i, carry):
        arrived[lax.div(i, step), mz, lax.rem(i, step)] = masked[mz * group + i]
        return carry

    lax.fori_loop(0, group, own_row, 0)
    for k in order:
        forward(chunks - 1, k).start()
    later, before = lax.rem(mx + 1, nx), lax.rem(mx + nx - 1, nx)
    to_later = pltpu.make_async_remote_copy(
        src_ref=masked.at[rows - 1], dst_ref=halo.at[0], send_sem=xs.at[0], recv_sem=xr.at[0],
        device_id={"tx": later}, device_id_type=MESH,
    )
    to_before = pltpu.make_async_remote_copy(
        src_ref=masked.at[0], dst_ref=halo.at[1], send_sem=xs.at[1], recv_sem=xr.at[1],
        device_id={"tx": before}, device_id_type=MESH,
    )
    to_later.start()
    to_before.start()
    for f in range(2):
        def edges(j, carry):
            first, last = carry
            value = field[middle(f * slab + j), :]
            first = jnp.where(lane == j, pltpu.roll(value, j, 1), first)
            last = jnp.where(lane == j, pltpu.roll(value, j + 1, 1), last)
            return first, last

        blank = jnp.zeros((rows, cells), F32)
        first, last = lax.fori_loop(0, slab, edges, (blank, blank), unroll=4)
        edge_out[0, f] = first.astype(BF16)
        edge_out[1, f] = last.astype(BF16)

    up, down = lax.rem(my + 1, ny), lax.rem(my + ny - 1, ny)
    to_up = pltpu.make_async_remote_copy(
        src_ref=edge_out.at[1], dst_ref=edge_in.at[0], send_sem=ys.at[0], recv_sem=yr.at[0],
        device_id={"ty": up}, device_id_type=MESH,
    )
    to_down = pltpu.make_async_remote_copy(
        src_ref=edge_out.at[0], dst_ref=edge_in.at[1], send_sem=ys.at[1], recv_sem=yr.at[1],
        device_id={"ty": down}, device_id_type=MESH,
    )
    col = units * layers * nz
    wide = nz * full

    def chooser(shape, dim, f):
        i = lax.broadcasted_iota(jnp.int32, shape, dim)
        j = lax.broadcasted_iota(jnp.int32, shape, 1 - dim)
        part, rest = i // full, lax.rem(i, full)
        field, entry = rest // slab, lax.rem(rest, slab)
        unit, layer = entry // layers, lax.rem(entry, layers)
        target = unit * (layers * nz) + part * layers + layer
        return jnp.where((target == j) & (field == f), 1.0, 0.0).astype(BF16)

    loads[2].wait()
    dense = k_ref[...]
    total = None
    for f in range(2):
        left = jnp.dot(
            chooser((wide, col), 0, f), dense, preferred_element_type=F32
        ).astype(BF16)
        both = jnp.dot(left, chooser((col, wide), 1, f), preferred_element_type=F32)
        total = both if total is None else total + both
    big_k[...] = total.astype(BF16)
    to_up.start()
    to_down.start()

    for load in loads[3:]:
        load.wait()
    zero = jnp.zeros((rows, cells), F32)
    sums = (zero, zero, zero)

    def norms(j, carry):
        bb, cc, cv = carry
        b = b_ref[j].astype(F32)
        c = c_ref[j].astype(F32)
        return bb + b * b, cc + c * c, cv + c * test_ref[j].astype(F32)

    quarter = slab // chunks
    for c in range(chunks):
        for k in order:
            forward_in(c, k).wait_recv()
        part = jnp.concatenate(
            [arrived[c, :, r].reshape(wide, cells) for r in range(step)], axis=1
        )
        result = jnp.dot(big_k[...], part, preferred_element_type=F32).astype(BF16)
        for d in range(nz):
            for r in range(step):
                product[c, d, r] = result[d * full:(d + 1) * full, r * cells:(r + 1) * cells]
        sums = lax.fori_loop(c * quarter, (c + 1) * quarter, norms, sums, unroll=2)
        for k in order:
            backward(c, k).start()
        for r in range(step):
            coupled[mz * group + c * step + r] = product[c, mz, r]

    to_later.wait_recv()
    to_before.wait_recv()
    to_up.wait_recv()
    to_down.wait_recv()
    field[pl.ds(MARGIN - 1, full, stride=pitch), :] = halo[0].astype(F32)
    field[pl.ds(MARGIN + rows, full, stride=pitch), :] = halo[1].astype(F32)

    @pl.when(my > 0)
    def _():
        edge_f[0] = edge_in[0].astype(F32)

    @pl.when(my == 0)
    def _():
        edge_f[0] = jnp.zeros((2, rows, cells), F32)

    @pl.when(my < ny - 1)
    def _():
        edge_f[1] = edge_in[1].astype(F32)

    @pl.when(my == ny - 1)
    def _():
        edge_f[1] = jnp.zeros((2, rows, cells), F32)

    for f in range(2):
        for u in range(units):
            def local(z, carry):
                j = u * layers + z
                q = f * slab + j
                here = field[middle(q), :]
                south = jnp.where(
                    lane == 0, pltpu.roll(edge_f[0, f], lax.rem(cells - j, cells), 1),
                    pltpu.roll(here, 1, 1),
                )
                north = jnp.where(
                    lane == cells - 1, pltpu.roll(edge_f[1, f], cells - 1 - j, 1),
                    pltpu.roll(here, cells - 1, 1),
                )
                near = field[pl.ds(q * pitch + MARGIN - 1, rows), :]
                near = near + field[pl.ds(q * pitch + MARGIN + 1, rows), :]
                value = kappa_ref[u] * (near + south + north - 4.0 * here)
                for w in range(units):
                    value = value + blocks_ref[units * u + w].astype(F32) * field[
                        middle(f * slab + w * layers + z), :
                    ]
                before_image[q] = value
                return carry

            lax.fori_loop(0, layers, local, 0, unroll=2)

    def insert(x, carry):
        back[pl.ds(x, full, stride=rows), :] = coupled[x].astype(F32)
        return carry

    for c in range(chunks):
        for k in order:
            backward_in(c, k).wait_recv()

        def chunk_row(i, carry):
            return insert(lax.div(i, step) * group + c * step + lax.rem(i, step), carry)

        lax.fori_loop(0, nz * step, chunk_row, 0, unroll=4)

    def image(j, carry):
        ba, be = carry
        b = b_ref[j].astype(F32)
        images = []
        for f in range(2):
            q = f * slab + j
            coup = back[pl.ds(pl.multiple_of(q * rows, 8), rows), :]
            images.append(ocean * (coup + before_image[q]))
            outs[f][j] = images[f].astype(BF16)
        return ba + b * images[0], be + b * images[1]

    pair = lax.fori_loop(0, slab, image, (zero, zero), unroll=6)

    lines = [jnp.sum(v, axis=0, keepdims=True) for v in (*sums, *pair)]
    value = jnp.concatenate(lines + [jnp.zeros((3, cells), F32)], axis=0)
    base = 0
    plane = [(i, k) for i in range(ny) for k in range(nx)]
    stages = (
        ([{"lz": lax.rem(mz + k, nz)} for k in range(nz)], nz, stat_z, sr_z, mz,
         [lax.rem(mz + nz - k, nz) for k in range(nz)]),
        ([{"ty": lax.rem(my + i, ny), "tx": lax.rem(mx + k, nx)} for i, k in plane],
         ny * nx, stat_y, sr_y, my * nx + mx,
         [lax.rem(my + ny - i, ny) * nx + lax.rem(mx + nx - k, nx) for i, k in plane]),
    )
    sends = []
    for s, (peers, size, box, sem, me, sources) in enumerate(stages):
        stat_out[s] = value
        box[me] = value
        for k in range(1, size):
            copy = pltpu.make_async_remote_copy(
                src_ref=stat_out.at[s], dst_ref=box.at[me], send_sem=ss.at[base + k - 1],
                recv_sem=sem.at[me], device_id=peers[k], device_id_type=MESH,
            )
            copy.start()
            sends.append(copy)
        base += size - 1
        for k in range(1, size):
            src = sources[k]
            pltpu.make_async_remote_copy(
                src_ref=stat_out.at[s], dst_ref=box.at[src], send_sem=ss.at[0],
                recv_sem=sem.at[src], device_id=peers[k], device_id_type=MESH,
            ).wait_recv()
        value = box[0]
        for i in range(1, size):
            value = value + box[i]
    final = jnp.broadcast_to(jnp.sum(value, axis=1, keepdims=True), (8, cells))
    bb, cc, cv, ba, be = (final[i:i + 1] for i in range(5))
    line = lax.broadcasted_iota(jnp.int32, (1, cells), 1)
    top = jnp.where(line == 0, ba, jnp.where(line == 1, be, cv))
    low = jnp.where(line == 2, cc, bb)
    border_ref[...] = top / jnp.sqrt(low)

    for c in range(chunks):
        for k in order:
            forward(c, k).wait_send()
            backward(c, k).wait_send()
    to_later.wait_send()
    to_before.wait_send()
    to_up.wait_send()
    to_down.wait_send()
    for copy in sends:
        copy.wait_send()


def stage_sizes(sizes):
    names = ("lz", "ty", "tx")
    dims = [(name, i, sizes[("tx", "ty", "lz").index(name)]) for i, name in enumerate(names)]
    if sizes[0] * sizes[1] * sizes[2] <= 64:
        return [dims]
    return [dims[:1], dims[1:]]


def put_kernel(t_ref, d_ref, border_ref, out_t, out_d, out_border, line, sems):
    line[...] = border_ref[0, :line.shape[0]]
    copies = [
        pltpu.make_async_copy(source, target, sems.at[i])
        for i, (source, target) in enumerate(((t_ref, out_t), (d_ref, out_d), (line, out_border)))
    ]
    for copy in copies:
        copy.start()
    for copy in copies:
        copy.wait()


def put_call(out_t, out_d, border):
    hbm = pl.BlockSpec(memory_space=pl.ANY)
    return pl.pallas_call(
        put_kernel,
        out_shape=(
            jax.ShapeDtypeStruct(out_t.shape, BF16),
            jax.ShapeDtypeStruct(out_d.shape, BF16),
            jax.ShapeDtypeStruct((3,), F32),
        ),
        in_specs=[hbm, hbm, pl.BlockSpec(memory_space=pltpu.VMEM)],
        out_specs=(hbm, hbm, hbm),
        scratch_shapes=[pltpu.VMEM((3,), F32), pltpu.SemaphoreType.DMA((3,))],
    )(out_t, out_d, border)


def fast_kernel(
    sizes, span, units,
    test_hbm, dir_hbm, b_hbm, c_hbm, land_ref, active_ref, blocks_hbm, k_hbm, kappa_hbm,
    out_t, out_d, border_ref, flag_ref,
    test_ref, dir_ref, b_ref, c_ref, blocks_ref, k_ref,
    kappa_ref, wide_ref, pick, packed, arrived, product, coupled, partial, weight, place, big_k,
    field, b_field, back, before_image, halo_out, halo, edge_out, edge_in, edge_f, stat_out,
    *rest,
):
    nx, ny, nz = sizes
    stages = len(stage_sizes(sizes))
    boxes, rest = rest[:stages], rest[stages:]
    ls, fs, fr, bs, br, xs, xr, ys, yr, ss = rest[:10]
    stat_sems = rest[10:]
    slab, rows, cells = test_ref.shape
    layers = slab // units
    full = 2 * slab
    halves = rows // span
    slots = packed.shape[0] * nz // halves
    per = slots // nz
    chunks = halves * per
    pitch = rows + 2 * MARGIN
    quad = nz * cells
    mx, my, mz = lax.axis_index("tx"), lax.axis_index("ty"), lax.axis_index("lz")
    fields = (test_ref, dir_ref)
    outs = (out_t, out_d)

    loads = [
        pltpu.make_async_copy(source, target, ls.at[i])
        for i, (source, target) in enumerate((
            (test_hbm, test_ref), (dir_hbm, dir_ref), (b_hbm, b_ref), (k_hbm, k_ref),
            (c_hbm, c_ref), (blocks_hbm, blocks_ref), (kappa_hbm, kappa_ref),
        ))
    ]
    for load in loads:
        load.start()

    barrier = pltpu.get_barrier_semaphore()
    for k in range(1, nz):
        pl.semaphore_signal(
            barrier, inc=1, device_id={"lz": lax.rem(mz + k, nz)}, device_id_type=MESH
        )
    for k in range(1, nx * ny):
        near = {"ty": lax.rem(my + k // nx, ny), "tx": lax.rem(mx + k % nx, nx)}
        pl.semaphore_signal(barrier, inc=1, device_id=near, device_id_type=MESH)

    lane = lax.broadcasted_iota(jnp.int32, (rows, cells), 1)
    line = lax.broadcasted_iota(jnp.int32, (rows, rows), 0)
    named = jnp.max(
        jnp.where(jnp.broadcast_to(active_ref[...], (rows, rows)) == line, 1.0, 0.0),
        axis=1, keepdims=True,
    )
    ocean = land_ref[...].astype(F32) * named
    weight[...] = ocean

    wet = ocean.astype(BF16)
    other = lax.broadcasted_iota(jnp.int32, (rows, rows), 1)
    earlier = jnp.where((other < line) & (other // span == line // span), 1.0, 0.0).astype(BF16)
    cell_i = lax.broadcasted_iota(jnp.int32, (cells, cells), 0)
    cell_j = lax.broadcasted_iota(jnp.int32, (cells, cells), 1)
    ahead = jnp.where(cell_i < cell_j, 1.0, 0.0).astype(BF16)
    above = jnp.dot(earlier, wet, preferred_element_type=F32).astype(BF16)
    count = jnp.dot(wet, ahead, preferred_element_type=F32)
    count = count + jnp.dot(above, jnp.ones((cells, cells), BF16), preferred_element_type=F32)
    place[...] = jnp.where(ocean > 0.0, count, -1.0)
    excess = jnp.where((ocean > 0.0) & (count >= float(slots * cells)), 1.0, 0.0)

    spot = lax.broadcasted_iota(jnp.int32, (quad, cells), 0).astype(F32)

    def choose(h, s):
        def one(i, carry):
            where = place[pl.ds(h * span + i, 1), :] - float(s * quad)
            hit = jnp.where(jnp.broadcast_to(where, (quad, cells)) == spot, 1.0, 0.0)
            pick[h * per + s, :, pl.ds(pl.multiple_of(i * cells, cells), cells)] = hit.astype(BF16)
            return carry

        lax.fori_loop(nz * s, span, one, 0, unroll=2)

    choose(0, 0)

    def middle(q, start, size):
        return pl.ds(pl.multiple_of(q * pitch + MARGIN + start, 8), size)

    def prepare(h):
        part = weight[h * span:(h + 1) * span, :]
        for f in range(2):
            def mask(j, carry):
                value = fields[f][j, h * span:(h + 1) * span, :].astype(F32) * part
                field[middle(f * slab + j, h * span, span), :] = value
                return carry

            lax.fori_loop(0, slab, mask, 0, unroll=8)

        def widen(j, carry):
            start = pl.multiple_of(j * rows + h * span, 8)
            b_field[pl.ds(start, span), :] = b_ref[j, h * span:(h + 1) * span, :].astype(F32)
            return carry

        lax.fori_loop(0, slab, widen, 0, unroll=8)

        def pack_row(i, carry):
            spot = pl.ds(pl.multiple_of(i * cells, cells), cells)
            row = field[pl.ds(MARGIN + h * span + i, full, stride=pitch), :].astype(BF16)
            wide_ref[h, :full, spot] = row
            row = b_field[pl.ds(h * span + i, slab, stride=rows), :].astype(BF16)
            wide_ref[h, full:, spot] = row
            return carry

        lax.fori_loop(0, span, pack_row, 0, unroll=4)

    def compact(h, s):
        c = h * per + s
        found = lax.dot_general(
            wide_ref[h, :, s * quad:span * cells], pick[c, :, s * quad:span * cells],
            (((1,), (1,)), ((), ())), preferred_element_type=F32,
        ).astype(BF16)
        for d in range(nz):
            packed[c, d] = found[:, d * cells:(d + 1) * cells]

    def sent(c):
        return full if c < chunks - 1 else full + slab

    def forward(c, k):
        to = lax.rem(mz + k, nz)
        part = pl.ds(0, sent(c))
        return pltpu.make_async_remote_copy(
            src_ref=packed.at[c, to, part], dst_ref=arrived.at[c, mz, part],
            send_sem=fs.at[c, to], recv_sem=fr.at[c, mz], device_id={"lz": to},
            device_id_type=MESH,
        )

    def forward_in(c, k):
        src = lax.rem(mz + nz - k, nz)
        part = pl.ds(0, sent(c))
        return pltpu.make_async_remote_copy(
            src_ref=arrived.at[c, src, part], dst_ref=arrived.at[c, src, part],
            send_sem=fs.at[c, src], recv_sem=fr.at[c, src], device_id={"lz": src},
            device_id_type=MESH,
        )

    def backward(c, k):
        to = lax.rem(mz + k, nz)
        return pltpu.make_async_remote_copy(
            src_ref=product.at[c, to], dst_ref=coupled.at[c, mz], send_sem=bs.at[c, to],
            recv_sem=br.at[c, mz], device_id={"lz": to}, device_id_type=MESH,
        )

    def backward_in(c, k):
        src = lax.rem(mz + nz - k, nz)
        return pltpu.make_async_remote_copy(
            src_ref=product.at[c, src], dst_ref=coupled.at[c, src], send_sem=bs.at[c, src],
            recv_sem=br.at[c, src], device_id={"lz": src}, device_id_type=MESH,
        )

    order = sorted(range(1, nz), key=lambda k: -min(k, nz - k))
    for load in loads[:3]:
        load.wait()
    for h in range(halves):
        prepare(h)
        for s in range(per):
            c = h * per + s
            if c:
                choose(h, s)
            compact(h, s)
            if c == 0:
                pl.semaphore_wait(barrier, nx * ny + nz - 2)
            for k in order:
                forward(c, k).start()
            arrived[c, mz] = packed[c, mz]

    halo_out[0] = wide_ref[halves - 1, :full, (span - 1) * cells:span * cells]
    halo_out[1] = wide_ref[0, :full, :cells]
    later, before = lax.rem(mx + 1, nx), lax.rem(mx + nx - 1, nx)
    to_later = pltpu.make_async_remote_copy(
        src_ref=halo_out.at[0], dst_ref=halo.at[0], send_sem=xs.at[0], recv_sem=xr.at[0],
        device_id={"tx": later}, device_id_type=MESH,
    )
    to_before = pltpu.make_async_remote_copy(
        src_ref=halo_out.at[1], dst_ref=halo.at[1], send_sem=xs.at[1], recv_sem=xr.at[1],
        device_id={"tx": before}, device_id_type=MESH,
    )
    to_later.start()
    to_before.start()
    for f in range(2):
        def edges(j, carry):
            first, last = carry
            value = field[middle(f * slab + j, 0, rows), :]
            first = jnp.where(lane == j, pltpu.roll(value, j, 1), first)
            last = jnp.where(lane == j, pltpu.roll(value, j + 1, 1), last)
            return first, last

        blank = jnp.zeros((rows, cells), F32)
        first, last = lax.fori_loop(0, slab, edges, (blank, blank), unroll=4)
        edge_out[0, f] = first.astype(BF16)
        edge_out[1, f] = last.astype(BF16)

    up, down = lax.rem(my + 1, ny), lax.rem(my + ny - 1, ny)
    to_up = pltpu.make_async_remote_copy(
        src_ref=edge_out.at[1], dst_ref=edge_in.at[0], send_sem=ys.at[0], recv_sem=yr.at[0],
        device_id={"ty": up}, device_id_type=MESH,
    )
    to_down = pltpu.make_async_remote_copy(
        src_ref=edge_out.at[0], dst_ref=edge_in.at[1], send_sem=ys.at[1], recv_sem=yr.at[1],
        device_id={"ty": down}, device_id_type=MESH,
    )
    to_up.start()
    to_down.start()
    col = units * layers * nz
    wide = nz * full

    def chooser(shape, dim, f):
        i = lax.broadcasted_iota(jnp.int32, shape, dim)
        j = lax.broadcasted_iota(jnp.int32, shape, 1 - dim)
        part, rest = i // full, lax.rem(i, full)
        field, entry = rest // slab, lax.rem(rest, slab)
        unit, layer = entry // layers, lax.rem(entry, layers)
        target = unit * (layers * nz) + part * layers + layer
        return jnp.where((target == j) & (field == f), 1.0, 0.0).astype(BF16)

    loads[3].wait()
    dense = k_ref[...]
    total = None
    for f in range(2):
        left = jnp.dot(
            chooser((wide, col), 0, f), dense, preferred_element_type=F32
        ).astype(BF16)
        both = jnp.dot(left, chooser((col, wide), 1, f), preferred_element_type=F32)
        total = both if total is None else total + both
    big_k[...] = total.astype(BF16)

    for load in loads[4:]:
        load.wait()
    zero = jnp.zeros((rows, cells), F32)
    sums = (zero, zero, zero)

    def norms(j, carry):
        bb, cc, cv = carry
        b = b_ref[j].astype(F32)
        c = c_ref[j].astype(F32)
        return bb + b * b, cc + c * c, cv + c * test_ref[j].astype(F32)

    to_later.wait_recv()
    to_before.wait_recv()
    to_up.wait_recv()
    to_down.wait_recv()
    field[pl.ds(MARGIN - 1, full, stride=pitch), :] = halo[0].astype(F32)
    field[pl.ds(MARGIN + rows, full, stride=pitch), :] = halo[1].astype(F32)

    @pl.when(my > 0)
    def _():
        edge_f[0] = edge_in[0].astype(F32)

    @pl.when(my == 0)
    def _():
        edge_f[0] = jnp.zeros((2, rows, cells), F32)

    @pl.when(my < ny - 1)
    def _():
        edge_f[1] = edge_in[1].astype(F32)

    @pl.when(my == ny - 1)
    def _():
        edge_f[1] = jnp.zeros((2, rows, cells), F32)


    totals = [zero, zero]

    def local_part(f, u):
        def local(z, total):
            j = u * layers + z
            q = f * slab + j
            here = field[middle(q, 0, rows), :]
            south = jnp.where(
                lane == 0, pltpu.roll(edge_f[0, f], lax.rem(cells - j, cells), 1),
                pltpu.roll(here, 1, 1),
            )
            north = jnp.where(
                lane == cells - 1, pltpu.roll(edge_f[1, f], cells - 1 - j, 1),
                pltpu.roll(here, cells - 1, 1),
            )
            near = field[pl.ds(q * pitch + MARGIN - 1, rows), :]
            near = near + field[pl.ds(q * pitch + MARGIN + 1, rows), :]
            value = kappa_ref[u] * (near + south + north - 4.0 * here)
            for w in range(units):
                value = value + blocks_ref[units * u + w].astype(F32) * field[
                    middle(f * slab + w * layers + z, 0, rows), :
                ]
            before_image[q] = value
            return total + b_ref[j].astype(F32) * value

        totals[f] = lax.fori_loop(0, layers, local, totals[f], unroll=2)

    jobs = [(f, u) for f in range(2) for u in range(units)]
    each = -(-len(jobs) // chunks)

    tile = jnp.zeros((8, cells), F32)

    def dots(pair, values, weights):
        ba, be = pair
        for d in range(nz):
            y = values[d].astype(F32)
            b = weights[d, full:].astype(F32)
            ba = ba + jnp.sum((y[:slab] * b).reshape(slab // 8, 8, cells), axis=0)
            be = be + jnp.sum((y[slab:] * b).reshape(slab // 8, 8, cells), axis=0)
        return ba, be

    pair = (tile, tile)
    share = slab // chunks
    for c in range(chunks):
        for k in order:
            forward_in(c, k).wait_recv()
        part = jnp.concatenate([arrived[c, d, :full] for d in range(nz)], axis=0)
        result = jnp.dot(big_k[...], part, preferred_element_type=F32).astype(BF16)
        for d in range(nz):
            product[c, d] = result[d * full:(d + 1) * full]
        for k in order:
            backward(c, k).start()
        coupled[c, mz] = product[c, mz]
        if sent(c) > full:
            pair = dots(pair, product.at[c], arrived.at[c])
        sums = lax.fori_loop(c * share, (c + 1) * share, norms, sums, unroll=2)
        for job in jobs[c * each:(c + 1) * each]:
            local_part(*job)
    if share * chunks < slab:
        sums = lax.fori_loop(share * chunks, slab, norms, sums)

    def image(start, stop):
        part = weight[start:stop, :]

        def one(j, carry):
            for f in range(2):
                q = f * slab + j
                coup = back[pl.ds(pl.multiple_of(q * rows + start, 8), stop - start), :]
                value = part * (coup + before_image[q, start:stop, :])
                outs[f][j, start:stop, :] = value.astype(BF16)
            return carry

        lax.fori_loop(0, slab, one, 0, unroll=6)

    def begin(s, value):
        stat_out[s] = value
        _, peers, me = reduce_stages[s]
        boxes[s][me] = value
        copies = []
        for n, (peer, source) in enumerate(peers):
            copy = pltpu.make_async_remote_copy(
                src_ref=stat_out.at[s], dst_ref=boxes[s].at[me], send_sem=ss.at[bases[s] + n],
                recv_sem=stat_sems[s].at[me], device_id=peer, device_id_type=MESH,
            )
            copy.start()
            copies.append(copy)
        return copies

    def finish(s):
        for n, (peer, source) in enumerate(reduce_stages[s][1]):
            pltpu.make_async_remote_copy(
                src_ref=stat_out.at[s], dst_ref=boxes[s].at[source],
                send_sem=ss.at[bases[s] + n], recv_sem=stat_sems[s].at[source], device_id=peer,
                device_id_type=MESH,
            ).wait_recv()
        return jnp.sum(boxes[s][...], axis=0)

    reduce_stages = []
    for dims in stage_sizes(sizes):
        me = 0
        for name, at, n in dims:
            me = me * n + lax.axis_index(name)
        peers = []
        for shift in itertools.product(*[range(n) for _, _, n in dims]):
            if any(shift):
                peer = {
                    name: lax.rem(lax.axis_index(name) + k, n)
                    for (name, _, n), k in zip(dims, shift)
                }
                source = 0
                for (name, _, n), k in zip(dims, shift):
                    source = source * n + lax.rem(lax.axis_index(name) + n - k, n)
                peers.append((peer, source))
        reduce_stages.append((dims, peers, me))
    bases = [sum(len(r[1]) for r in reduce_stages[:s]) for s in range(stages)]
    sends = []

    seat = lax.broadcasted_iota(jnp.int32, (8, cells), 0)
    spot = lax.broadcasted_iota(jnp.int32, (8, cells), 1)
    for h in range(halves):
        drawn = 0
        for s in range(per):
            c = h * per + s
            for k in order:
                backward_in(c, k).wait_recv()
            if sent(c) == full:
                pair = dots(pair, coupled.at[c], packed.at[c])
            if c == chunks - 2:
                ba, be = (
                    jnp.sum(v, axis=0, keepdims=True) + jnp.sum(w, axis=0, keepdims=True)
                    for v, w in zip(pair, [ocean * v for v in totals])
                )
                lines = [jnp.sum(v, axis=0, keepdims=True) for v in sums]
                lines += [ba, be, jnp.sum(excess, axis=0, keepdims=True)]
                lines += [jnp.zeros((2, cells), F32)]
                value = jnp.sum(jnp.concatenate(lines, axis=0), axis=1, keepdims=True)
                value = jnp.where(seat == spot, jnp.broadcast_to(value, (8, cells)), 0.0)
                sends += begin(0, jnp.sum(value, axis=0, keepdims=True))
            block = jnp.concatenate([coupled[c, d] for d in range(nz)], axis=1)
            spread = jnp.dot(
                block, pick[c, :, s * quad:span * cells], preferred_element_type=F32
            )
            if s:
                spread = spread + partial[:, s * quad:span * cells]
            done = nz if s + 1 < per else span - nz * s
            for i in range(done):
                x = h * span + nz * s + i
                back[pl.ds(x, full, stride=rows), :] = spread[:, i * cells:(i + 1) * cells]
            if s + 1 < per:
                partial[:, (s + 1) * quad:span * cells] = spread[:, quad:]
            ready = (nz * s + done) // 8 * 8
            if s == per - 1 or (h == halves - 1 and s == per - 2 and ready > drawn):
                image(h * span + drawn, h * span + ready)
                drawn = ready

    value = finish(0)
    for s in range(1, stages):
        sends += begin(s, value)
        value = finish(s)
    value = jnp.broadcast_to(value, (8, cells))
    top = jnp.where(spot < 2, pltpu.roll(value, cells - 3, 1), value)
    low = jnp.where(spot == 0, value, pltpu.roll(value, 1, 1))
    border_ref[...] = (top / jnp.sqrt(low))[:1]
    flag_ref[0] = jnp.where(jnp.sum(jnp.where(spot == 5, value, 0.0)) > 0.0, 1, 0)

    for c in range(chunks):
        for k in order:
            forward(c, k).wait_send()
            backward(c, k).wait_send()
    to_later.wait_send()
    to_before.wait_send()
    to_up.wait_send()
    to_down.wait_send()
    for copy in sends:
        copy.wait_send()


def dense_call(sizes, units, layers, args):
    nx, ny, nz = sizes
    slab, rows, cells = args[0].shape
    full = 2 * slab
    group = rows // nz
    chunks = 4 if group % 4 == 0 else 1
    step = group // chunks
    vmem = pl.BlockSpec(memory_space=pltpu.VMEM)
    smem = pl.BlockSpec(memory_space=pltpu.SMEM)
    hbm = pl.BlockSpec(memory_space=pl.ANY)
    dma = pltpu.SemaphoreType.DMA
    return pl.pallas_call(
        functools.partial(dense_kernel, sizes, chunks, units),
        out_shape=(
            jax.ShapeDtypeStruct((slab, rows, cells), BF16),
            jax.ShapeDtypeStruct((slab, rows, cells), BF16),
            jax.ShapeDtypeStruct((1, cells), F32),
        ),
        in_specs=[hbm] * 4 + [vmem] * 2 + [hbm] * 2 + [smem],
        out_specs=(vmem, vmem, vmem),
        scratch_shapes=[
            *[pltpu.VMEM((slab, rows, cells), BF16)] * 4,
            pltpu.VMEM(args[6].shape, BF16),
            pltpu.VMEM(args[7].shape, BF16),
            pltpu.VMEM((rows, full, cells), BF16),
            pltpu.VMEM((chunks, nz, step, full, cells), BF16),
            pltpu.VMEM((chunks, nz, step, full, cells), BF16),
            pltpu.VMEM((rows, full, cells), BF16),
            pltpu.VMEM((rows, cells), F32),
            pltpu.VMEM((nz * full, nz * full), BF16),
            pltpu.VMEM((full * (rows + 2 * MARGIN), cells), F32),
            pltpu.VMEM((full * rows, cells), F32),
            pltpu.VMEM((full, rows, cells), F32),
            pltpu.VMEM((2, full, cells), BF16),
            pltpu.VMEM((2, 2, rows, cells), BF16),
            pltpu.VMEM((2, 2, rows, cells), BF16),
            pltpu.VMEM((2, 2, rows, cells), F32),
            pltpu.VMEM((2, 8, cells), F32),
            pltpu.VMEM((nz, 8, cells), F32),
            pltpu.VMEM((ny * nx, 8, cells), F32),
            dma((6,)),
            *[dma((chunks, nz))] * 4,
            *[dma((2,))] * 4,
            dma((nx * ny + nz - 2,)),
            dma((nz,)),
            dma((ny * nx,)),
        ],
        compiler_params=pltpu.CompilerParams(
            collective_id=0, has_side_effects=True, vmem_limit_bytes=52 * 1024 * 1024
        ),
    )(*args)


def fast_call(sizes, span, units, layers, args):
    nx, ny, nz = sizes
    slab, rows, cells = args[0].shape
    full = 2 * slab
    chunks = (rows * 3 // 4) // nz
    quad = nz * cells
    groups = [math.prod(n for _, _, n in dims) for dims in stage_sizes(sizes)]
    vmem = pl.BlockSpec(memory_space=pltpu.VMEM)
    smem = pl.BlockSpec(memory_space=pltpu.SMEM)
    hbm = pl.BlockSpec(memory_space=pl.ANY)
    dma = pltpu.SemaphoreType.DMA
    return pl.pallas_call(
        functools.partial(fast_kernel, sizes, span, units),
        out_shape=(
            jax.ShapeDtypeStruct((slab, rows, cells), BF16),
            jax.ShapeDtypeStruct((slab, rows, cells), BF16),
            jax.ShapeDtypeStruct((1, cells), F32),
            jax.ShapeDtypeStruct((1,), jnp.int32),
        ),
        in_specs=[hbm] * 4 + [vmem] * 2 + [hbm] * 3,
        out_specs=(vmem, vmem, vmem, smem),
        scratch_shapes=[
            *[pltpu.VMEM((slab, rows, cells), BF16)] * 4,
            pltpu.VMEM(args[6].shape, BF16),
            pltpu.VMEM(args[7].shape, BF16),
            pltpu.SMEM(args[8].shape, F32),
            pltpu.VMEM((rows // span, full + slab, span * cells), BF16),
            pltpu.VMEM((chunks, quad, span * cells), BF16),
            *[pltpu.VMEM((chunks, nz, full + slab, cells), BF16)] * 2,
            *[pltpu.VMEM((chunks, nz, full, cells), BF16)] * 2,
            pltpu.VMEM((full, span * cells), F32),
            pltpu.VMEM((rows, cells), F32),
            pltpu.VMEM((rows, cells), F32),
            pltpu.VMEM((nz * full, nz * full), BF16),
            pltpu.VMEM((full * (rows + 2 * MARGIN), cells), F32),
            pltpu.VMEM((slab * rows, cells), F32),
            pltpu.VMEM((full * rows, cells), F32),
            pltpu.VMEM((full, rows, cells), F32),
            pltpu.VMEM((2, full, cells), BF16),
            pltpu.VMEM((2, full, cells), BF16),
            pltpu.VMEM((2, 2, rows, cells), BF16),
            pltpu.VMEM((2, 2, rows, cells), BF16),
            pltpu.VMEM((2, 2, rows, cells), F32),
            pltpu.VMEM((len(groups), 1, cells), F32),
            *[pltpu.VMEM((n, 1, cells), F32) for n in groups],
            dma((7,)),
            *[dma((chunks, nz))] * 4,
            *[dma((2,))] * 4,
            dma((sum(groups) - len(groups),)),
            *[dma((n,)) for n in groups],
        ],
        compiler_params=pltpu.CompilerParams(
            collective_id=1, has_side_effects=True, vmem_limit_bytes=52 * 1024 * 1024
        ),
    )(*args)


def body(sizes, *arrays):
    nx, ny, nz = sizes
    rows, units, layers, cells = arrays[0].shape
    slab = units * layers
    wide = [v.transpose(1, 2, 0, 3).reshape(slab, rows, cells) for v in arrays[:4]]
    args = (*wide, arrays[4], arrays[5].T, arrays[6].transpose(1, 0, 2), *arrays[7:])
    held = [pltpu.with_memory_space_constraint(v, pltpu.HBM) for v in args]
    span = rows // 2
    if rows % 16 == 0 and (span * 3 // 4) % nz == 0:
        *quick, flag = fast_call(sizes, span, units, layers, held)
        out_t, out_d, border = lax.cond(
            flag[0] > 0, lambda: dense_call(sizes, units, layers, held), lambda: tuple(quick)
        )
    else:
        out_t, out_d, border = dense_call(sizes, units, layers, held)
    out_t, out_d, border = put_call(out_t, out_d, border)
    outs = [
        v.reshape(units, layers, rows, cells).transpose(2, 0, 1, 3) for v in (out_t, out_d)
    ]
    return (*outs, border)


def solution(mesh):
    wide = P("tx", None, "lz", "ty")
    in_specs = (
        wide, wide, wide, wide, P("tx", "ty"), P("tx", "ty"), P("tx", None, "ty"), P(), P(),
    )
    sizes = tuple(mesh.shape[name] for name in ("tx", "ty", "lz"))
    return jax.shard_map(
        functools.partial(body, sizes), mesh=mesh, in_specs=in_specs,
        out_specs=(wide, wide, P()), check_vma=False,
    )
```

```python
import functools
import itertools
import math
import jax
import jax.numpy as jnp
from jax import lax
from jax.experimental import pallas as pl
from jax.experimental.pallas import tpu as pltpu
from jax.sharding import PartitionSpec as P

MESH = pl.DeviceIdType.MESH
F32 = jnp.float32
BF16 = jnp.bfloat16


MARGIN = 8


def dense_kernel(
    sizes, chunks, units,
    test_hbm, dir_hbm, b_hbm, c_hbm, land_ref, active_ref, blocks_hbm, k_hbm, kappa_ref,
    out_t, out_d, border_ref,
    test_ref, dir_ref, b_ref, c_ref, blocks_ref, k_ref,
    masked, arrived, product, coupled, weight, big_k, field, back, before_image, halo,
    edge_out, edge_in, edge_f, stat_out, stat_z, stat_y,
    ls, fs, fr, bs, br, xs, xr, ys, yr, ss, sr_z, sr_y,
):
    nx, ny, nz = sizes
    slab, rows, cells = test_ref.shape
    layers = slab // units
    full = 2 * slab
    group = rows // nz
    step = group // chunks
    pitch = rows + 2 * MARGIN
    mx, my, mz = lax.axis_index("tx"), lax.axis_index("ty"), lax.axis_index("lz")
    fields = (test_ref, dir_ref)
    outs = (out_t, out_d)

    loads = [
        pltpu.make_async_copy(source, target, ls.at[i])
        for i, (source, target) in enumerate((
            (test_hbm, test_ref), (dir_hbm, dir_ref), (k_hbm, k_ref), (b_hbm, b_ref),
            (c_hbm, c_ref), (blocks_hbm, blocks_ref),
        ))
    ]
    for load in loads:
        load.start()

    barrier = pltpu.get_barrier_semaphore()
    for k in range(1, nz):
        pl.semaphore_signal(
            barrier, inc=1, device_id={"lz": lax.rem(mz + k, nz)}, device_id_type=MESH
        )
    for k in range(1, nx * ny):
        near = {"ty": lax.rem(my + k // nx, ny), "tx": lax.rem(mx + k % nx, nx)}
        pl.semaphore_signal(barrier, inc=1, device_id=near, device_id_type=MESH)

    lane = lax.broadcasted_iota(jnp.int32, (rows, cells), 1)
    line = lax.broadcasted_iota(jnp.int32, (rows, rows), 0)
    named = jnp.max(
        jnp.where(jnp.broadcast_to(active_ref[...], (rows, rows)) == line, 1.0, 0.0),
        axis=1, keepdims=True,
    )
    weight[...] = land_ref[...].astype(F32) * named
    ocean = weight[...]

    def middle(q):
        return pl.ds(pl.multiple_of(q * pitch + MARGIN, 8), rows)

    for f in range(2):
        loads[f].wait()

        def mask(j, carry):
            field[middle(f * slab + j), :] = fields[f][j].astype(F32) * ocean
            return carry

        lax.fori_loop(0, slab, mask, 0, unroll=8)

    def pack(c):
        def pack_row(i, carry):
            x = lax.div(i, step) * group + c * step + lax.rem(i, step)
            masked[x] = field[pl.ds(MARGIN + x, full, stride=pitch), :].astype(BF16)
            return carry

        lax.fori_loop(0, nz * step, pack_row, 0, unroll=4)

    pack(0)

    pl.semaphore_wait(barrier, nx * ny + nz - 2)

    def forward(c, k):
        to = lax.rem(mz + k, nz)
        return pltpu.make_async_remote_copy(
            src_ref=masked.at[pl.ds(to * group + c * step, step)],
            dst_ref=arrived.at[c, mz],
            send_sem=fs.at[c, to],
            recv_sem=fr.at[c, mz],
            device_id={"lz": to},
            device_id_type=MESH,
        )

    def forward_in(c, k):
        src = lax.rem(mz + nz - k, nz)
        return pltpu.make_async_remote_copy(
            src_ref=arrived.at[c, src],
            dst_ref=arrived.at[c, src],
            send_sem=fs.at[c, src],
            recv_sem=fr.at[c, src],
            device_id={"lz": src},
            device_id_type=MESH,
        )

    def backward(c, k):
        to = lax.rem(mz + k, nz)
        return pltpu.make_async_remote_copy(
            src_ref=product.at[c, to],
            dst_ref=coupled.at[pl.ds(mz * group + c * step, step)],
            send_sem=bs.at[c, to],
            recv_sem=br.at[c, mz],
            device_id={"lz": to},
            device_id_type=MESH,
        )

    def backward_in(c, k):
        src = lax.rem(mz + nz - k, nz)
        return pltpu.make_async_remote_copy(
            src_ref=product.at[c, src],
            dst_ref=coupled.at[pl.ds(src * group + c * step, step)],
            send_sem=bs.at[c, src],
            recv_sem=br.at[c, src],
            device_id={"lz": src},
            device_id_type=MESH,
        )

    order = sorted(range(1, nz), key=lambda k: -min(k, nz - k))
    for c in range(1, chunks):
        pack(c)
        for k in order:
            forward(c - 1, k).start()

    def own_row(i, carry):
        arrived[lax.div(i, step), mz, lax.rem(i, step)] = masked[mz * group + i]
        return carry

    lax.fori_loop(0, group, own_row, 0)
    for k in order:
        forward(chunks - 1, k).start()
    later, before = lax.rem(mx + 1, nx), lax.rem(mx + nx - 1, nx)
    to_later = pltpu.make_async_remote_copy(
        src_ref=masked.at[rows - 1], dst_ref=halo.at[0], send_sem=xs.at[0], recv_sem=xr.at[0],
        device_id={"tx": later}, device_id_type=MESH,
    )
    to_before = pltpu.make_async_remote_copy(
        src_ref=masked.at[0], dst_ref=halo.at[1], send_sem=xs.at[1], recv_sem=xr.at[1],
        device_id={"tx": before}, device_id_type=MESH,
    )
    to_later.start()
    to_before.start()
    for f in range(2):
        def edges(j, carry):
            first, last = carry
            value = field[middle(f * slab + j), :]
            first = jnp.where(lane == j, pltpu.roll(value, j, 1), first)
            last = jnp.where(lane == j, pltpu.roll(value, j + 1, 1), last)
            return first, last

        blank = jnp.zeros((rows, cells), F32)
        first, last = lax.fori_loop(0, slab, edges, (blank, blank), unroll=4)
        edge_out[0, f] = first.astype(BF16)
        edge_out[1, f] = last.astype(BF16)

    up, down = lax.rem(my + 1, ny), lax.rem(my + ny - 1, ny)
    to_up = pltpu.make_async_remote_copy(
        src_ref=edge_out.at[1], dst_ref=edge_in.at[0], send_sem=ys.at[0], recv_sem=yr.at[0],
        device_id={"ty": up}, device_id_type=MESH,
    )
    to_down = pltpu.make_async_remote_copy(
        src_ref=edge_out.at[0], dst_ref=edge_in.at[1], send_sem=ys.at[1], recv_sem=yr.at[1],
        device_id={"ty": down}, device_id_type=MESH,
    )
    col = units * layers * nz
    wide = nz * full

    def chooser(shape, dim, f):
        i = lax.broadcasted_iota(jnp.int32, shape, dim)
        j = lax.broadcasted_iota(jnp.int32, shape, 1 - dim)
        part, rest = i // full, lax.rem(i, full)
        field, entry = rest // slab, lax.rem(rest, slab)
        unit, layer = entry // layers, lax.rem(entry, layers)
        target = unit * (layers * nz) + part * layers + layer
        return jnp.where((target == j) & (field == f), 1.0, 0.0).astype(BF16)

    loads[2].wait()
    dense = k_ref[...]
    total = None
    for f in range(2):
        left = jnp.dot(
            chooser((wide, col), 0, f), dense, preferred_element_type=F32
        ).astype(BF16)
        both = jnp.dot(left, chooser((col, wide), 1, f), preferred_element_type=F32)
        total = both if total is None else total + both
    big_k[...] = total.astype(BF16)
    to_up.start()
    to_down.start()

    for load in loads[3:]:
        load.wait()
    zero = jnp.zeros((rows, cells), F32)
    sums = (zero, zero, zero)

    def norms(j, carry):
        bb, cc, cv = carry
        b = b_ref[j].astype(F32)
        c = c_ref[j].astype(F32)
        return bb + b * b, cc + c * c, cv + c * test_ref[j].astype(F32)

    quarter = slab // chunks
    for c in range(chunks):
        for k in order:
            forward_in(c, k).wait_recv()
        part = jnp.concatenate(
            [arrived[c, :, r].reshape(wide, cells) for r in range(step)], axis=1
        )
        result = jnp.dot(big_k[...], part, preferred_element_type=F32).astype(BF16)
        for d in range(nz):
            for r in range(step):
                product[c, d, r] = result[d * full:(d + 1) * full, r * cells:(r + 1) * cells]
        sums = lax.fori_loop(c * quarter, (c + 1) * quarter, norms, sums, unroll=2)
        for k in order:
            backward(c, k).start()
        for r in range(step):
            coupled[mz * group + c * step + r] = product[c, mz, r]

    to_later.wait_recv()
    to_before.wait_recv()
    to_up.wait_recv()
    to_down.wait_recv()
    field[pl.ds(MARGIN - 1, full, stride=pitch), :] = halo[0].astype(F32)
    field[pl.ds(MARGIN + rows, full, stride=pitch), :] = halo[1].astype(F32)

    @pl.when(my > 0)
    def _():
        edge_f[0] = edge_in[0].astype(F32)

    @pl.when(my == 0)
    def _():
        edge_f[0] = jnp.zeros((2, rows, cells), F32)

    @pl.when(my < ny - 1)
    def _():
        edge_f[1] = edge_in[1].astype(F32)

    @pl.when(my == ny - 1)
    def _():
        edge_f[1] = jnp.zeros((2, rows, cells), F32)

    for f in range(2):
        for u in range(units):
            def local(z, carry):
                j = u * layers + z
                q = f * slab + j
                here = field[middle(q), :]
                south = jnp.where(
                    lane == 0, pltpu.roll(edge_f[0, f], lax.rem(cells - j, cells), 1),
                    pltpu.roll(here, 1, 1),
                )
                north = jnp.where(
                    lane == cells - 1, pltpu.roll(edge_f[1, f], cells - 1 - j, 1),
                    pltpu.roll(here, cells - 1, 1),
                )
                near = field[pl.ds(q * pitch + MARGIN - 1, rows), :]
                near = near + field[pl.ds(q * pitch + MARGIN + 1, rows), :]
                value = kappa_ref[u] * (near + south + north - 4.0 * here)
                for w in range(units):
                    value = value + blocks_ref[units * u + w].astype(F32) * field[
                        middle(f * slab + w * layers + z), :
                    ]
                before_image[q] = value
                return carry

            lax.fori_loop(0, layers, local, 0, unroll=2)

    def insert(x, carry):
        back[pl.ds(x, full, stride=rows), :] = coupled[x].astype(F32)
        return carry

    for c in range(chunks):
        for k in order:
            backward_in(c, k).wait_recv()

        def chunk_row(i, carry):
            return insert(lax.div(i, step) * group + c * step + lax.rem(i, step), carry)

        lax.fori_loop(0, nz * step, chunk_row, 0, unroll=4)

    def image(j, carry):
        ba, be = carry
        b = b_ref[j].astype(F32)
        images = []
        for f in range(2):
            q = f * slab + j
            coup = back[pl.ds(pl.multiple_of(q * rows, 8), rows), :]
            images.append(ocean * (coup + before_image[q]))
            outs[f][j] = images[f].astype(BF16)
        return ba + b * images[0], be + b * images[1]

    pair = lax.fori_loop(0, slab, image, (zero, zero), unroll=6)

    lines = [jnp.sum(v, axis=0, keepdims=True) for v in (*sums, *pair)]
    value = jnp.concatenate(lines + [jnp.zeros((3, cells), F32)], axis=0)
    base = 0
    plane = [(i, k) for i in range(ny) for k in range(nx)]
    stages = (
        ([{"lz": lax.rem(mz + k, nz)} for k in range(nz)], nz, stat_z, sr_z, mz,
         [lax.rem(mz + nz - k, nz) for k in range(nz)]),
        ([{"ty": lax.rem(my + i, ny), "tx": lax.rem(mx + k, nx)} for i, k in plane],
         ny * nx, stat_y, sr_y, my * nx + mx,
         [lax.rem(my + ny - i, ny) * nx + lax.rem(mx + nx - k, nx) for i, k in plane]),
    )
    sends = []
    for s, (peers, size, box, sem, me, sources) in enumerate(stages):
        stat_out[s] = value
        box[me] = value
        for k in range(1, size):
            copy = pltpu.make_async_remote_copy(
                src_ref=stat_out.at[s], dst_ref=box.at[me], send_sem=ss.at[base + k - 1],
                recv_sem=sem.at[me], device_id=peers[k], device_id_type=MESH,
            )
            copy.start()
            sends.append(copy)
        base += size - 1
        for k in range(1, size):
            src = sources[k]
            pltpu.make_async_remote_copy(
                src_ref=stat_out.at[s], dst_ref=box.at[src], send_sem=ss.at[0],
                recv_sem=sem.at[src], device_id=peers[k], device_id_type=MESH,
            ).wait_recv()
        value = box[0]
        for i in range(1, size):
            value = value + box[i]
    final = jnp.broadcast_to(jnp.sum(value, axis=1, keepdims=True), (8, cells))
    bb, cc, cv, ba, be = (final[i:i + 1] for i in range(5))
    line = lax.broadcasted_iota(jnp.int32, (1, cells), 1)
    top = jnp.where(line == 0, ba, jnp.where(line == 1, be, cv))
    low = jnp.where(line == 2, cc, bb)
    border_ref[...] = top / jnp.sqrt(low)

    for c in range(chunks):
        for k in order:
            forward(c, k).wait_send()
            backward(c, k).wait_send()
    to_later.wait_send()
    to_before.wait_send()
    to_up.wait_send()
    to_down.wait_send()
    for copy in sends:
        copy.wait_send()


def stage_sizes(sizes):
    names = ("lz", "ty", "tx")
    dims = [(name, i, sizes[("tx", "ty", "lz").index(name)]) for i, name in enumerate(names)]
    if sizes[0] * sizes[1] * sizes[2] <= 64:
        return [dims]
    return [dims[:1], dims[1:]]


def put_kernel(t_ref, d_ref, border_ref, out_t, out_d, out_border, line, sems):
    line[...] = border_ref[0, :line.shape[0]]
    copies = [
        pltpu.make_async_copy(source, target, sems.at[i])
        for i, (source, target) in enumerate(((t_ref, out_t), (d_ref, out_d), (line, out_border)))
    ]
    for copy in copies:
        copy.start()
    for copy in copies:
        copy.wait()


def put_call(out_t, out_d, border):
    hbm = pl.BlockSpec(memory_space=pl.ANY)
    return pl.pallas_call(
        put_kernel,
        out_shape=(
            jax.ShapeDtypeStruct(out_t.shape, BF16),
            jax.ShapeDtypeStruct(out_d.shape, BF16),
            jax.ShapeDtypeStruct((3,), F32),
        ),
        in_specs=[hbm, hbm, pl.BlockSpec(memory_space=pltpu.VMEM)],
        out_specs=(hbm, hbm, hbm),
        scratch_shapes=[pltpu.VMEM((3,), F32), pltpu.SemaphoreType.DMA((3,))],
    )(out_t, out_d, border)


def fast_kernel(
    sizes, span, units,
    test_hbm, dir_hbm, b_hbm, c_hbm, land_ref, active_ref, blocks_hbm, k_hbm, kappa_hbm,
    out_t, out_d, border_ref, flag_ref,
    test_ref, dir_ref, b_ref, c_ref, blocks_ref, k_ref,
    kappa_ref, wide_ref, pick, packed, arrived, product, coupled, partial, weight, place, big_k,
    field, b_field, back, before_image, halo_out, halo, edge_out, edge_in, edge_f, stat_out,
    *rest,
):
    nx, ny, nz = sizes
    stages = len(stage_sizes(sizes))
    boxes, rest = rest[:stages], rest[stages:]
    ls, fs, fr, bs, br, xs, xr, ys, yr, ss = rest[:10]
    stat_sems = rest[10]
    slab, rows, cells = test_ref.shape
    layers = slab // units
    full = 2 * slab
    halves = rows // span
    slots = packed.shape[0] * nz // halves
    per = slots // nz
    chunks = halves * per
    pitch = rows + 2 * MARGIN
    quad = nz * cells
    mx, my, mz = lax.axis_index("tx"), lax.axis_index("ty"), lax.axis_index("lz")
    fields = (test_ref, dir_ref)
    outs = (out_t, out_d)

    loads = [
        pltpu.make_async_copy(source, target, ls.at[i])
        for i, (source, target) in enumerate((
            (test_hbm, test_ref), (dir_hbm, dir_ref), (b_hbm, b_ref), (k_hbm, k_ref),
            (c_hbm, c_ref), (blocks_hbm, blocks_ref), (kappa_hbm, kappa_ref),
        ))
    ]
    for load in loads:
        load.start()

    barrier = pltpu.get_barrier_semaphore()
    for k in range(1, nz):
        pl.semaphore_signal(
            barrier, inc=1, device_id={"lz": lax.rem(mz + k, nz)}, device_id_type=MESH
        )
    for k in range(1, nx * ny):
        near = {"ty": lax.rem(my + k // nx, ny), "tx": lax.rem(mx + k % nx, nx)}
        pl.semaphore_signal(barrier, inc=1, device_id=near, device_id_type=MESH)

    lane = lax.broadcasted_iota(jnp.int32, (rows, cells), 1)
    line = lax.broadcasted_iota(jnp.int32, (rows, rows), 0)
    named = jnp.max(
        jnp.where(jnp.broadcast_to(active_ref[...], (rows, rows)) == line, 1.0, 0.0),
        axis=1, keepdims=True,
    )
    ocean = land_ref[...].astype(F32) * named
    weight[...] = ocean

    wet = ocean.astype(BF16)
    other = lax.broadcasted_iota(jnp.int32, (rows, rows), 1)
    earlier = jnp.where((other < line) & (other // span == line // span), 1.0, 0.0).astype(BF16)
    cell_i = lax.broadcasted_iota(jnp.int32, (cells, cells), 0)
    cell_j = lax.broadcasted_iota(jnp.int32, (cells, cells), 1)
    ahead = jnp.where(cell_i < cell_j, 1.0, 0.0).astype(BF16)
    above = jnp.dot(earlier, wet, preferred_element_type=F32).astype(BF16)
    count = jnp.dot(wet, ahead, preferred_element_type=F32)
    count = count + jnp.dot(above, jnp.ones((cells, cells), BF16), preferred_element_type=F32)
    place[...] = jnp.where(ocean > 0.0, count, -1.0)
    excess = jnp.where((ocean > 0.0) & (count >= float(slots * cells)), 1.0, 0.0)

    spot = lax.broadcasted_iota(jnp.int32, (quad, cells), 0).astype(F32)

    def choose(h, s):
        def one(i, carry):
            where = place[pl.ds(h * span + i, 1), :] - float(s * quad)
            hit = jnp.where(jnp.broadcast_to(where, (quad, cells)) == spot, 1.0, 0.0)
            pick[h * per + s, :, pl.ds(pl.multiple_of(i * cells, cells), cells)] = hit.astype(BF16)
            return carry

        lax.fori_loop(nz * s, span, one, 0, unroll=2)

    choose(0, 0)

    def middle(q, start, size):
        return pl.ds(pl.multiple_of(q * pitch + MARGIN + start, 8), size)

    def prepare(h):
        part = weight[h * span:(h + 1) * span, :]
        for f in range(2):
            def mask(j, carry):
                value = fields[f][j, h * span:(h + 1) * span, :].astype(F32) * part
                field[middle(f * slab + j, h * span, span), :] = value
                return carry

            lax.fori_loop(0, slab, mask, 0, unroll=8)

        def widen(j, carry):
            start = pl.multiple_of(j * rows + h * span, 8)
            b_field[pl.ds(start, span), :] = b_ref[j, h * span:(h + 1) * span, :].astype(F32)
            return carry

        lax.fori_loop(0, slab, widen, 0, unroll=8)

        def pack_row(i, carry):
            spot = pl.ds(pl.multiple_of(i * cells, cells), cells)
            row = field[pl.ds(MARGIN + h * span + i, full, stride=pitch), :].astype(BF16)
            wide_ref[h, :full, spot] = row
            row = b_field[pl.ds(h * span + i, slab, stride=rows), :].astype(BF16)
            wide_ref[h, full:, spot] = row
            return carry

        lax.fori_loop(0, span, pack_row, 0, unroll=4)

    def compact(h, s):
        c = h * per + s
        found = lax.dot_general(
            wide_ref[h, :, s * quad:span * cells], pick[c, :, s * quad:span * cells],
            (((1,), (1,)), ((), ())), preferred_element_type=F32,
        ).astype(BF16)
        for d in range(nz):
            packed[c, d] = found[:, d * cells:(d + 1) * cells]

    def target(k):
        down = nz - k
        low = down - jnp.where(down <= mz, 1, 0)
        high = k - 1 + jnp.where(k - 1 >= mz, 1, 0)
        return jnp.where(mz < nz // 2, low, high)

    def forward(c, k):
        to = target(k)
        return pltpu.make_async_remote_copy(
            src_ref=packed.at[c, to, pl.ds(0, full)], dst_ref=arrived.at[c, mz],
            send_sem=fs.at[c, to], recv_sem=fr.at[c, mz], device_id={"lz": to},
            device_id_type=MESH,
        )

    def forward_in(c, k):
        src = lax.rem(mz + nz - k, nz)
        return pltpu.make_async_remote_copy(
            src_ref=arrived.at[c, src], dst_ref=arrived.at[c, src],
            send_sem=fs.at[c, src], recv_sem=fr.at[c, src], device_id={"lz": src},
            device_id_type=MESH,
        )

    def backward(c, k):
        to = target(k)
        return pltpu.make_async_remote_copy(
            src_ref=product.at[c, to], dst_ref=coupled.at[c, mz], send_sem=bs.at[c, to],
            recv_sem=br.at[c, mz], device_id={"lz": to}, device_id_type=MESH,
        )

    def backward_in(c, k):
        src = lax.rem(mz + nz - k, nz)
        return pltpu.make_async_remote_copy(
            src_ref=product.at[c, src], dst_ref=coupled.at[c, src], send_sem=bs.at[c, src],
            recv_sem=br.at[c, src], device_id={"lz": src}, device_id_type=MESH,
        )

    order = range(1, nz)
    for load in loads[:3]:
        load.wait()
    for h in range(halves):
        prepare(h)
        for s in range(per):
            c = h * per + s
            if c:
                choose(h, s)
            compact(h, s)
            if c == 0:
                pl.semaphore_wait(barrier, nx * ny + nz - 2)
            for k in order:
                forward(c, k).start()
            arrived[c, mz] = packed[c, mz, :full]

    halo_out[0] = wide_ref[halves - 1, :full, (span - 1) * cells:span * cells]
    halo_out[1] = wide_ref[0, :full, :cells]
    later, before = lax.rem(mx + 1, nx), lax.rem(mx + nx - 1, nx)
    to_later = pltpu.make_async_remote_copy(
        src_ref=halo_out.at[0], dst_ref=halo.at[0], send_sem=xs.at[0], recv_sem=xr.at[0],
        device_id={"tx": later}, device_id_type=MESH,
    )
    to_before = pltpu.make_async_remote_copy(
        src_ref=halo_out.at[1], dst_ref=halo.at[1], send_sem=xs.at[1], recv_sem=xr.at[1],
        device_id={"tx": before}, device_id_type=MESH,
    )
    to_later.start()
    to_before.start()
    for f in range(2):
        def edges(j, carry):
            first, last = carry
            value = field[middle(f * slab + j, 0, rows), :]
            first = jnp.where(lane == j, pltpu.roll(value, j, 1), first)
            last = jnp.where(lane == j, pltpu.roll(value, j + 1, 1), last)
            return first, last

        blank = jnp.zeros((rows, cells), F32)
        first, last = lax.fori_loop(0, slab, edges, (blank, blank), unroll=4)
        edge_out[0, f] = first.astype(BF16)
        edge_out[1, f] = last.astype(BF16)

    up, down = lax.rem(my + 1, ny), lax.rem(my + ny - 1, ny)
    to_up = pltpu.make_async_remote_copy(
        src_ref=edge_out.at[1], dst_ref=edge_in.at[0], send_sem=ys.at[0], recv_sem=yr.at[0],
        device_id={"ty": up}, device_id_type=MESH,
    )
    to_down = pltpu.make_async_remote_copy(
        src_ref=edge_out.at[0], dst_ref=edge_in.at[1], send_sem=ys.at[1], recv_sem=yr.at[1],
        device_id={"ty": down}, device_id_type=MESH,
    )
    to_up.start()
    to_down.start()
    col = units * layers * nz
    wide = nz * full

    def chooser(shape, dim, f):
        i = lax.broadcasted_iota(jnp.int32, shape, dim)
        j = lax.broadcasted_iota(jnp.int32, shape, 1 - dim)
        part, rest = i // full, lax.rem(i, full)
        field, entry = rest // slab, lax.rem(rest, slab)
        unit, layer = entry // layers, lax.rem(entry, layers)
        target = unit * (layers * nz) + part * layers + layer
        return jnp.where((target == j) & (field == f), 1.0, 0.0).astype(BF16)

    loads[3].wait()
    dense = k_ref[...]
    total = None
    for f in range(2):
        left = jnp.dot(
            chooser((wide, col), 0, f), dense, preferred_element_type=F32
        ).astype(BF16)
        both = jnp.dot(left, chooser((col, wide), 1, f), preferred_element_type=F32)
        total = both if total is None else total + both
    big_k[...] = total.astype(BF16)

    for load in loads[4:]:
        load.wait()
    zero = jnp.zeros((rows, cells), F32)
    sums = (zero, zero, zero)

    def norms(j, carry):
        bb, cc, cv = carry
        b = b_ref[j].astype(F32)
        c = c_ref[j].astype(F32)
        return bb + b * b, cc + c * c, cv + c * test_ref[j].astype(F32)

    to_later.wait_recv()
    to_before.wait_recv()
    to_up.wait_recv()
    to_down.wait_recv()
    field[pl.ds(MARGIN - 1, full, stride=pitch), :] = halo[0].astype(F32)
    field[pl.ds(MARGIN + rows, full, stride=pitch), :] = halo[1].astype(F32)

    @pl.when(my > 0)
    def _():
        edge_f[0] = edge_in[0].astype(F32)

    @pl.when(my == 0)
    def _():
        edge_f[0] = jnp.zeros((2, rows, cells), F32)

    @pl.when(my < ny - 1)
    def _():
        edge_f[1] = edge_in[1].astype(F32)

    @pl.when(my == ny - 1)
    def _():
        edge_f[1] = jnp.zeros((2, rows, cells), F32)


    totals = [zero, zero]

    def local_part(f, u):
        def local(z, total):
            j = u * layers + z
            q = f * slab + j
            here = field[middle(q, 0, rows), :]
            south = jnp.where(
                lane == 0, pltpu.roll(edge_f[0, f], lax.rem(cells - j, cells), 1),
                pltpu.roll(here, 1, 1),
            )
            north = jnp.where(
                lane == cells - 1, pltpu.roll(edge_f[1, f], cells - 1 - j, 1),
                pltpu.roll(here, cells - 1, 1),
            )
            near = field[pl.ds(q * pitch + MARGIN - 1, rows), :]
            near = near + field[pl.ds(q * pitch + MARGIN + 1, rows), :]
            value = kappa_ref[u] * (near + south + north - 4.0 * here)
            for w in range(units):
                value = value + blocks_ref[units * u + w].astype(F32) * field[
                    middle(f * slab + w * layers + z, 0, rows), :
                ]
            before_image[q] = value
            return total + b_ref[j].astype(F32) * value

        totals[f] = lax.fori_loop(0, layers, local, totals[f], unroll=2)

    jobs = [(f, u) for f in range(2) for u in range(units)]
    each = -(-len(jobs) // chunks)

    tile = jnp.zeros((8, cells), F32)

    def dots(pair, values, weights):
        ba, be = pair
        for d in range(nz):
            y = values[d].astype(F32)
            b = weights[d, full:].astype(F32)
            ba = ba + jnp.sum((y[:slab] * b).reshape(slab // 8, 8, cells), axis=0)
            be = be + jnp.sum((y[slab:] * b).reshape(slab // 8, 8, cells), axis=0)
        return ba, be

    pair = (tile, tile)
    share = slab // chunks
    for c in range(chunks):
        for k in order:
            forward_in(c, k).wait_recv()
        part = arrived[c].reshape(wide, cells)
        result = jnp.dot(big_k[...], part, preferred_element_type=F32).astype(BF16)
        for d in range(nz):
            product[c, d] = result[d * full:(d + 1) * full]
        for k in order:
            backward(c, k).start()
        coupled[c, mz] = product[c, mz]
        sums = lax.fori_loop(c * share, (c + 1) * share, norms, sums, unroll=2)
        for job in jobs[c * each:(c + 1) * each]:
            local_part(*job)
    if share * chunks < slab:
        sums = lax.fori_loop(share * chunks, slab, norms, sums)

    def image(start, stop):
        part = weight[start:stop, :]

        def one(j, carry):
            for f in range(2):
                q = f * slab + j
                coup = back[pl.ds(pl.multiple_of(q * rows + start, 8), stop - start), :]
                value = part * (coup + before_image[q, start:stop, :])
                outs[f][j, start:stop, :] = value.astype(BF16)
            return carry

        lax.fori_loop(0, slab, one, 0, unroll=6)

    def begin(s, value):
        stat_out[s] = value
        _, peers, me = reduce_stages[s]
        boxes[s][me] = value
        for peer in peers:
            pltpu.make_async_remote_copy(
                src_ref=stat_out.at[s], dst_ref=boxes[s].at[me], send_sem=ss.at[s],
                recv_sem=stat_sems.at[s], device_id=peer, device_id_type=MESH,
            ).start()

    def every(s, sem):
        rows_in = boxes[s].at[pl.ds(0, len(reduce_stages[s][1]))]
        return pltpu.make_async_copy(rows_in, rows_in, sem.at[s])

    def finish(s):
        every(s, stat_sems).wait()
        return jnp.sum(boxes[s][...], axis=0)

    reduce_stages = []
    for dims in stage_sizes(sizes):
        me = 0
        for name, at, n in dims:
            me = me * n + lax.axis_index(name)
        peers = []
        for shift in itertools.product(*[range(n) for _, _, n in dims]):
            if any(shift):
                peer = {
                    name: lax.rem(lax.axis_index(name) + k, n)
                    for (name, _, n), k in zip(dims, shift)
                }
                peers.append(peer)
        reduce_stages.append((dims, peers, me))

    seat = lax.broadcasted_iota(jnp.int32, (8, cells), 0)
    spot = lax.broadcasted_iota(jnp.int32, (8, cells), 1)
    for h in range(halves):
        drawn = 0
        for s in range(per):
            c = h * per + s
            for k in order:
                backward_in(c, k).wait_recv()
            pair = dots(pair, coupled.at[c], packed.at[c])
            if c == chunks - 1:
                ba, be = (
                    jnp.sum(v, axis=0, keepdims=True) + jnp.sum(w, axis=0, keepdims=True)
                    for v, w in zip(pair, [ocean * v for v in totals])
                )
                lines = [jnp.sum(v, axis=0, keepdims=True) for v in sums]
                lines += [ba, be, jnp.sum(excess, axis=0, keepdims=True)]
                lines += [jnp.zeros((2, cells), F32)]
                value = jnp.sum(jnp.concatenate(lines, axis=0), axis=1, keepdims=True)
                value = jnp.where(seat == spot, jnp.broadcast_to(value, (8, cells)), 0.0)
                begin(0, jnp.sum(value, axis=0, keepdims=True))
            block = jnp.concatenate([coupled[c, d] for d in range(nz)], axis=1)
            spread = jnp.dot(
                block, pick[c, :, s * quad:span * cells], preferred_element_type=F32
            )
            if s:
                spread = spread + partial[:, s * quad:span * cells]
            done = nz if s + 1 < per else span - nz * s
            for i in range(done):
                x = h * span + nz * s + i
                back[pl.ds(x, full, stride=rows), :] = spread[:, i * cells:(i + 1) * cells]
            if s + 1 < per:
                partial[:, (s + 1) * quad:span * cells] = spread[:, quad:]
            ready = (nz * s + done) // 8 * 8
            if s == per - 1 or (h == halves - 1 and s == per - 2 and ready > drawn):
                image(h * span + drawn, h * span + ready)
                drawn = ready

    value = finish(0)
    for s in range(1, stages):
        begin(s, value)
        value = finish(s)
    value = jnp.broadcast_to(value, (8, cells))
    top = jnp.where(spot < 2, pltpu.roll(value, cells - 3, 1), value)
    low = jnp.where(spot == 0, value, pltpu.roll(value, 1, 1))
    border_ref[...] = (top / jnp.sqrt(low))[:1]
    flag_ref[0] = jnp.where(jnp.sum(jnp.where(spot == 5, value, 0.0)) > 0.0, 1, 0)

    for c in range(chunks):
        for k in order:
            forward(c, k).wait_send()
            backward(c, k).wait_send()
    to_later.wait_send()
    to_before.wait_send()
    to_up.wait_send()
    to_down.wait_send()
    for s in range(stages):
        every(s, ss).wait()


def dense_call(sizes, units, layers, args):
    nx, ny, nz = sizes
    slab, rows, cells = args[0].shape
    full = 2 * slab
    group = rows // nz
    chunks = 4 if group % 4 == 0 else 1
    step = group // chunks
    vmem = pl.BlockSpec(memory_space=pltpu.VMEM)
    smem = pl.BlockSpec(memory_space=pltpu.SMEM)
    hbm = pl.BlockSpec(memory_space=pl.ANY)
    dma = pltpu.SemaphoreType.DMA
    return pl.pallas_call(
        functools.partial(dense_kernel, sizes, chunks, units),
        out_shape=(
            jax.ShapeDtypeStruct((slab, rows, cells), BF16),
            jax.ShapeDtypeStruct((slab, rows, cells), BF16),
            jax.ShapeDtypeStruct((1, cells), F32),
        ),
        in_specs=[hbm] * 4 + [vmem] * 2 + [hbm] * 2 + [smem],
        out_specs=(vmem, vmem, vmem),
        scratch_shapes=[
            *[pltpu.VMEM((slab, rows, cells), BF16)] * 4,
            pltpu.VMEM(args[6].shape, BF16),
            pltpu.VMEM(args[7].shape, BF16),
            pltpu.VMEM((rows, full, cells), BF16),
            pltpu.VMEM((chunks, nz, step, full, cells), BF16),
            pltpu.VMEM((chunks, nz, step, full, cells), BF16),
            pltpu.VMEM((rows, full, cells), BF16),
            pltpu.VMEM((rows, cells), F32),
            pltpu.VMEM((nz * full, nz * full), BF16),
            pltpu.VMEM((full * (rows + 2 * MARGIN), cells), F32),
            pltpu.VMEM((full * rows, cells), F32),
            pltpu.VMEM((full, rows, cells), F32),
            pltpu.VMEM((2, full, cells), BF16),
            pltpu.VMEM((2, 2, rows, cells), BF16),
            pltpu.VMEM((2, 2, rows, cells), BF16),
            pltpu.VMEM((2, 2, rows, cells), F32),
            pltpu.VMEM((2, 8, cells), F32),
            pltpu.VMEM((nz, 8, cells), F32),
            pltpu.VMEM((ny * nx, 8, cells), F32),
            dma((6,)),
            *[dma((chunks, nz))] * 4,
            *[dma((2,))] * 4,
            dma((nx * ny + nz - 2,)),
            dma((nz,)),
            dma((ny * nx,)),
        ],
        compiler_params=pltpu.CompilerParams(
            collective_id=0, has_side_effects=True, vmem_limit_bytes=52 * 1024 * 1024
        ),
    )(*args)


def fast_call(sizes, span, units, layers, args):
    nx, ny, nz = sizes
    slab, rows, cells = args[0].shape
    full = 2 * slab
    chunks = (rows * 3 // 4) // nz
    quad = nz * cells
    groups = [math.prod(n for _, _, n in dims) for dims in stage_sizes(sizes)]
    vmem = pl.BlockSpec(memory_space=pltpu.VMEM)
    smem = pl.BlockSpec(memory_space=pltpu.SMEM)
    hbm = pl.BlockSpec(memory_space=pl.ANY)
    dma = pltpu.SemaphoreType.DMA
    return pl.pallas_call(
        functools.partial(fast_kernel, sizes, span, units),
        out_shape=(
            jax.ShapeDtypeStruct((slab, rows, cells), BF16),
            jax.ShapeDtypeStruct((slab, rows, cells), BF16),
            jax.ShapeDtypeStruct((1, cells), F32),
            jax.ShapeDtypeStruct((1,), jnp.int32),
        ),
        in_specs=[hbm] * 4 + [vmem] * 2 + [hbm] * 3,
        out_specs=(vmem, vmem, vmem, smem),
        scratch_shapes=[
            *[pltpu.VMEM((slab, rows, cells), BF16)] * 4,
            pltpu.VMEM(args[6].shape, BF16),
            pltpu.VMEM(args[7].shape, BF16),
            pltpu.SMEM(args[8].shape, F32),
            pltpu.VMEM((rows // span, full + slab, span * cells), BF16),
            pltpu.VMEM((chunks, quad, span * cells), BF16),
            pltpu.VMEM((chunks, nz, full + slab, cells), BF16),
            *[pltpu.VMEM((chunks, nz, full, cells), BF16)] * 3,
            pltpu.VMEM((full, span * cells), F32),
            pltpu.VMEM((rows, cells), F32),
            pltpu.VMEM((rows, cells), F32),
            pltpu.VMEM((nz * full, nz * full), BF16),
            pltpu.VMEM((full * (rows + 2 * MARGIN), cells), F32),
            pltpu.VMEM((slab * rows, cells), F32),
            pltpu.VMEM((full * rows, cells), F32),
            pltpu.VMEM((full, rows, cells), F32),
            pltpu.VMEM((2, full, cells), BF16),
            pltpu.VMEM((2, full, cells), BF16),
            pltpu.VMEM((2, 2, rows, cells), BF16),
            pltpu.VMEM((2, 2, rows, cells), BF16),
            pltpu.VMEM((2, 2, rows, cells), F32),
            pltpu.VMEM((len(groups), 1, cells), F32),
            *[pltpu.VMEM((n, 1, cells), F32) for n in groups],
            dma((7,)),
            *[dma((chunks, nz))] * 4,
            *[dma((2,))] * 4,
            *[dma((len(groups),))] * 2,
        ],
        compiler_params=pltpu.CompilerParams(
            collective_id=1, has_side_effects=True, vmem_limit_bytes=52 * 1024 * 1024
        ),
    )(*args)


def body(sizes, *arrays):
    nx, ny, nz = sizes
    rows, units, layers, cells = arrays[0].shape
    slab = units * layers
    wide = [v.transpose(1, 2, 0, 3).reshape(slab, rows, cells) for v in arrays[:4]]
    args = (*wide, arrays[4], arrays[5].T, arrays[6].transpose(1, 0, 2), *arrays[7:])
    held = [pltpu.with_memory_space_constraint(v, pltpu.HBM) for v in args]
    span = rows // 2
    if rows % 16 == 0 and (span * 3 // 4) % nz == 0:
        *quick, flag = fast_call(sizes, span, units, layers, held)
        out_t, out_d, border = lax.cond(
            flag[0] > 0, lambda: dense_call(sizes, units, layers, held), lambda: tuple(quick)
        )
    else:
        out_t, out_d, border = dense_call(sizes, units, layers, held)
    out_t, out_d, border = put_call(out_t, out_d, border)
    outs = [
        v.reshape(units, layers, rows, cells).transpose(2, 0, 1, 3) for v in (out_t, out_d)
    ]
    return (*outs, border)


def solution(mesh):
    wide = P("tx", None, "lz", "ty")
    in_specs = (
        wide, wide, wide, wide, P("tx", "ty"), P("tx", "ty"), P("tx", None, "ty"), P(), P(),
    )
    sizes = tuple(mesh.shape[name] for name in ("tx", "ty", "lz"))
    return jax.shard_map(
        functools.partial(body, sizes), mesh=mesh, in_specs=in_specs,
        out_specs=(wide, wide, P()), check_vma=False,
    )
```

```python
import functools
import itertools
import math
import jax
import jax.numpy as jnp
from jax import lax
from jax.experimental import pallas as pl
from jax.experimental.pallas import tpu as pltpu
from jax.sharding import PartitionSpec as P

MESH = pl.DeviceIdType.MESH
F32 = jnp.float32
BF16 = jnp.bfloat16


MARGIN = 8


def dense_kernel(
    sizes, chunks, units,
    test_hbm, dir_hbm, b_hbm, c_hbm, land_ref, active_ref, blocks_hbm, k_hbm, kappa_ref,
    out_t, out_d, border_ref,
    test_ref, dir_ref, b_ref, c_ref, blocks_ref, k_ref,
    masked, arrived, product, coupled, weight, big_k, field, back, before_image, halo,
    edge_out, edge_in, edge_f, stat_out, stat_z, stat_y,
    ls, fs, fr, bs, br, xs, xr, ys, yr, ss, sr_z, sr_y,
):
    nx, ny, nz = sizes
    slab, rows, cells = test_ref.shape
    layers = slab // units
    full = 2 * slab
    group = rows // nz
    step = group // chunks
    pitch = rows + 2 * MARGIN
    mx, my, mz = lax.axis_index("tx"), lax.axis_index("ty"), lax.axis_index("lz")
    fields = (test_ref, dir_ref)
    outs = (out_t, out_d)

    loads = [
        pltpu.make_async_copy(source, target, ls.at[i])
        for i, (source, target) in enumerate((
            (test_hbm, test_ref), (dir_hbm, dir_ref), (k_hbm, k_ref), (b_hbm, b_ref),
            (c_hbm, c_ref), (blocks_hbm, blocks_ref),
        ))
    ]
    for load in loads:
        load.start()

    barrier = pltpu.get_barrier_semaphore()
    for k in range(1, nz):
        pl.semaphore_signal(
            barrier, inc=1, device_id={"lz": lax.rem(mz + k, nz)}, device_id_type=MESH
        )
    for k in range(1, nx * ny):
        near = {"ty": lax.rem(my + k // nx, ny), "tx": lax.rem(mx + k % nx, nx)}
        pl.semaphore_signal(barrier, inc=1, device_id=near, device_id_type=MESH)

    lane = lax.broadcasted_iota(jnp.int32, (rows, cells), 1)
    line = lax.broadcasted_iota(jnp.int32, (rows, rows), 0)
    named = jnp.max(
        jnp.where(jnp.broadcast_to(active_ref[...], (rows, rows)) == line, 1.0, 0.0),
        axis=1, keepdims=True,
    )
    weight[...] = land_ref[...].astype(F32) * named
    ocean = weight[...]

    def middle(q):
        return pl.ds(pl.multiple_of(q * pitch + MARGIN, 8), rows)

    for f in range(2):
        loads[f].wait()

        def mask(j, carry):
            field[middle(f * slab + j), :] = fields[f][j].astype(F32) * ocean
            return carry

        lax.fori_loop(0, slab, mask, 0, unroll=8)

    def pack(c):
        def pack_row(i, carry):
            x = lax.div(i, step) * group + c * step + lax.rem(i, step)
            masked[x] = field[pl.ds(MARGIN + x, full, stride=pitch), :].astype(BF16)
            return carry

        lax.fori_loop(0, nz * step, pack_row, 0, unroll=4)

    pack(0)

    pl.semaphore_wait(barrier, nx * ny + nz - 2)

    def forward(c, k):
        to = lax.rem(mz + k, nz)
        return pltpu.make_async_remote_copy(
            src_ref=masked.at[pl.ds(to * group + c * step, step)],
            dst_ref=arrived.at[c, mz],
            send_sem=fs.at[c, to],
            recv_sem=fr.at[c, mz],
            device_id={"lz": to},
            device_id_type=MESH,
        )

    def forward_in(c, k):
        src = lax.rem(mz + nz - k, nz)
        return pltpu.make_async_remote_copy(
            src_ref=arrived.at[c, src],
            dst_ref=arrived.at[c, src],
            send_sem=fs.at[c, src],
            recv_sem=fr.at[c, src],
            device_id={"lz": src},
            device_id_type=MESH,
        )

    def backward(c, k):
        to = lax.rem(mz + k, nz)
        return pltpu.make_async_remote_copy(
            src_ref=product.at[c, to],
            dst_ref=coupled.at[pl.ds(mz * group + c * step, step)],
            send_sem=bs.at[c, to],
            recv_sem=br.at[c, mz],
            device_id={"lz": to},
            device_id_type=MESH,
        )

    def backward_in(c, k):
        src = lax.rem(mz + nz - k, nz)
        return pltpu.make_async_remote_copy(
            src_ref=product.at[c, src],
            dst_ref=coupled.at[pl.ds(src * group + c * step, step)],
            send_sem=bs.at[c, src],
            recv_sem=br.at[c, src],
            device_id={"lz": src},
            device_id_type=MESH,
        )

    order = sorted(range(1, nz), key=lambda k: -min(k, nz - k))
    for c in range(1, chunks):
        pack(c)
        for k in order:
            forward(c - 1, k).start()

    def own_row(i, carry):
        arrived[lax.div(i, step), mz, lax.rem(i, step)] = masked[mz * group + i]
        return carry

    lax.fori_loop(0, group, own_row, 0)
    for k in order:
        forward(chunks - 1, k).start()
    later, before = lax.rem(mx + 1, nx), lax.rem(mx + nx - 1, nx)
    to_later = pltpu.make_async_remote_copy(
        src_ref=masked.at[rows - 1], dst_ref=halo.at[0], send_sem=xs.at[0], recv_sem=xr.at[0],
        device_id={"tx": later}, device_id_type=MESH,
    )
    to_before = pltpu.make_async_remote_copy(
        src_ref=masked.at[0], dst_ref=halo.at[1], send_sem=xs.at[1], recv_sem=xr.at[1],
        device_id={"tx": before}, device_id_type=MESH,
    )
    to_later.start()
    to_before.start()
    for f in range(2):
        def edges(j, carry):
            first, last = carry
            value = field[middle(f * slab + j), :]
            first = jnp.where(lane == j, pltpu.roll(value, j, 1), first)
            last = jnp.where(lane == j, pltpu.roll(value, j + 1, 1), last)
            return first, last

        blank = jnp.zeros((rows, cells), F32)
        first, last = lax.fori_loop(0, slab, edges, (blank, blank), unroll=4)
        edge_out[0, f] = first.astype(BF16)
        edge_out[1, f] = last.astype(BF16)

    up, down = lax.rem(my + 1, ny), lax.rem(my + ny - 1, ny)
    to_up = pltpu.make_async_remote_copy(
        src_ref=edge_out.at[1], dst_ref=edge_in.at[0], send_sem=ys.at[0], recv_sem=yr.at[0],
        device_id={"ty": up}, device_id_type=MESH,
    )
    to_down = pltpu.make_async_remote_copy(
        src_ref=edge_out.at[0], dst_ref=edge_in.at[1], send_sem=ys.at[1], recv_sem=yr.at[1],
        device_id={"ty": down}, device_id_type=MESH,
    )
    col = units * layers * nz
    wide = nz * full

    def chooser(shape, dim, f):
        i = lax.broadcasted_iota(jnp.int32, shape, dim)
        j = lax.broadcasted_iota(jnp.int32, shape, 1 - dim)
        part, rest = i // full, lax.rem(i, full)
        field, entry = rest // slab, lax.rem(rest, slab)
        unit, layer = entry // layers, lax.rem(entry, layers)
        target = unit * (layers * nz) + part * layers + layer
        return jnp.where((target == j) & (field == f), 1.0, 0.0).astype(BF16)

    loads[2].wait()
    dense = k_ref[...]
    total = None
    for f in range(2):
        left = jnp.dot(
            chooser((wide, col), 0, f), dense, preferred_element_type=F32
        ).astype(BF16)
        both = jnp.dot(left, chooser((col, wide), 1, f), preferred_element_type=F32)
        total = both if total is None else total + both
    big_k[...] = total.astype(BF16)
    to_up.start()
    to_down.start()

    for load in loads[3:]:
        load.wait()
    zero = jnp.zeros((rows, cells), F32)
    sums = (zero, zero, zero)

    def norms(j, carry):
        bb, cc, cv = carry
        b = b_ref[j].astype(F32)
        c = c_ref[j].astype(F32)
        return bb + b * b, cc + c * c, cv + c * test_ref[j].astype(F32)

    quarter = slab // chunks
    for c in range(chunks):
        for k in order:
            forward_in(c, k).wait_recv()
        part = jnp.concatenate(
            [arrived[c, :, r].reshape(wide, cells) for r in range(step)], axis=1
        )
        result = jnp.dot(big_k[...], part, preferred_element_type=F32).astype(BF16)
        for d in range(nz):
            for r in range(step):
                product[c, d, r] = result[d * full:(d + 1) * full, r * cells:(r + 1) * cells]
        sums = lax.fori_loop(c * quarter, (c + 1) * quarter, norms, sums, unroll=2)
        for k in order:
            backward(c, k).start()
        for r in range(step):
            coupled[mz * group + c * step + r] = product[c, mz, r]

    to_later.wait_recv()
    to_before.wait_recv()
    to_up.wait_recv()
    to_down.wait_recv()
    field[pl.ds(MARGIN - 1, full, stride=pitch), :] = halo[0].astype(F32)
    field[pl.ds(MARGIN + rows, full, stride=pitch), :] = halo[1].astype(F32)

    @pl.when(my > 0)
    def _():
        edge_f[0] = edge_in[0].astype(F32)

    @pl.when(my == 0)
    def _():
        edge_f[0] = jnp.zeros((2, rows, cells), F32)

    @pl.when(my < ny - 1)
    def _():
        edge_f[1] = edge_in[1].astype(F32)

    @pl.when(my == ny - 1)
    def _():
        edge_f[1] = jnp.zeros((2, rows, cells), F32)

    for f in range(2):
        for u in range(units):
            def local(z, carry):
                j = u * layers + z
                q = f * slab + j
                here = field[middle(q), :]
                south = jnp.where(
                    lane == 0, pltpu.roll(edge_f[0, f], lax.rem(cells - j, cells), 1),
                    pltpu.roll(here, 1, 1),
                )
                north = jnp.where(
                    lane == cells - 1, pltpu.roll(edge_f[1, f], cells - 1 - j, 1),
                    pltpu.roll(here, cells - 1, 1),
                )
                near = field[pl.ds(q * pitch + MARGIN - 1, rows), :]
                near = near + field[pl.ds(q * pitch + MARGIN + 1, rows), :]
                value = kappa_ref[u] * (near + south + north - 4.0 * here)
                for w in range(units):
                    value = value + blocks_ref[units * u + w].astype(F32) * field[
                        middle(f * slab + w * layers + z), :
                    ]
                before_image[q] = value
                return carry

            lax.fori_loop(0, layers, local, 0, unroll=2)

    def insert(x, carry):
        back[pl.ds(x, full, stride=rows), :] = coupled[x].astype(F32)
        return carry

    for c in range(chunks):
        for k in order:
            backward_in(c, k).wait_recv()

        def chunk_row(i, carry):
            return insert(lax.div(i, step) * group + c * step + lax.rem(i, step), carry)

        lax.fori_loop(0, nz * step, chunk_row, 0, unroll=4)

    def image(j, carry):
        ba, be = carry
        b = b_ref[j].astype(F32)
        images = []
        for f in range(2):
            q = f * slab + j
            coup = back[pl.ds(pl.multiple_of(q * rows, 8), rows), :]
            images.append(ocean * (coup + before_image[q]))
            outs[f][j] = images[f].astype(BF16)
        return ba + b * images[0], be + b * images[1]

    pair = lax.fori_loop(0, slab, image, (zero, zero), unroll=6)

    lines = [jnp.sum(v, axis=0, keepdims=True) for v in (*sums, *pair)]
    value = jnp.concatenate(lines + [jnp.zeros((3, cells), F32)], axis=0)
    base = 0
    plane = [(i, k) for i in range(ny) for k in range(nx)]
    stages = (
        ([{"lz": lax.rem(mz + k, nz)} for k in range(nz)], nz, stat_z, sr_z, mz,
         [lax.rem(mz + nz - k, nz) for k in range(nz)]),
        ([{"ty": lax.rem(my + i, ny), "tx": lax.rem(mx + k, nx)} for i, k in plane],
         ny * nx, stat_y, sr_y, my * nx + mx,
         [lax.rem(my + ny - i, ny) * nx + lax.rem(mx + nx - k, nx) for i, k in plane]),
    )
    sends = []
    for s, (peers, size, box, sem, me, sources) in enumerate(stages):
        stat_out[s] = value
        box[me] = value
        for k in range(1, size):
            copy = pltpu.make_async_remote_copy(
                src_ref=stat_out.at[s], dst_ref=box.at[me], send_sem=ss.at[base + k - 1],
                recv_sem=sem.at[me], device_id=peers[k], device_id_type=MESH,
            )
            copy.start()
            sends.append(copy)
        base += size - 1
        for k in range(1, size):
            src = sources[k]
            pltpu.make_async_remote_copy(
                src_ref=stat_out.at[s], dst_ref=box.at[src], send_sem=ss.at[0],
                recv_sem=sem.at[src], device_id=peers[k], device_id_type=MESH,
            ).wait_recv()
        value = box[0]
        for i in range(1, size):
            value = value + box[i]
    final = jnp.broadcast_to(jnp.sum(value, axis=1, keepdims=True), (8, cells))
    bb, cc, cv, ba, be = (final[i:i + 1] for i in range(5))
    line = lax.broadcasted_iota(jnp.int32, (1, cells), 1)
    top = jnp.where(line == 0, ba, jnp.where(line == 1, be, cv))
    low = jnp.where(line == 2, cc, bb)
    border_ref[...] = top / jnp.sqrt(low)

    for c in range(chunks):
        for k in order:
            forward(c, k).wait_send()
            backward(c, k).wait_send()
    to_later.wait_send()
    to_before.wait_send()
    to_up.wait_send()
    to_down.wait_send()
    for copy in sends:
        copy.wait_send()


def stage_sizes(sizes):
    names = ("lz", "ty", "tx")
    dims = [(name, i, sizes[("tx", "ty", "lz").index(name)]) for i, name in enumerate(names)]
    if sizes[0] * sizes[1] * sizes[2] <= 64:
        return [dims]
    return [dims[:1], dims[1:]]


def put_kernel(t_ref, d_ref, border_ref, out_t, out_d, out_border, line, sems):
    line[...] = border_ref[0, :line.shape[0]]
    copies = [
        pltpu.make_async_copy(source, target, sems.at[i])
        for i, (source, target) in enumerate(((t_ref, out_t), (d_ref, out_d), (line, out_border)))
    ]
    for copy in copies:
        copy.start()
    for copy in copies:
        copy.wait()


def put_call(out_t, out_d, border):
    hbm = pl.BlockSpec(memory_space=pl.ANY)
    return pl.pallas_call(
        put_kernel,
        out_shape=(
            jax.ShapeDtypeStruct(out_t.shape, BF16),
            jax.ShapeDtypeStruct(out_d.shape, BF16),
            jax.ShapeDtypeStruct((3,), F32),
        ),
        in_specs=[hbm, hbm, pl.BlockSpec(memory_space=pltpu.VMEM)],
        out_specs=(hbm, hbm, hbm),
        scratch_shapes=[pltpu.VMEM((3,), F32), pltpu.SemaphoreType.DMA((3,))],
    )(out_t, out_d, border)


def fast_kernel(
    sizes, span, units,
    test_hbm, dir_hbm, b_hbm, c_hbm, land_ref, active_ref, blocks_hbm, k_hbm, kappa_hbm,
    out_t, out_d, border_ref, flag_ref,
    test_ref, dir_ref, b_ref, c_ref, blocks_ref, k_ref,
    kappa_ref, wide_ref, wide_b, pick, packed, packed_b, arrived, product, coupled, partial, weight, place, big_k,
    field, b_field, back, before_image, halo_out, halo, edge_out, edge_in, edge_f, stat_out,
    *rest,
):
    nx, ny, nz = sizes
    stages = len(stage_sizes(sizes))
    boxes, rest = rest[:stages], rest[stages:]
    ls, fs, fr, bs, br, xs, xr, ys, yr, ss = rest[:10]
    stat_sems = rest[10]
    slab, rows, cells = test_ref.shape
    layers = slab // units
    full = 2 * slab
    halves = rows // span
    slots = packed.shape[0] * nz // halves
    per = slots // nz
    chunks = halves * per
    pitch = rows + 2 * MARGIN
    quad = nz * cells
    mx, my, mz = lax.axis_index("tx"), lax.axis_index("ty"), lax.axis_index("lz")
    fields = (test_ref, dir_ref)
    outs = (out_t, out_d)

    loads = [
        pltpu.make_async_copy(source, target, ls.at[i])
        for i, (source, target) in enumerate((
            (test_hbm, test_ref), (dir_hbm, dir_ref), (b_hbm, b_ref), (k_hbm, k_ref),
            (c_hbm, c_ref), (blocks_hbm, blocks_ref), (kappa_hbm, kappa_ref),
        ))
    ]
    for load in loads:
        load.start()

    barrier = pltpu.get_barrier_semaphore()
    for k in range(1, nz):
        pl.semaphore_signal(
            barrier, inc=1, device_id={"lz": lax.rem(mz + k, nz)}, device_id_type=MESH
        )
    for k in range(1, nx * ny):
        near = {"ty": lax.rem(my + k // nx, ny), "tx": lax.rem(mx + k % nx, nx)}
        pl.semaphore_signal(barrier, inc=1, device_id=near, device_id_type=MESH)

    lane = lax.broadcasted_iota(jnp.int32, (rows, cells), 1)
    line = lax.broadcasted_iota(jnp.int32, (rows, rows), 0)
    named = jnp.max(
        jnp.where(jnp.broadcast_to(active_ref[...], (rows, rows)) == line, 1.0, 0.0),
        axis=1, keepdims=True,
    )
    ocean = land_ref[...].astype(F32) * named
    weight[...] = ocean

    wet = ocean.astype(BF16)
    other = lax.broadcasted_iota(jnp.int32, (rows, rows), 1)
    earlier = jnp.where((other < line) & (other // span == line // span), 1.0, 0.0).astype(BF16)
    cell_i = lax.broadcasted_iota(jnp.int32, (cells, cells), 0)
    cell_j = lax.broadcasted_iota(jnp.int32, (cells, cells), 1)
    ahead = jnp.where(cell_i < cell_j, 1.0, 0.0).astype(BF16)
    above = jnp.dot(earlier, wet, preferred_element_type=F32).astype(BF16)
    count = jnp.dot(wet, ahead, preferred_element_type=F32)
    count = count + jnp.dot(above, jnp.ones((cells, cells), BF16), preferred_element_type=F32)
    place[...] = jnp.where(ocean > 0.0, count, -1.0)
    excess = jnp.where((ocean > 0.0) & (count >= float(slots * cells)), 1.0, 0.0)

    spot = lax.broadcasted_iota(jnp.int32, (quad, cells), 0).astype(F32)

    def choose(h, s):
        def one(i, carry):
            where = place[pl.ds(h * span + i, 1), :] - float(s * quad)
            hit = jnp.where(jnp.broadcast_to(where, (quad, cells)) == spot, 1.0, 0.0)
            pick[h * per + s, :, pl.ds(pl.multiple_of(i * cells, cells), cells)] = hit.astype(BF16)
            return carry

        lax.fori_loop(nz * s, span, one, 0, unroll=2)

    choose(0, 0)

    def middle(q, start, size):
        return pl.ds(pl.multiple_of(q * pitch + MARGIN + start, 8), size)

    def prepare(h):
        part = weight[h * span:(h + 1) * span, :]
        for f in range(2):
            def mask(j, carry):
                value = fields[f][j, h * span:(h + 1) * span, :].astype(F32) * part
                field[middle(f * slab + j, h * span, span), :] = value
                return carry

            lax.fori_loop(0, slab, mask, 0, unroll=8)

        def pack_row(i, carry):
            spot = pl.ds(pl.multiple_of(i * cells, cells), cells)
            row = field[pl.ds(MARGIN + h * span + i, full, stride=pitch), :].astype(BF16)
            wide_ref[h, :, spot] = row
            return carry

        lax.fori_loop(0, span, pack_row, 0, unroll=4)

    def prepare_b():
        def widen(j, carry):
            start = pl.multiple_of(j * rows, 8)
            b_field[pl.ds(start, rows), :] = b_ref[j].astype(F32)
            return carry

        lax.fori_loop(0, slab, widen, 0, unroll=4)
        for h in range(halves):
            def pack_row(i, carry):
                row = b_field[pl.ds(h * span + i, slab, stride=rows), :].astype(BF16)
                wide_b[h, :, pl.ds(pl.multiple_of(i * cells, cells), cells)] = row
                return carry

            lax.fori_loop(0, span, pack_row, 0, unroll=4)

    def compact(h, s, source, target):
        c = h * per + s
        found = lax.dot_general(
            source[h, :, s * quad:span * cells], pick[c, :, s * quad:span * cells],
            (((1,), (1,)), ((), ())), preferred_element_type=F32,
        ).astype(BF16)
        for d in range(nz):
            target[c, d] = found[:, d * cells:(d + 1) * cells]

    def target(k):
        down = nz - k
        low = down - jnp.where(down <= mz, 1, 0)
        high = k - 1 + jnp.where(k - 1 >= mz, 1, 0)
        return jnp.where(mz < nz // 2, low, high)

    def forward(c, k):
        to = target(k)
        return pltpu.make_async_remote_copy(
            src_ref=packed.at[c, to], dst_ref=arrived.at[c, mz],
            send_sem=fs.at[c, to], recv_sem=fr.at[c, mz], device_id={"lz": to},
            device_id_type=MESH,
        )

    def forward_in(c, k):
        src = lax.rem(mz + nz - k, nz)
        return pltpu.make_async_remote_copy(
            src_ref=arrived.at[c, src], dst_ref=arrived.at[c, src],
            send_sem=fs.at[c, src], recv_sem=fr.at[c, src], device_id={"lz": src},
            device_id_type=MESH,
        )

    def backward(c, k):
        to = target(k)
        return pltpu.make_async_remote_copy(
            src_ref=product.at[c, to], dst_ref=coupled.at[c, mz], send_sem=bs.at[c, to],
            recv_sem=br.at[c, mz], device_id={"lz": to}, device_id_type=MESH,
        )

    def backward_in(c, k):
        src = lax.rem(mz + nz - k, nz)
        return pltpu.make_async_remote_copy(
            src_ref=product.at[c, src], dst_ref=coupled.at[c, src], send_sem=bs.at[c, src],
            recv_sem=br.at[c, src], device_id={"lz": src}, device_id_type=MESH,
        )

    order = range(1, nz)
    loads[0].wait()
    loads[1].wait()
    for h in range(halves):
        prepare(h)
        for s in range(per):
            c = h * per + s
            if c:
                choose(h, s)
            compact(h, s, wide_ref, packed)
            if c == 0:
                pl.semaphore_wait(barrier, nx * ny + nz - 2)
            for k in order:
                forward(c, k).start()
            arrived[c, mz] = packed[c, mz]

    halo_out[0] = wide_ref[halves - 1, :, (span - 1) * cells:span * cells]
    halo_out[1] = wide_ref[0, :, :cells]
    later, before = lax.rem(mx + 1, nx), lax.rem(mx + nx - 1, nx)
    to_later = pltpu.make_async_remote_copy(
        src_ref=halo_out.at[0], dst_ref=halo.at[0], send_sem=xs.at[0], recv_sem=xr.at[0],
        device_id={"tx": later}, device_id_type=MESH,
    )
    to_before = pltpu.make_async_remote_copy(
        src_ref=halo_out.at[1], dst_ref=halo.at[1], send_sem=xs.at[1], recv_sem=xr.at[1],
        device_id={"tx": before}, device_id_type=MESH,
    )
    to_later.start()
    to_before.start()
    for f in range(2):
        def edges(j, carry):
            first, last = carry
            value = field[middle(f * slab + j, 0, rows), :]
            first = jnp.where(lane == j, pltpu.roll(value, j, 1), first)
            last = jnp.where(lane == j, pltpu.roll(value, j + 1, 1), last)
            return first, last

        blank = jnp.zeros((rows, cells), F32)
        first, last = lax.fori_loop(0, slab, edges, (blank, blank), unroll=4)
        edge_out[0, f] = first.astype(BF16)
        edge_out[1, f] = last.astype(BF16)

    up, down = lax.rem(my + 1, ny), lax.rem(my + ny - 1, ny)
    to_up = pltpu.make_async_remote_copy(
        src_ref=edge_out.at[1], dst_ref=edge_in.at[0], send_sem=ys.at[0], recv_sem=yr.at[0],
        device_id={"ty": up}, device_id_type=MESH,
    )
    to_down = pltpu.make_async_remote_copy(
        src_ref=edge_out.at[0], dst_ref=edge_in.at[1], send_sem=ys.at[1], recv_sem=yr.at[1],
        device_id={"ty": down}, device_id_type=MESH,
    )
    to_up.start()
    to_down.start()
    col = units * layers * nz
    wide = nz * full

    def chooser(shape, dim, f):
        i = lax.broadcasted_iota(jnp.int32, shape, dim)
        j = lax.broadcasted_iota(jnp.int32, shape, 1 - dim)
        part, rest = i // full, lax.rem(i, full)
        field, entry = rest // slab, lax.rem(rest, slab)
        unit, layer = entry // layers, lax.rem(entry, layers)
        target = unit * (layers * nz) + part * layers + layer
        return jnp.where((target == j) & (field == f), 1.0, 0.0).astype(BF16)

    loads[3].wait()
    dense = k_ref[...]
    total = None
    for f in range(2):
        left = jnp.dot(
            chooser((wide, col), 0, f), dense, preferred_element_type=F32
        ).astype(BF16)
        both = jnp.dot(left, chooser((col, wide), 1, f), preferred_element_type=F32)
        total = both if total is None else total + both
    big_k[...] = total.astype(BF16)

    loads[2].wait()
    for load in loads[4:]:
        load.wait()
    zero = jnp.zeros((rows, cells), F32)
    sums = (zero, zero, zero)

    def norms(j, carry):
        bb, cc, cv = carry
        b = b_ref[j].astype(F32)
        c = c_ref[j].astype(F32)
        return bb + b * b, cc + c * c, cv + c * test_ref[j].astype(F32)

    to_later.wait_recv()
    to_before.wait_recv()
    to_up.wait_recv()
    to_down.wait_recv()
    field[pl.ds(MARGIN - 1, full, stride=pitch), :] = halo[0].astype(F32)
    field[pl.ds(MARGIN + rows, full, stride=pitch), :] = halo[1].astype(F32)

    @pl.when(my > 0)
    def _():
        edge_f[0] = edge_in[0].astype(F32)

    @pl.when(my == 0)
    def _():
        edge_f[0] = jnp.zeros((2, rows, cells), F32)

    @pl.when(my < ny - 1)
    def _():
        edge_f[1] = edge_in[1].astype(F32)

    @pl.when(my == ny - 1)
    def _():
        edge_f[1] = jnp.zeros((2, rows, cells), F32)


    totals = [zero, zero]

    def local_part(f, u):
        def local(z, total):
            j = u * layers + z
            q = f * slab + j
            here = field[middle(q, 0, rows), :]
            south = jnp.where(
                lane == 0, pltpu.roll(edge_f[0, f], lax.rem(cells - j, cells), 1),
                pltpu.roll(here, 1, 1),
            )
            north = jnp.where(
                lane == cells - 1, pltpu.roll(edge_f[1, f], cells - 1 - j, 1),
                pltpu.roll(here, cells - 1, 1),
            )
            near = field[pl.ds(q * pitch + MARGIN - 1, rows), :]
            near = near + field[pl.ds(q * pitch + MARGIN + 1, rows), :]
            value = kappa_ref[u] * (near + south + north - 4.0 * here)
            for w in range(units):
                value = value + blocks_ref[units * u + w].astype(F32) * field[
                    middle(f * slab + w * layers + z, 0, rows), :
                ]
            before_image[q] = value
            return total + b_ref[j].astype(F32) * value

        totals[f] = lax.fori_loop(0, layers, local, totals[f], unroll=2)

    jobs = [(f, u) for f in range(2) for u in range(units)]
    each = -(-len(jobs) // chunks)

    tile = jnp.zeros((8, cells), F32)

    def dots(pair, values, weights):
        ba, be = pair
        for d in range(nz):
            y = values[d].astype(F32)
            b = weights[d].astype(F32)
            ba = ba + jnp.sum((y[:slab] * b).reshape(slab // 8, 8, cells), axis=0)
            be = be + jnp.sum((y[slab:] * b).reshape(slab // 8, 8, cells), axis=0)
        return ba, be

    pair = (tile, tile)
    share = slab // chunks
    for c in range(chunks):
        for k in order:
            forward_in(c, k).wait_recv()
        part = arrived[c].reshape(wide, cells)
        result = jnp.dot(big_k[...], part, preferred_element_type=F32).astype(BF16)
        for d in range(nz):
            product[c, d] = result[d * full:(d + 1) * full]
        for k in order:
            backward(c, k).start()
        coupled[c, mz] = product[c, mz]
        sums = lax.fori_loop(c * share, (c + 1) * share, norms, sums, unroll=2)
        if c == 0:
            prepare_b()
        compact(c // per, c % per, wide_b, packed_b)
        for job in jobs[c * each:(c + 1) * each]:
            local_part(*job)
    if share * chunks < slab:
        sums = lax.fori_loop(share * chunks, slab, norms, sums)

    def image(start, stop):
        part = weight[start:stop, :]

        def one(j, carry):
            for f in range(2):
                q = f * slab + j
                coup = back[pl.ds(pl.multiple_of(q * rows + start, 8), stop - start), :]
                value = part * (coup + before_image[q, start:stop, :])
                outs[f][j, start:stop, :] = value.astype(BF16)
            return carry

        lax.fori_loop(0, slab, one, 0, unroll=6)

    def begin(s, value):
        stat_out[s] = value
        _, peers, me = reduce_stages[s]
        boxes[s][me] = value
        for peer in reversed(peers):
            pltpu.make_async_remote_copy(
                src_ref=stat_out.at[s], dst_ref=boxes[s].at[me], send_sem=ss.at[s],
                recv_sem=stat_sems.at[s], device_id=peer, device_id_type=MESH,
            ).start()

    def every(s, sem):
        rows_in = boxes[s].at[pl.ds(0, len(reduce_stages[s][1]))]
        return pltpu.make_async_copy(rows_in, rows_in, sem.at[s])

    def finish(s):
        every(s, stat_sems).wait()
        return jnp.sum(boxes[s][...], axis=0)

    reduce_stages = []
    for dims in stage_sizes(sizes):
        me = 0
        for name, at, n in dims:
            me = me * n + lax.axis_index(name)
        peers = []
        for shift in itertools.product(*[range(n) for _, _, n in dims]):
            if any(shift):
                peer = {
                    name: lax.rem(lax.axis_index(name) + k, n)
                    for (name, _, n), k in zip(dims, shift)
                }
                peers.append(peer)
        reduce_stages.append((dims, peers, me))

    seat = lax.broadcasted_iota(jnp.int32, (8, cells), 0)
    spot = lax.broadcasted_iota(jnp.int32, (8, cells), 1)

    def line_of(values):
        lines = [jnp.sum(v, axis=0, keepdims=True) for v in values]
        lines += [jnp.zeros((8 - len(lines), cells), F32)]
        value = jnp.sum(jnp.concatenate(lines, axis=0), axis=1, keepdims=True)
        value = jnp.where(seat == spot, jnp.broadcast_to(value, (8, cells)), 0.0)
        return jnp.sum(value, axis=0, keepdims=True)

    for h in range(halves):
        drawn = 0
        for s in range(per):
            c = h * per + s
            if c == chunks - 1:
                early = line_of((*sums, *(ocean * v for v in totals), excess))
                early = early + line_of((tile, tile, tile, *pair, tile))
                pair = (tile, tile)
            for k in order:
                backward_in(c, k).wait_recv()
            pair = dots(pair, coupled.at[c], packed_b.at[c])
            if c == chunks - 1:
                begin(0, early + line_of((tile, tile, tile, *pair, tile)))
            block = jnp.concatenate([coupled[c, d] for d in range(nz)], axis=1)
            spread = jnp.dot(
                block, pick[c, :, s * quad:span * cells], preferred_element_type=F32
            )
            if s:
                spread = spread + partial[:, s * quad:span * cells]
            done = nz if s + 1 < per else span - nz * s
            for i in range(done):
                x = h * span + nz * s + i
                back[pl.ds(x, full, stride=rows), :] = spread[:, i * cells:(i + 1) * cells]
            if s + 1 < per:
                partial[:, (s + 1) * quad:span * cells] = spread[:, quad:]
            ready = (nz * s + done) // 8 * 8
            if s == per - 1 or (h == halves - 1 and s == per - 2 and ready > drawn):
                image(h * span + drawn, h * span + ready)
                drawn = ready

    value = finish(0)
    for s in range(1, stages):
        begin(s, value)
        value = finish(s)
    value = jnp.broadcast_to(value, (8, cells))
    top = jnp.where(spot < 2, pltpu.roll(value, cells - 3, 1), value)
    low = jnp.where(spot == 0, value, pltpu.roll(value, 1, 1))
    border_ref[...] = (top / jnp.sqrt(low))[:1]
    flag_ref[0] = jnp.where(jnp.sum(jnp.where(spot == 5, value, 0.0)) > 0.0, 1, 0)

    for c in range(chunks):
        for k in order:
            forward(c, k).wait_send()
            backward(c, k).wait_send()
    to_later.wait_send()
    to_before.wait_send()
    to_up.wait_send()
    to_down.wait_send()
    for s in range(stages):
        every(s, ss).wait()


def dense_call(sizes, units, layers, args):
    nx, ny, nz = sizes
    slab, rows, cells = args[0].shape
    full = 2 * slab
    group = rows // nz
    chunks = 4 if group % 4 == 0 else 1
    step = group // chunks
    vmem = pl.BlockSpec(memory_space=pltpu.VMEM)
    smem = pl.BlockSpec(memory_space=pltpu.SMEM)
    hbm = pl.BlockSpec(memory_space=pl.ANY)
    dma = pltpu.SemaphoreType.DMA
    return pl.pallas_call(
        functools.partial(dense_kernel, sizes, chunks, units),
        out_shape=(
            jax.ShapeDtypeStruct((slab, rows, cells), BF16),
            jax.ShapeDtypeStruct((slab, rows, cells), BF16),
            jax.ShapeDtypeStruct((1, cells), F32),
        ),
        in_specs=[hbm] * 4 + [vmem] * 2 + [hbm] * 2 + [smem],
        out_specs=(vmem, vmem, vmem),
        scratch_shapes=[
            *[pltpu.VMEM((slab, rows, cells), BF16)] * 4,
            pltpu.VMEM(args[6].shape, BF16),
            pltpu.VMEM(args[7].shape, BF16),
            pltpu.VMEM((rows, full, cells), BF16),
            pltpu.VMEM((chunks, nz, step, full, cells), BF16),
            pltpu.VMEM((chunks, nz, step, full, cells), BF16),
            pltpu.VMEM((rows, full, cells), BF16),
            pltpu.VMEM((rows, cells), F32),
            pltpu.VMEM((nz * full, nz * full), BF16),
            pltpu.VMEM((full * (rows + 2 * MARGIN), cells), F32),
            pltpu.VMEM((full * rows, cells), F32),
            pltpu.VMEM((full, rows, cells), F32),
            pltpu.VMEM((2, full, cells), BF16),
            pltpu.VMEM((2, 2, rows, cells), BF16),
            pltpu.VMEM((2, 2, rows, cells), BF16),
            pltpu.VMEM((2, 2, rows, cells), F32),
            pltpu.VMEM((2, 8, cells), F32),
            pltpu.VMEM((nz, 8, cells), F32),
            pltpu.VMEM((ny * nx, 8, cells), F32),
            dma((6,)),
            *[dma((chunks, nz))] * 4,
            *[dma((2,))] * 4,
            dma((nx * ny + nz - 2,)),
            dma((nz,)),
            dma((ny * nx,)),
        ],
        compiler_params=pltpu.CompilerParams(
            collective_id=0, has_side_effects=True, vmem_limit_bytes=52 * 1024 * 1024
        ),
    )(*args)


def fast_call(sizes, span, units, layers, args):
    nx, ny, nz = sizes
    slab, rows, cells = args[0].shape
    full = 2 * slab
    chunks = (rows * 3 // 4) // nz
    quad = nz * cells
    groups = [math.prod(n for _, _, n in dims) for dims in stage_sizes(sizes)]
    vmem = pl.BlockSpec(memory_space=pltpu.VMEM)
    smem = pl.BlockSpec(memory_space=pltpu.SMEM)
    hbm = pl.BlockSpec(memory_space=pl.ANY)
    dma = pltpu.SemaphoreType.DMA
    return pl.pallas_call(
        functools.partial(fast_kernel, sizes, span, units),
        out_shape=(
            jax.ShapeDtypeStruct((slab, rows, cells), BF16),
            jax.ShapeDtypeStruct((slab, rows, cells), BF16),
            jax.ShapeDtypeStruct((1, cells), F32),
            jax.ShapeDtypeStruct((1,), jnp.int32),
        ),
        in_specs=[hbm] * 4 + [vmem] * 2 + [hbm] * 3,
        out_specs=(vmem, vmem, vmem, smem),
        scratch_shapes=[
            *[pltpu.VMEM((slab, rows, cells), BF16)] * 4,
            pltpu.VMEM(args[6].shape, BF16),
            pltpu.VMEM(args[7].shape, BF16),
            pltpu.SMEM(args[8].shape, F32),
            pltpu.VMEM((rows // span, full, span * cells), BF16),
            pltpu.VMEM((rows // span, slab, span * cells), BF16),
            pltpu.VMEM((chunks, quad, span * cells), BF16),
            pltpu.VMEM((chunks, nz, full, cells), BF16),
            pltpu.VMEM((chunks, nz, slab, cells), BF16),
            *[pltpu.VMEM((chunks, nz, full, cells), BF16)] * 3,
            pltpu.VMEM((full, span * cells), F32),
            pltpu.VMEM((rows, cells), F32),
            pltpu.VMEM((rows, cells), F32),
            pltpu.VMEM((nz * full, nz * full), BF16),
            pltpu.VMEM((full * (rows + 2 * MARGIN), cells), F32),
            pltpu.VMEM((slab * rows, cells), F32),
            pltpu.VMEM((full * rows, cells), F32),
            pltpu.VMEM((full, rows, cells), F32),
            pltpu.VMEM((2, full, cells), BF16),
            pltpu.VMEM((2, full, cells), BF16),
            pltpu.VMEM((2, 2, rows, cells), BF16),
            pltpu.VMEM((2, 2, rows, cells), BF16),
            pltpu.VMEM((2, 2, rows, cells), F32),
            pltpu.VMEM((len(groups), 1, cells), F32),
            *[pltpu.VMEM((n, 1, cells), F32) for n in groups],
            dma((7,)),
            *[dma((chunks, nz))] * 4,
            *[dma((2,))] * 4,
            *[dma((len(groups),))] * 2,
        ],
        compiler_params=pltpu.CompilerParams(
            collective_id=1, has_side_effects=True, vmem_limit_bytes=52 * 1024 * 1024
        ),
    )(*args)


def body(sizes, *arrays):
    nx, ny, nz = sizes
    rows, units, layers, cells = arrays[0].shape
    slab = units * layers
    wide = [v.transpose(1, 2, 0, 3).reshape(slab, rows, cells) for v in arrays[:4]]
    args = (*wide, arrays[4], arrays[5].T, arrays[6].transpose(1, 0, 2), *arrays[7:])
    held = [pltpu.with_memory_space_constraint(v, pltpu.HBM) for v in args]
    span = rows // 2
    if rows % 16 == 0 and (span * 3 // 4) % nz == 0:
        *quick, flag = fast_call(sizes, span, units, layers, held)
        out_t, out_d, border = lax.cond(
            flag[0] > 0, lambda: dense_call(sizes, units, layers, held), lambda: tuple(quick)
        )
    else:
        out_t, out_d, border = dense_call(sizes, units, layers, held)
    out_t, out_d, border = put_call(out_t, out_d, border)
    outs = [
        v.reshape(units, layers, rows, cells).transpose(2, 0, 1, 3) for v in (out_t, out_d)
    ]
    return (*outs, border)


def solution(mesh):
    wide = P("tx", None, "lz", "ty")
    in_specs = (
        wide, wide, wide, wide, P("tx", "ty"), P("tx", "ty"), P("tx", None, "ty"), P(), P(),
    )
    sizes = tuple(mesh.shape[name] for name in ("tx", "ty", "lz"))
    return jax.shard_map(
        functools.partial(body, sizes), mesh=mesh, in_specs=in_specs,
        out_specs=(wide, wide, P()), check_vma=False,
    )
```

```python
import functools
import itertools
import math
import jax
import jax.numpy as jnp
from jax import lax
from jax.experimental import pallas as pl
from jax.experimental.pallas import tpu as pltpu
from jax.sharding import PartitionSpec as P

MESH = pl.DeviceIdType.MESH
F32 = jnp.float32
BF16 = jnp.bfloat16


MARGIN = 8


def dense_kernel(
    sizes, chunks, units,
    test_hbm, dir_hbm, b_hbm, c_hbm, land_ref, active_ref, blocks_hbm, k_hbm, kappa_ref,
    out_t, out_d, border_ref,
    test_ref, dir_ref, b_ref, c_ref, blocks_ref, k_ref,
    masked, arrived, product, coupled, weight, big_k, field, back, before_image, halo,
    edge_out, edge_in, edge_f, stat_out, stat_z, stat_y,
    ls, fs, fr, bs, br, xs, xr, ys, yr, ss, sr_z, sr_y,
):
    nx, ny, nz = sizes
    slab, rows, cells = test_ref.shape
    layers = slab // units
    full = 2 * slab
    group = rows // nz
    step = group // chunks
    pitch = rows + 2 * MARGIN
    mx, my, mz = lax.axis_index("tx"), lax.axis_index("ty"), lax.axis_index("lz")
    fields = (test_ref, dir_ref)
    outs = (out_t, out_d)

    loads = [
        pltpu.make_async_copy(source, target, ls.at[i])
        for i, (source, target) in enumerate((
            (test_hbm, test_ref), (dir_hbm, dir_ref), (k_hbm, k_ref), (b_hbm, b_ref),
            (c_hbm, c_ref), (blocks_hbm, blocks_ref),
        ))
    ]
    for load in loads:
        load.start()

    barrier = pltpu.get_barrier_semaphore()
    for k in range(1, nz):
        pl.semaphore_signal(
            barrier, inc=1, device_id={"lz": lax.rem(mz + k, nz)}, device_id_type=MESH
        )
    for k in range(1, nx * ny):
        near = {"ty": lax.rem(my + k // nx, ny), "tx": lax.rem(mx + k % nx, nx)}
        pl.semaphore_signal(barrier, inc=1, device_id=near, device_id_type=MESH)

    lane = lax.broadcasted_iota(jnp.int32, (rows, cells), 1)
    line = lax.broadcasted_iota(jnp.int32, (rows, rows), 0)
    named = jnp.max(
        jnp.where(jnp.broadcast_to(active_ref[...], (rows, rows)) == line, 1.0, 0.0),
        axis=1, keepdims=True,
    )
    weight[...] = land_ref[...].astype(F32) * named
    ocean = weight[...]

    def middle(q):
        return pl.ds(pl.multiple_of(q * pitch + MARGIN, 8), rows)

    for f in range(2):
        loads[f].wait()

        def mask(j, carry):
            field[middle(f * slab + j), :] = fields[f][j].astype(F32) * ocean
            return carry

        lax.fori_loop(0, slab, mask, 0, unroll=8)

    def pack(c):
        def pack_row(i, carry):
            x = lax.div(i, step) * group + c * step + lax.rem(i, step)
            masked[x] = field[pl.ds(MARGIN + x, full, stride=pitch), :].astype(BF16)
            return carry

        lax.fori_loop(0, nz * step, pack_row, 0, unroll=4)

    pack(0)

    pl.semaphore_wait(barrier, nx * ny + nz - 2)

    def forward(c, k):
        to = lax.rem(mz + k, nz)
        return pltpu.make_async_remote_copy(
            src_ref=masked.at[pl.ds(to * group + c * step, step)],
            dst_ref=arrived.at[c, mz],
            send_sem=fs.at[c, to],
            recv_sem=fr.at[c, mz],
            device_id={"lz": to},
            device_id_type=MESH,
        )

    def forward_in(c, k):
        src = lax.rem(mz + nz - k, nz)
        return pltpu.make_async_remote_copy(
            src_ref=arrived.at[c, src],
            dst_ref=arrived.at[c, src],
            send_sem=fs.at[c, src],
            recv_sem=fr.at[c, src],
            device_id={"lz": src},
            device_id_type=MESH,
        )

    def backward(c, k):
        to = lax.rem(mz + k, nz)
        return pltpu.make_async_remote_copy(
            src_ref=product.at[c, to],
            dst_ref=coupled.at[pl.ds(mz * group + c * step, step)],
            send_sem=bs.at[c, to],
            recv_sem=br.at[c, mz],
            device_id={"lz": to},
            device_id_type=MESH,
        )

    def backward_in(c, k):
        src = lax.rem(mz + nz - k, nz)
        return pltpu.make_async_remote_copy(
            src_ref=product.at[c, src],
            dst_ref=coupled.at[pl.ds(src * group + c * step, step)],
            send_sem=bs.at[c, src],
            recv_sem=br.at[c, src],
            device_id={"lz": src},
            device_id_type=MESH,
        )

    order = sorted(range(1, nz), key=lambda k: -min(k, nz - k))
    for c in range(1, chunks):
        pack(c)
        for k in order:
            forward(c - 1, k).start()

    def own_row(i, carry):
        arrived[lax.div(i, step), mz, lax.rem(i, step)] = masked[mz * group + i]
        return carry

    lax.fori_loop(0, group, own_row, 0)
    for k in order:
        forward(chunks - 1, k).start()
    later, before = lax.rem(mx + 1, nx), lax.rem(mx + nx - 1, nx)
    to_later = pltpu.make_async_remote_copy(
        src_ref=masked.at[rows - 1], dst_ref=halo.at[0], send_sem=xs.at[0], recv_sem=xr.at[0],
        device_id={"tx": later}, device_id_type=MESH,
    )
    to_before = pltpu.make_async_remote_copy(
        src_ref=masked.at[0], dst_ref=halo.at[1], send_sem=xs.at[1], recv_sem=xr.at[1],
        device_id={"tx": before}, device_id_type=MESH,
    )
    to_later.start()
    to_before.start()
    for f in range(2):
        def edges(j, carry):
            first, last = carry
            value = field[middle(f * slab + j), :]
            first = jnp.where(lane == j, pltpu.roll(value, j, 1), first)
            last = jnp.where(lane == j, pltpu.roll(value, j + 1, 1), last)
            return first, last

        blank = jnp.zeros((rows, cells), F32)
        first, last = lax.fori_loop(0, slab, edges, (blank, blank), unroll=4)
        edge_out[0, f] = first.astype(BF16)
        edge_out[1, f] = last.astype(BF16)

    up, down = lax.rem(my + 1, ny), lax.rem(my + ny - 1, ny)
    to_up = pltpu.make_async_remote_copy(
        src_ref=edge_out.at[1], dst_ref=edge_in.at[0], send_sem=ys.at[0], recv_sem=yr.at[0],
        device_id={"ty": up}, device_id_type=MESH,
    )
    to_down = pltpu.make_async_remote_copy(
        src_ref=edge_out.at[0], dst_ref=edge_in.at[1], send_sem=ys.at[1], recv_sem=yr.at[1],
        device_id={"ty": down}, device_id_type=MESH,
    )
    col = units * layers * nz
    wide = nz * full

    def chooser(shape, dim, f):
        i = lax.broadcasted_iota(jnp.int32, shape, dim)
        j = lax.broadcasted_iota(jnp.int32, shape, 1 - dim)
        part, rest = i // full, lax.rem(i, full)
        field, entry = rest // slab, lax.rem(rest, slab)
        unit, layer = entry // layers, lax.rem(entry, layers)
        target = unit * (layers * nz) + part * layers + layer
        return jnp.where((target == j) & (field == f), 1.0, 0.0).astype(BF16)

    loads[2].wait()
    dense = k_ref[...]
    total = None
    for f in range(2):
        left = jnp.dot(
            chooser((wide, col), 0, f), dense, preferred_element_type=F32
        ).astype(BF16)
        both = jnp.dot(left, chooser((col, wide), 1, f), preferred_element_type=F32)
        total = both if total is None else total + both
    big_k[...] = total.astype(BF16)
    to_up.start()
    to_down.start()

    for load in loads[3:]:
        load.wait()
    zero = jnp.zeros((rows, cells), F32)
    sums = (zero, zero, zero)

    def norms(j, carry):
        bb, cc, cv = carry
        b = b_ref[j].astype(F32)
        c = c_ref[j].astype(F32)
        return bb + b * b, cc + c * c, cv + c * test_ref[j].astype(F32)

    quarter = slab // chunks
    for c in range(chunks):
        for k in order:
            forward_in(c, k).wait_recv()
        part = jnp.concatenate(
            [arrived[c, :, r].reshape(wide, cells) for r in range(step)], axis=1
        )
        result = jnp.dot(big_k[...], part, preferred_element_type=F32).astype(BF16)
        for d in range(nz):
            for r in range(step):
                product[c, d, r] = result[d * full:(d + 1) * full, r * cells:(r + 1) * cells]
        sums = lax.fori_loop(c * quarter, (c + 1) * quarter, norms, sums, unroll=2)
        for k in order:
            backward(c, k).start()
        for r in range(step):
            coupled[mz * group + c * step + r] = product[c, mz, r]

    to_later.wait_recv()
    to_before.wait_recv()
    to_up.wait_recv()
    to_down.wait_recv()
    field[pl.ds(MARGIN - 1, full, stride=pitch), :] = halo[0].astype(F32)
    field[pl.ds(MARGIN + rows, full, stride=pitch), :] = halo[1].astype(F32)

    @pl.when(my > 0)
    def _():
        edge_f[0] = edge_in[0].astype(F32)

    @pl.when(my == 0)
    def _():
        edge_f[0] = jnp.zeros((2, rows, cells), F32)

    @pl.when(my < ny - 1)
    def _():
        edge_f[1] = edge_in[1].astype(F32)

    @pl.when(my == ny - 1)
    def _():
        edge_f[1] = jnp.zeros((2, rows, cells), F32)

    for f in range(2):
        for u in range(units):
            def local(z, carry):
                j = u * layers + z
                q = f * slab + j
                here = field[middle(q), :]
                south = jnp.where(
                    lane == 0, pltpu.roll(edge_f[0, f], lax.rem(cells - j, cells), 1),
                    pltpu.roll(here, 1, 1),
                )
                north = jnp.where(
                    lane == cells - 1, pltpu.roll(edge_f[1, f], cells - 1 - j, 1),
                    pltpu.roll(here, cells - 1, 1),
                )
                near = field[pl.ds(q * pitch + MARGIN - 1, rows), :]
                near = near + field[pl.ds(q * pitch + MARGIN + 1, rows), :]
                value = kappa_ref[u] * (near + south + north - 4.0 * here)
                for w in range(units):
                    value = value + blocks_ref[units * u + w].astype(F32) * field[
                        middle(f * slab + w * layers + z), :
                    ]
                before_image[q] = value
                return carry

            lax.fori_loop(0, layers, local, 0, unroll=2)

    def insert(x, carry):
        back[pl.ds(x, full, stride=rows), :] = coupled[x].astype(F32)
        return carry

    for c in range(chunks):
        for k in order:
            backward_in(c, k).wait_recv()

        def chunk_row(i, carry):
            return insert(lax.div(i, step) * group + c * step + lax.rem(i, step), carry)

        lax.fori_loop(0, nz * step, chunk_row, 0, unroll=4)

    def image(j, carry):
        ba, be = carry
        b = b_ref[j].astype(F32)
        images = []
        for f in range(2):
            q = f * slab + j
            coup = back[pl.ds(pl.multiple_of(q * rows, 8), rows), :]
            images.append(ocean * (coup + before_image[q]))
            outs[f][j] = images[f].astype(BF16)
        return ba + b * images[0], be + b * images[1]

    pair = lax.fori_loop(0, slab, image, (zero, zero), unroll=6)

    lines = [jnp.sum(v, axis=0, keepdims=True) for v in (*sums, *pair)]
    value = jnp.concatenate(lines + [jnp.zeros((3, cells), F32)], axis=0)
    base = 0
    plane = [(i, k) for i in range(ny) for k in range(nx)]
    stages = (
        ([{"lz": lax.rem(mz + k, nz)} for k in range(nz)], nz, stat_z, sr_z, mz,
         [lax.rem(mz + nz - k, nz) for k in range(nz)]),
        ([{"ty": lax.rem(my + i, ny), "tx": lax.rem(mx + k, nx)} for i, k in plane],
         ny * nx, stat_y, sr_y, my * nx + mx,
         [lax.rem(my + ny - i, ny) * nx + lax.rem(mx + nx - k, nx) for i, k in plane]),
    )
    sends = []
    for s, (peers, size, box, sem, me, sources) in enumerate(stages):
        stat_out[s] = value
        box[me] = value
        for k in range(1, size):
            copy = pltpu.make_async_remote_copy(
                src_ref=stat_out.at[s], dst_ref=box.at[me], send_sem=ss.at[base + k - 1],
                recv_sem=sem.at[me], device_id=peers[k], device_id_type=MESH,
            )
            copy.start()
            sends.append(copy)
        base += size - 1
        for k in range(1, size):
            src = sources[k]
            pltpu.make_async_remote_copy(
                src_ref=stat_out.at[s], dst_ref=box.at[src], send_sem=ss.at[0],
                recv_sem=sem.at[src], device_id=peers[k], device_id_type=MESH,
            ).wait_recv()
        value = box[0]
        for i in range(1, size):
            value = value + box[i]
    final = jnp.broadcast_to(jnp.sum(value, axis=1, keepdims=True), (8, cells))
    bb, cc, cv, ba, be = (final[i:i + 1] for i in range(5))
    line = lax.broadcasted_iota(jnp.int32, (1, cells), 1)
    top = jnp.where(line == 0, ba, jnp.where(line == 1, be, cv))
    low = jnp.where(line == 2, cc, bb)
    border_ref[...] = top / jnp.sqrt(low)

    for c in range(chunks):
        for k in order:
            forward(c, k).wait_send()
            backward(c, k).wait_send()
    to_later.wait_send()
    to_before.wait_send()
    to_up.wait_send()
    to_down.wait_send()
    for copy in sends:
        copy.wait_send()


def stage_sizes(sizes):
    names = ("lz", "ty", "tx")
    dims = [(name, i, sizes[("tx", "ty", "lz").index(name)]) for i, name in enumerate(names)]
    if sizes[0] * sizes[1] * sizes[2] <= 64:
        return [dims]
    return [dims[:1], dims[1:]]


def put_kernel(t_ref, d_ref, border_ref, out_t, out_d, out_border, line, sems):
    line[...] = border_ref[0, :line.shape[0]]
    copies = [
        pltpu.make_async_copy(source, target, sems.at[i])
        for i, (source, target) in enumerate(((t_ref, out_t), (d_ref, out_d), (line, out_border)))
    ]
    for copy in copies:
        copy.start()
    for copy in copies:
        copy.wait()


def put_call(out_t, out_d, border):
    hbm = pl.BlockSpec(memory_space=pl.ANY)
    return pl.pallas_call(
        put_kernel,
        out_shape=(
            jax.ShapeDtypeStruct(out_t.shape, BF16),
            jax.ShapeDtypeStruct(out_d.shape, BF16),
            jax.ShapeDtypeStruct((3,), F32),
        ),
        in_specs=[hbm, hbm, pl.BlockSpec(memory_space=pltpu.VMEM)],
        out_specs=(hbm, hbm, hbm),
        scratch_shapes=[pltpu.VMEM((3,), F32), pltpu.SemaphoreType.DMA((3,))],
    )(out_t, out_d, border)


def fast_kernel(
    sizes, span, units,
    test_hbm, dir_hbm, b_hbm, c_hbm, land_ref, active_ref, blocks_hbm, k_hbm, kappa_hbm,
    out_t, out_d, border_ref, flag_ref,
    test_ref, dir_ref, b_ref, c_ref, blocks_ref, k_ref,
    kappa_ref, wide_ref, wide_b, pick, packed, packed_b, arrived, product, coupled, partial, weight, place, big_k,
    field, b_field, back, before_image, halo_out, halo, edge_out, edge_in, edge_f, stat_out,
    *rest,
):
    nx, ny, nz = sizes
    stages = len(stage_sizes(sizes))
    boxes, rest = rest[:stages], rest[stages:]
    ls, fs, fr, bs, br, xs, xr, ys, yr, ss = rest[:10]
    stat_sems = rest[10]
    slab, rows, cells = test_ref.shape
    layers = slab // units
    full = 2 * slab
    halves = rows // span
    slots = packed.shape[0] * nz // halves
    per = slots // nz
    chunks = halves * per
    pitch = rows + 2 * MARGIN
    quad = nz * cells
    mx, my, mz = lax.axis_index("tx"), lax.axis_index("ty"), lax.axis_index("lz")
    fields = (test_ref, dir_ref)
    outs = (out_t, out_d)

    loads = [
        pltpu.make_async_copy(source, target, ls.at[i])
        for i, (source, target) in enumerate((
            (test_hbm, test_ref), (dir_hbm, dir_ref), (b_hbm, b_ref), (k_hbm, k_ref),
            (c_hbm, c_ref), (blocks_hbm, blocks_ref), (kappa_hbm, kappa_ref),
        ))
    ]
    for load in loads:
        load.start()

    barrier = pltpu.get_barrier_semaphore()
    for k in range(1, nz):
        pl.semaphore_signal(
            barrier, inc=1, device_id={"lz": lax.rem(mz + k, nz)}, device_id_type=MESH
        )
    for k in range(1, nx * ny):
        near = {"ty": lax.rem(my + k // nx, ny), "tx": lax.rem(mx + k % nx, nx)}
        pl.semaphore_signal(barrier, inc=1, device_id=near, device_id_type=MESH)

    lane = lax.broadcasted_iota(jnp.int32, (rows, cells), 1)
    line = lax.broadcasted_iota(jnp.int32, (rows, rows), 0)
    named = jnp.max(
        jnp.where(jnp.broadcast_to(active_ref[...], (rows, rows)) == line, 1.0, 0.0),
        axis=1, keepdims=True,
    )
    ocean = land_ref[...].astype(F32) * named
    weight[...] = ocean

    wet = ocean.astype(BF16)
    other = lax.broadcasted_iota(jnp.int32, (rows, rows), 1)
    earlier = jnp.where((other < line) & (other // span == line // span), 1.0, 0.0).astype(BF16)
    cell_i = lax.broadcasted_iota(jnp.int32, (cells, cells), 0)
    cell_j = lax.broadcasted_iota(jnp.int32, (cells, cells), 1)
    ahead = jnp.where(cell_i < cell_j, 1.0, 0.0).astype(BF16)
    above = jnp.dot(earlier, wet, preferred_element_type=F32).astype(BF16)
    count = jnp.dot(wet, ahead, preferred_element_type=F32)
    count = count + jnp.dot(above, jnp.ones((cells, cells), BF16), preferred_element_type=F32)
    place[...] = jnp.where(ocean > 0.0, count, -1.0)
    excess = jnp.where((ocean > 0.0) & (count >= float(slots * cells)), 1.0, 0.0)

    spot = lax.broadcasted_iota(jnp.int32, (quad, cells), 0).astype(F32)

    def choose(h, s):
        def one(i, carry):
            where = place[pl.ds(h * span + i, 1), :] - float(s * quad)
            hit = jnp.where(jnp.broadcast_to(where, (quad, cells)) == spot, 1.0, 0.0)
            pick[h * per + s, :, pl.ds(pl.multiple_of(i * cells, cells), cells)] = hit.astype(BF16)
            return carry

        lax.fori_loop(nz * s, span, one, 0, unroll=2)

    choose(0, 0)

    def middle(q, start, size):
        return pl.ds(pl.multiple_of(q * pitch + MARGIN + start, 8), size)

    def prepare(h):
        part = weight[h * span:(h + 1) * span, :]
        for f in range(2):
            def mask(j, carry):
                value = fields[f][j, h * span:(h + 1) * span, :].astype(F32) * part
                field[middle(f * slab + j, h * span, span), :] = value
                return carry

            lax.fori_loop(0, slab, mask, 0, unroll=8)

        def pack_row(i, carry):
            spot = pl.ds(pl.multiple_of(i * cells, cells), cells)
            row = field[pl.ds(MARGIN + h * span + i, full, stride=pitch), :].astype(BF16)
            wide_ref[h, :, spot] = row
            return carry

        lax.fori_loop(0, span, pack_row, 0, unroll=4)

    def prepare_b():
        def widen(j, carry):
            start = pl.multiple_of(j * rows, 8)
            b_field[pl.ds(start, rows), :] = b_ref[j].astype(F32)
            return carry

        lax.fori_loop(0, slab, widen, 0, unroll=4)
        for h in range(halves):
            def pack_row(i, carry):
                row = b_field[pl.ds(h * span + i, slab, stride=rows), :].astype(BF16)
                wide_b[h, :, pl.ds(pl.multiple_of(i * cells, cells), cells)] = row
                return carry

            lax.fori_loop(0, span, pack_row, 0, unroll=4)

    def compact(h, s, source, target):
        c = h * per + s
        found = lax.dot_general(
            source[h, :, s * quad:span * cells], pick[c, :, s * quad:span * cells],
            (((1,), (1,)), ((), ())), preferred_element_type=F32,
        ).astype(BF16)
        for d in range(nz):
            target[c, d] = found[:, d * cells:(d + 1) * cells]

    def target(k):
        down = nz - k
        low = down - jnp.where(down <= mz, 1, 0)
        high = k - 1 + jnp.where(k - 1 >= mz, 1, 0)
        return jnp.where(mz < nz // 2, low, high)

    def forward(c, k):
        to = target(k)
        return pltpu.make_async_remote_copy(
            src_ref=packed.at[c, to], dst_ref=arrived.at[c, mz],
            send_sem=fs.at[c, to], recv_sem=fr.at[c, mz], device_id={"lz": to},
            device_id_type=MESH,
        )

    def forward_in(c, k):
        src = lax.rem(mz + nz - k, nz)
        return pltpu.make_async_remote_copy(
            src_ref=arrived.at[c, src], dst_ref=arrived.at[c, src],
            send_sem=fs.at[c, src], recv_sem=fr.at[c, src], device_id={"lz": src},
            device_id_type=MESH,
        )

    def backward(c, k):
        to = target(k)
        return pltpu.make_async_remote_copy(
            src_ref=product.at[c, to], dst_ref=coupled.at[c, mz], send_sem=bs.at[c, to],
            recv_sem=br.at[c, mz], device_id={"lz": to}, device_id_type=MESH,
        )

    def backward_in(c, k):
        src = lax.rem(mz + nz - k, nz)
        return pltpu.make_async_remote_copy(
            src_ref=product.at[c, src], dst_ref=coupled.at[c, src], send_sem=bs.at[c, src],
            recv_sem=br.at[c, src], device_id={"lz": src}, device_id_type=MESH,
        )

    order = range(1, nz)
    loads[0].wait()
    loads[1].wait()
    for h in range(halves):
        prepare(h)
        for s in range(per):
            c = h * per + s
            if c:
                choose(h, s)
            compact(h, s, wide_ref, packed)
            if c == 0:
                pl.semaphore_wait(barrier, nx * ny + nz - 2)
            for k in order:
                forward(c, k).start()
            arrived[c, mz] = packed[c, mz]

    halo_out[0] = wide_ref[halves - 1, :, (span - 1) * cells:span * cells]
    halo_out[1] = wide_ref[0, :, :cells]
    later, before = lax.rem(mx + 1, nx), lax.rem(mx + nx - 1, nx)
    to_later = pltpu.make_async_remote_copy(
        src_ref=halo_out.at[0], dst_ref=halo.at[0], send_sem=xs.at[0], recv_sem=xr.at[0],
        device_id={"tx": later}, device_id_type=MESH,
    )
    to_before = pltpu.make_async_remote_copy(
        src_ref=halo_out.at[1], dst_ref=halo.at[1], send_sem=xs.at[1], recv_sem=xr.at[1],
        device_id={"tx": before}, device_id_type=MESH,
    )
    to_later.start()
    to_before.start()
    for f in range(2):
        def edges(j, carry):
            first, last = carry
            value = field[middle(f * slab + j, 0, rows), :]
            first = jnp.where(lane == j, pltpu.roll(value, j, 1), first)
            last = jnp.where(lane == j, pltpu.roll(value, j + 1, 1), last)
            return first, last

        blank = jnp.zeros((rows, cells), F32)
        first, last = lax.fori_loop(0, slab, edges, (blank, blank), unroll=4)
        edge_out[0, f] = first.astype(BF16)
        edge_out[1, f] = last.astype(BF16)

    up, down = lax.rem(my + 1, ny), lax.rem(my + ny - 1, ny)
    to_up = pltpu.make_async_remote_copy(
        src_ref=edge_out.at[1], dst_ref=edge_in.at[0], send_sem=ys.at[0], recv_sem=yr.at[0],
        device_id={"ty": up}, device_id_type=MESH,
    )
    to_down = pltpu.make_async_remote_copy(
        src_ref=edge_out.at[0], dst_ref=edge_in.at[1], send_sem=ys.at[1], recv_sem=yr.at[1],
        device_id={"ty": down}, device_id_type=MESH,
    )
    to_up.start()
    to_down.start()
    col = units * layers * nz
    wide = nz * full

    def chooser(shape, dim, f):
        i = lax.broadcasted_iota(jnp.int32, shape, dim)
        j = lax.broadcasted_iota(jnp.int32, shape, 1 - dim)
        part, rest = i // full, lax.rem(i, full)
        field, entry = rest // slab, lax.rem(rest, slab)
        unit, layer = entry // layers, lax.rem(entry, layers)
        target = unit * (layers * nz) + part * layers + layer
        return jnp.where((target == j) & (field == f), 1.0, 0.0).astype(BF16)

    loads[3].wait()
    dense = k_ref[...]
    total = None
    for f in range(2):
        left = jnp.dot(
            chooser((wide, col), 0, f), dense, preferred_element_type=F32
        ).astype(BF16)
        both = jnp.dot(left, chooser((col, wide), 1, f), preferred_element_type=F32)
        total = both if total is None else total + both
    big_k[...] = total.astype(BF16)

    loads[2].wait()
    for load in loads[4:]:
        load.wait()
    zero = jnp.zeros((rows, cells), F32)
    sums = (zero, zero, zero)

    def norms(j, carry):
        bb, cc, cv = carry
        b = b_ref[j].astype(F32)
        c = c_ref[j].astype(F32)
        return bb + b * b, cc + c * c, cv + c * test_ref[j].astype(F32)

    to_later.wait_recv()
    to_before.wait_recv()
    to_up.wait_recv()
    to_down.wait_recv()
    field[pl.ds(MARGIN - 1, full, stride=pitch), :] = halo[0].astype(F32)
    field[pl.ds(MARGIN + rows, full, stride=pitch), :] = halo[1].astype(F32)

    @pl.when(my > 0)
    def _():
        edge_f[0] = edge_in[0].astype(F32)

    @pl.when(my == 0)
    def _():
        edge_f[0] = jnp.zeros((2, rows, cells), F32)

    @pl.when(my < ny - 1)
    def _():
        edge_f[1] = edge_in[1].astype(F32)

    @pl.when(my == ny - 1)
    def _():
        edge_f[1] = jnp.zeros((2, rows, cells), F32)


    totals = [zero, zero]

    def local_part(f, u):
        def local(z, total):
            j = u * layers + z
            q = f * slab + j
            here = field[middle(q, 0, rows), :]
            south = jnp.where(
                lane == 0, pltpu.roll(edge_f[0, f], lax.rem(cells - j, cells), 1),
                pltpu.roll(here, 1, 1),
            )
            north = jnp.where(
                lane == cells - 1, pltpu.roll(edge_f[1, f], cells - 1 - j, 1),
                pltpu.roll(here, cells - 1, 1),
            )
            near = field[pl.ds(q * pitch + MARGIN - 1, rows), :]
            near = near + field[pl.ds(q * pitch + MARGIN + 1, rows), :]
            value = kappa_ref[u] * (near + south + north - 4.0 * here)
            for w in range(units):
                value = value + blocks_ref[units * u + w].astype(F32) * field[
                    middle(f * slab + w * layers + z, 0, rows), :
                ]
            before_image[q] = value
            return total + b_ref[j].astype(F32) * value

        totals[f] = lax.fori_loop(0, layers, local, totals[f], unroll=2)

    jobs = [(f, u) for f in range(2) for u in range(units)]
    each = -(-len(jobs) // chunks)

    tile = jnp.zeros((8, cells), F32)

    def dots(pair, values, weights):
        ba, be = pair
        for d in range(nz):
            y = values[d].astype(F32)
            b = weights[d].astype(F32)
            ba = ba + jnp.sum((y[:slab] * b).reshape(slab // 8, 8, cells), axis=0)
            be = be + jnp.sum((y[slab:] * b).reshape(slab // 8, 8, cells), axis=0)
        return ba, be

    pair = (tile, tile)
    share = slab // chunks
    for c in range(chunks):
        for k in order:
            forward_in(c, k).wait_recv()
        part = arrived[c].reshape(wide, cells)
        result = jnp.dot(big_k[...], part, preferred_element_type=F32).astype(BF16)
        for d in range(nz):
            product[c, d] = result[d * full:(d + 1) * full]
        for k in order:
            backward(c, k).start()
        coupled[c, mz] = product[c, mz]
        sums = lax.fori_loop(c * share, (c + 1) * share, norms, sums, unroll=2)
        if c == 0:
            prepare_b()
        compact(c // per, c % per, wide_b, packed_b)
        for job in jobs[c * each:(c + 1) * each]:
            local_part(*job)
    if share * chunks < slab:
        sums = lax.fori_loop(share * chunks, slab, norms, sums)

    def image(start, stop):
        part = weight[start:stop, :]

        def one(j, carry):
            for f in range(2):
                q = f * slab + j
                coup = back[pl.ds(pl.multiple_of(q * rows + start, 8), stop - start), :]
                value = part * (coup + before_image[q, start:stop, :])
                outs[f][j, start:stop, :] = value.astype(BF16)
            return carry

        lax.fori_loop(0, slab, one, 0, unroll=6)

    def begin(s, value):
        stat_out[s] = value
        _, peers, me = reduce_stages[s]
        boxes[s][me] = value
        for peer in reversed(peers):
            pltpu.make_async_remote_copy(
                src_ref=stat_out.at[s], dst_ref=boxes[s].at[me], send_sem=ss.at[s],
                recv_sem=stat_sems.at[s], device_id=peer, device_id_type=MESH,
            ).start()

    def every(s, sem):
        rows_in = boxes[s].at[pl.ds(0, len(reduce_stages[s][1]))]
        return pltpu.make_async_copy(rows_in, rows_in, sem.at[s])

    def finish(s):
        every(s, stat_sems).wait()
        return jnp.sum(boxes[s][...], axis=0)

    reduce_stages = []
    for dims in stage_sizes(sizes):
        me = 0
        for name, at, n in dims:
            me = me * n + lax.axis_index(name)
        peers = []
        for shift in itertools.product(*[range(n) for _, _, n in dims]):
            if any(shift):
                peer = {
                    name: lax.rem(lax.axis_index(name) + k, n)
                    for (name, _, n), k in zip(dims, shift)
                }
                peers.append(peer)
        reduce_stages.append((dims, peers, me))

    seat = lax.broadcasted_iota(jnp.int32, (8, cells), 0)
    spot = lax.broadcasted_iota(jnp.int32, (8, cells), 1)

    def line_of(values):
        lines = [jnp.sum(v, axis=0, keepdims=True) for v in values]
        lines += [jnp.zeros((8 - len(lines), cells), F32)]
        value = jnp.sum(jnp.concatenate(lines, axis=0), axis=1, keepdims=True)
        value = jnp.where(seat == spot, jnp.broadcast_to(value, (8, cells)), 0.0)
        return jnp.sum(value, axis=0, keepdims=True)

    for h in range(halves):
        drawn = 0
        for s in range(per):
            c = h * per + s
            if c == chunks - 1:
                early = line_of((*sums, *(ocean * v for v in totals), excess))
                early = early + line_of((tile, tile, tile, *pair, tile))
                pair = (tile, tile)
            for k in order:
                backward_in(c, k).wait_recv()
            pair = dots(pair, coupled.at[c], packed_b.at[c])
            if c == chunks - 1:
                begin(0, early + line_of((tile, tile, tile, *pair, tile)))
            block = jnp.concatenate([coupled[c, d] for d in range(nz)], axis=1)
            spread = jnp.dot(
                block, pick[c, :, s * quad:span * cells], preferred_element_type=F32
            )
            if s:
                spread = spread + partial[:, s * quad:span * cells]
            done = nz if s + 1 < per else span - nz * s
            for i in range(done):
                x = h * span + nz * s + i
                back[pl.ds(x, full, stride=rows), :] = spread[:, i * cells:(i + 1) * cells]
            if s + 1 < per:
                partial[:, (s + 1) * quad:span * cells] = spread[:, quad:]
            ready = (nz * s + done) // 8 * 8
            if s == per - 1 or (h == halves - 1 and s == per - 2 and ready > drawn):
                image(h * span + drawn, h * span + ready)
                drawn = ready

    for c in range(chunks):
        for k in order:
            forward(c, k).wait_send()
            backward(c, k).wait_send()
    to_later.wait_send()
    to_before.wait_send()
    to_up.wait_send()
    to_down.wait_send()
    value = finish(0)
    for s in range(1, stages):
        begin(s, value)
        value = finish(s)
    value = jnp.broadcast_to(value, (8, cells))
    top = jnp.where(spot < 2, pltpu.roll(value, cells - 3, 1), value)
    low = jnp.where(spot == 0, value, pltpu.roll(value, 1, 1))
    border_ref[...] = (top / jnp.sqrt(low))[:1]
    flag_ref[0] = jnp.where(jnp.sum(jnp.where(spot == 5, value, 0.0)) > 0.0, 1, 0)

    for s in range(stages):
        every(s, ss).wait()


def dense_call(sizes, units, layers, args):
    nx, ny, nz = sizes
    slab, rows, cells = args[0].shape
    full = 2 * slab
    group = rows // nz
    chunks = 4 if group % 4 == 0 else 1
    step = group // chunks
    vmem = pl.BlockSpec(memory_space=pltpu.VMEM)
    smem = pl.BlockSpec(memory_space=pltpu.SMEM)
    hbm = pl.BlockSpec(memory_space=pl.ANY)
    dma = pltpu.SemaphoreType.DMA
    return pl.pallas_call(
        functools.partial(dense_kernel, sizes, chunks, units),
        out_shape=(
            jax.ShapeDtypeStruct((slab, rows, cells), BF16),
            jax.ShapeDtypeStruct((slab, rows, cells), BF16),
            jax.ShapeDtypeStruct((1, cells), F32),
        ),
        in_specs=[hbm] * 4 + [vmem] * 2 + [hbm] * 2 + [smem],
        out_specs=(vmem, vmem, vmem),
        scratch_shapes=[
            *[pltpu.VMEM((slab, rows, cells), BF16)] * 4,
            pltpu.VMEM(args[6].shape, BF16),
            pltpu.VMEM(args[7].shape, BF16),
            pltpu.VMEM((rows, full, cells), BF16),
            pltpu.VMEM((chunks, nz, step, full, cells), BF16),
            pltpu.VMEM((chunks, nz, step, full, cells), BF16),
            pltpu.VMEM((rows, full, cells), BF16),
            pltpu.VMEM((rows, cells), F32),
            pltpu.VMEM((nz * full, nz * full), BF16),
            pltpu.VMEM((full * (rows + 2 * MARGIN), cells), F32),
            pltpu.VMEM((full * rows, cells), F32),
            pltpu.VMEM((full, rows, cells), F32),
            pltpu.VMEM((2, full, cells), BF16),
            pltpu.VMEM((2, 2, rows, cells), BF16),
            pltpu.VMEM((2, 2, rows, cells), BF16),
            pltpu.VMEM((2, 2, rows, cells), F32),
            pltpu.VMEM((2, 8, cells), F32),
            pltpu.VMEM((nz, 8, cells), F32),
            pltpu.VMEM((ny * nx, 8, cells), F32),
            dma((6,)),
            *[dma((chunks, nz))] * 4,
            *[dma((2,))] * 4,
            dma((nx * ny + nz - 2,)),
            dma((nz,)),
            dma((ny * nx,)),
        ],
        compiler_params=pltpu.CompilerParams(
            collective_id=0, has_side_effects=True, vmem_limit_bytes=52 * 1024 * 1024
        ),
    )(*args)


def fast_call(sizes, span, units, layers, args):
    nx, ny, nz = sizes
    slab, rows, cells = args[0].shape
    full = 2 * slab
    chunks = (rows * 3 // 4) // nz
    quad = nz * cells
    groups = [math.prod(n for _, _, n in dims) for dims in stage_sizes(sizes)]
    vmem = pl.BlockSpec(memory_space=pltpu.VMEM)
    smem = pl.BlockSpec(memory_space=pltpu.SMEM)
    hbm = pl.BlockSpec(memory_space=pl.ANY)
    dma = pltpu.SemaphoreType.DMA
    return pl.pallas_call(
        functools.partial(fast_kernel, sizes, span, units),
        out_shape=(
            jax.ShapeDtypeStruct((slab, rows, cells), BF16),
            jax.ShapeDtypeStruct((slab, rows, cells), BF16),
            jax.ShapeDtypeStruct((1, cells), F32),
            jax.ShapeDtypeStruct((1,), jnp.int32),
        ),
        in_specs=[hbm] * 4 + [vmem] * 2 + [hbm] * 3,
        out_specs=(vmem, vmem, vmem, smem),
        scratch_shapes=[
            *[pltpu.VMEM((slab, rows, cells), BF16)] * 4,
            pltpu.VMEM(args[6].shape, BF16),
            pltpu.VMEM(args[7].shape, BF16),
            pltpu.SMEM(args[8].shape, F32),
            pltpu.VMEM((rows // span, full, span * cells), BF16),
            pltpu.VMEM((rows // span, slab, span * cells), BF16),
            pltpu.VMEM((chunks, quad, span * cells), BF16),
            pltpu.VMEM((chunks, nz, full, cells), BF16),
            pltpu.VMEM((chunks, nz, slab, cells), BF16),
            *[pltpu.VMEM((chunks, nz, full, cells), BF16)] * 3,
            pltpu.VMEM((full, span * cells), F32),
            pltpu.VMEM((rows, cells), F32),
            pltpu.VMEM((rows, cells), F32),
            pltpu.VMEM((nz * full, nz * full), BF16),
            pltpu.VMEM((full * (rows + 2 * MARGIN), cells), F32),
            pltpu.VMEM((slab * rows, cells), F32),
            pltpu.VMEM((full * rows, cells), F32),
            pltpu.VMEM((full, rows, cells), F32),
            pltpu.VMEM((2, full, cells), BF16),
            pltpu.VMEM((2, full, cells), BF16),
            pltpu.VMEM((2, 2, rows, cells), BF16),
            pltpu.VMEM((2, 2, rows, cells), BF16),
            pltpu.VMEM((2, 2, rows, cells), F32),
            pltpu.VMEM((len(groups), 1, cells), F32),
            *[pltpu.VMEM((n, 1, cells), F32) for n in groups],
            dma((7,)),
            *[dma((chunks, nz))] * 4,
            *[dma((2,))] * 4,
            *[dma((len(groups),))] * 2,
        ],
        compiler_params=pltpu.CompilerParams(
            collective_id=1, has_side_effects=True, vmem_limit_bytes=52 * 1024 * 1024
        ),
    )(*args)


def body(sizes, *arrays):
    nx, ny, nz = sizes
    rows, units, layers, cells = arrays[0].shape
    slab = units * layers
    wide = [v.transpose(1, 2, 0, 3).reshape(slab, rows, cells) for v in arrays[:4]]
    args = (*wide, arrays[4], arrays[5].T, arrays[6].transpose(1, 0, 2), *arrays[7:])
    held = [pltpu.with_memory_space_constraint(v, pltpu.HBM) for v in args]
    span = rows // 2
    if rows % 16 == 0 and (span * 3 // 4) % nz == 0:
        *quick, flag = fast_call(sizes, span, units, layers, held)
        out_t, out_d, border = lax.cond(
            flag[0] > 0, lambda: dense_call(sizes, units, layers, held), lambda: tuple(quick)
        )
    else:
        out_t, out_d, border = dense_call(sizes, units, layers, held)
    out_t, out_d, border = put_call(out_t, out_d, border)
    outs = [
        v.reshape(units, layers, rows, cells).transpose(2, 0, 1, 3) for v in (out_t, out_d)
    ]
    return (*outs, border)


def solution(mesh):
    wide = P("tx", None, "lz", "ty")
    in_specs = (
        wide, wide, wide, wide, P("tx", "ty"), P("tx", "ty"), P("tx", None, "ty"), P(), P(),
    )
    sizes = tuple(mesh.shape[name] for name in ("tx", "ty", "lz"))
    return jax.shard_map(
        functools.partial(body, sizes), mesh=mesh, in_specs=in_specs,
        out_specs=(wide, wide, P()), check_vma=False,
    )
```
